32 devices in a mesh: shard: 4 (over x, core), rep: 8 (over z, y).
Axes of the slice: x: 2, y: 2, z: 4, core: 2. Of those that a mesh axis runs over, the one named last changes fastest.
Arguments:
- tokens: bfloat16 [32, 1024, 1536], P(('shard', 'rep')), may hold values from -6 to 6
- norm_gain: bfloat16 [1536], P('shard'), may hold values from 0.5 to 1.5
- in_weight: bfloat16 [1536, 6448], P('shard'), may hold values from -0.15625 to 0.15625
- conv_weight: bfloat16 [4, 3328], P(None, 'shard'), may hold values from -0.5 to 0.5
- conv_bias: bfloat16 [3328], P('shard'), may hold values from -0.5 to 0.5
- dt_bias: bfloat16 [48], P('shard'), may hold values from -4 to -1
- a_log: bfloat16 [48], P('shard'), may hold values from -4 to 1.5
- skip: bfloat16 [48], P('shard'), may hold values from 0.5 to 1.5
- gate_gain: bfloat16 [3072], P('shard'), may hold values from 0.5 to 1.5
- out_weight: bfloat16 [3072, 1536], P('shard'), may hold values from -0.109375 to 0.109375
- cotangent: bfloat16 [32, 1024, 1536], P(('shard', 'rep')), may hold values from -6 to 6
Outputs:
- output: bfloat16 [32, 1024, 1536], P(('shard', 'rep'))
- input_grad: float32 [32, 1024, 1536], P(('shard', 'rep'))
- norm_gain_grad: float32 [1536], P('shard')
- in_weight_grad: float32 [1536, 6448], P('shard')
- conv_weight_grad: float32 [4, 3328], P(None, 'shard')
- conv_bias_grad: float32 [3328], P('shard')
- dt_bias_grad: float32 [48], P('shard')
- a_log_grad: float32 [48], P('shard')
- skip_grad: float32 [48], P('shard')
- gate_gain_grad: float32 [3072], P('shard')
- out_weight_grad: float32 [3072, 1536], P('shard')
The draws below stay inside these ranges and needn't reach their ends.
All inputs are finite; a program needn't handle non-finite values.
Results may differ from the reference program's by a relative error of at most 0.0077.
Values may be sent and summed in bfloat16 or wider, within the bound.
No kernel may reach another device: no remote copies, remote signals or barrier semaphores. Data moves between devices by JAX's collectives and lax.ppermute only.
A program may use at most 448 MiB of HBM per device.

```python
import jax
import jax.numpy as jnp
from jax import lax

D = 1536
NHEADS = 48
TAPS = 4
STRETCH = 256
LEN = 1024
INNER = 3072
CONVCH = 3328
PROJ = 6448
SEQS = 32


def steps_of(key, dims, pieces, low, largest):
    level = 1.0
    for position, shards_of in pieces:
        heights = jax.random.uniform(jax.random.fold_in(jax.random.fold_in(key, 6), position), (shards_of,), jnp.float32, low / len(pieces), largest / len(pieces))
        level = level * jnp.repeat(jnp.exp(heights), dims[position] // shards_of).reshape((-1,) + (1,) * (len(dims) - 1 - position))
    return level


def noise(own_key, dims, scale, limit, split=(), kind=jnp.bfloat16):
    values = scale * jax.random.normal(own_key, dims, jnp.float32)
    if split:
        values = values * steps_of(own_key, dims, split, -0.22, 0.18)
    return jnp.clip(values, -limit, limit).astype(kind)


def setup_inputs(seed: int = 0) -> dict:
    key_list = jax.random.split(jax.random.key(seed), 12)
    tokens = noise(key_list[0], (SEQS, LEN, D), 1.0, 6.0, ((0, 32),))
    norm_gain = jnp.clip(1.0 + 0.1 * jax.random.normal(key_list[1], (D,), jnp.float32), 0.5, 1.5).astype(jnp.bfloat16)
    in_weight = noise(key_list[2], (D, PROJ), D ** -0.5, 0.15625, ((0, 4),))
    conv_weight = jnp.clip(jax.random.uniform(key_list[3], (TAPS, CONVCH), jnp.float32, -0.5, 0.5) * steps_of(key_list[3], (TAPS, CONVCH), ((1, 4),), -0.4, 0.0), -0.5, 0.5).astype(jnp.bfloat16)
    conv_bias = jnp.clip(jax.random.uniform(key_list[4], (CONVCH,), jnp.float32, -0.5, 0.5) * steps_of(key_list[4], (CONVCH,), ((0, 4),), -0.4, 0.0), -0.5, 0.5).astype(jnp.bfloat16)
    dt_bias = jnp.clip(-4.0 + 3.0 * jax.random.uniform(key_list[5], (NHEADS,), jnp.float32) ** steps_of(key_list[5], (NHEADS,), ((0, 4),), -0.2, 0.2), -4.0, -1.0).astype(jnp.bfloat16)
    a_log = jnp.clip(-4.0 + 5.5 * jax.random.uniform(key_list[6], (NHEADS,), jnp.float32) ** steps_of(key_list[6], (NHEADS,), ((0, 4),), -0.2, 0.2), -4.0, 1.5).astype(jnp.bfloat16)
    skip = jnp.clip(0.5 + 1.0 * jax.random.uniform(key_list[7], (NHEADS,), jnp.float32) ** steps_of(key_list[7], (NHEADS,), ((0, 4),), -0.2, 0.2), 0.5, 1.5).astype(jnp.bfloat16)
    gate_gain = jnp.clip(1.0 + 0.1 * jax.random.normal(key_list[8], (INNER,), jnp.float32), 0.5, 1.5).astype(jnp.bfloat16)
    out_weight = noise(key_list[9], (INNER, D), INNER ** -0.5, 0.109375, ((0, 4),))
    cotangent = noise(key_list[10], (SEQS, LEN, D), 1.0, 6.0, ((0, 32),))
    return {"tokens": tokens, "norm_gain": norm_gain, "in_weight": in_weight, "conv_weight": conv_weight, "conv_bias": conv_bias, "dt_bias": dt_bias, "a_log": a_log, "skip": skip, "gate_gain": gate_gain, "out_weight": out_weight, "cotangent": cotangent}


@jax.custom_vjp
def low(v):
    return lax.optimization_barrier(v.astype(jnp.bfloat16)).astype(jnp.float32)

@jax.custom_vjp
def low_back(v):
    return v

def low_keep(v):
    return (low(v), None)

def low_pass(kept, grad):
    return (grad,)

def back_keep(v):
    return (v, None)

def back_low(kept, grad):
    return (low(grad),)
low.defvjp(low_keep, low_pass)
low_back.defvjp(back_keep, back_low)
epsilon = 1e-05

def rms_scale(values, gain):
    return values * lax.rsqrt(lax.optimization_barrier(jnp.mean(values * values, axis=-1, keepdims=True)) + epsilon) * gain

def stretch_step(state, values, keys_b, keys_c, steps, decay_rate):
    logs = jnp.cumsum(steps * decay_rate, axis=0)
    span = logs.shape[0]
    rows = lax.broadcasted_iota(jnp.int32, (span, span), 0)
    cols = lax.broadcasted_iota(jnp.int32, (span, span), 1)
    causal = (rows >= cols)[None, :, :]
    logs_heads = logs.T
    gaps = logs_heads[:, :, None] - logs_heads[:, None, :]
    weights = jnp.where(causal, jnp.exp(jnp.where(causal, gaps, 0.0)), 0.0)
    inner = jnp.dot(keys_c, keys_b.T, precision=lax.Precision.HIGHEST)
    mixing = inner[None, :, :] * weights * steps.T[:, None, :]
    local = jnp.einsum('hts,shp->thp', mixing, values, precision=lax.Precision.HIGHEST)
    carried = jnp.einsum('hpn,tn->thp', state, keys_c, precision=lax.Precision.HIGHEST) * jnp.exp(logs)[:, :, None]
    last = logs[-1]
    tails = jnp.exp(last[None, :] - logs) * steps
    scaled = values * tails[:, :, None]
    fresh = jnp.einsum('shp,sn->hpn', scaled, keys_b, precision=lax.Precision.HIGHEST)
    new_state = jnp.exp(last)[:, None, None] * state + fresh
    return (new_state, (local + carried).reshape(span, -1))

def mixer(proj, conv_weight, conv_bias, dt_bias, a_log, skip, gate_gain):
    length = proj.shape[0]
    inner_width = gate_gain.shape[0]
    state_size = (conv_bias.shape[0] - inner_width) // 2
    heads = dt_bias.shape[0]
    head_width = inner_width // heads
    taps = conv_weight.shape[0]
    gate = proj[:, :inner_width]
    conv_in = proj[:, inner_width:2 * inner_width + 2 * state_size]
    raw_steps = proj[:, 2 * inner_width + 2 * state_size:]
    padded = jnp.pad(conv_in, ((taps - 1, 0), (0, 0)))
    conv_sum = jnp.zeros_like(conv_in) + conv_bias
    for offset in range(taps):
        conv_sum = conv_sum + conv_weight[offset] * padded[offset:offset + length]
    act = jax.nn.silu(conv_sum)
    values = act[:, :inner_width]
    keys_b = act[:, inner_width:inner_width + state_size]
    keys_c = act[:, inner_width + state_size:]
    steps = jax.nn.softplus(raw_steps + dt_bias)
    decay_rate = -jnp.exp(a_log)
    blocks = length // STRETCH

    def advance(state, block_values, block_b, block_c, block_steps):
        return stretch_step(state, block_values.reshape(STRETCH, heads, head_width), block_b, block_c, block_steps, decay_rate)
    stepper = jax.checkpoint(advance)
    state = jnp.zeros((heads, head_width, state_size), jnp.float32)
    outputs = []
    for index in range(blocks):
        lower = index * STRETCH
        state, piece = stepper(state, values[lower:lower + STRETCH], keys_b[lower:lower + STRETCH], keys_c[lower:lower + STRETCH], steps[lower:lower + STRETCH])
        outputs.append(piece)
    scan_flat = jnp.concatenate(outputs, axis=0)
    skip_cols = jnp.repeat(skip, head_width)
    scan_out = scan_flat + skip_cols[None, :] * values
    gated = scan_out * jax.nn.silu(gate)
    return rms_scale(gated, gate_gain)

def branch(sequence, norm_gain, in_weight, conv_weight, conv_bias, dt_bias, a_log, skip, gate_gain, out_weight):
    normed = low(rms_scale(sequence, norm_gain))
    proj = low_back(jnp.dot(normed, in_weight, precision=lax.Precision.HIGHEST))
    mixed = low(mixer(proj, conv_weight, conv_bias, dt_bias, a_log, skip, gate_gain))
    return sequence + jnp.dot(mixed, out_weight, precision=lax.Precision.HIGHEST)

def reference(tokens, norm_gain, in_weight, conv_weight, conv_bias, dt_bias, a_log, skip, gate_gain, out_weight, cotangent):
    params = tuple((item.astype(jnp.float32) for item in (norm_gain, in_weight, conv_weight, conv_bias, dt_bias, a_log, skip, gate_gain, out_weight)))

    def per_sequence(totals, inputs_pair):
        sequence, seq_cot = inputs_pair
        result, pull = jax.vjp(branch, sequence.astype(jnp.float32), *params)
        grads = pull(seq_cot.astype(jnp.float32))
        new_totals = tuple((left + right for left, right in zip(totals, grads[1:])))
        return (new_totals, (result.astype(jnp.bfloat16), grads[0]))
    zeros = tuple((jnp.zeros(item.shape, jnp.float32) for item in params))
    totals, (output, input_grad) = lax.scan(per_sequence, zeros, (tokens, cotangent))
    return (output, input_grad, totals[0], totals[1], totals[2], totals[3], totals[4], totals[5], totals[6], totals[7], totals[8])
```

```python
import functools

import jax
import jax.numpy as jnp
from jax import lax
from jax.experimental import pallas as pl
from jax.experimental.pallas import tpu as pltpu
from jax.sharding import PartitionSpec as P

Q = 128
LANES = 128
HEAD = 64
EPS = 1e-05
F32 = jnp.float32
BF16 = jnp.bfloat16
HI = lax.Precision.HIGHEST
NEG = -1e30


def mm(a, b):
    return jnp.dot(a, b, preferred_element_type=F32)


def mm_t(a, b):
    return lax.dot_general(a, b, (((1,), (1,)), ((), ())), preferred_element_type=F32)


def softplus(v):
    return jnp.maximum(v, 0.0) + jnp.log1p(jnp.exp(-jnp.abs(v)))


def sigmoid(v):
    return 1.0 / (1.0 + jnp.exp(-v))


def tri_lower():
    rows = lax.broadcasted_iota(jnp.int32, (Q, Q), 0)
    cols = lax.broadcasted_iota(jnp.int32, (Q, Q), 1)
    return rows >= cols


def spread(table, lane):
    return jnp.broadcast_to(table[:, lane : lane + 1], (Q, LANES))


def fill_tables(dt, logs, dt_tab, log_tab, log_rows, low, groups, per):
    log_rows[...] = jnp.transpose(logs)
    for g in range(groups):
        shift = (LANES - (low + g) * per) % LANES
        dt_tab[g] = pltpu.roll(dt, shift, 1) if shift else dt
        log_tab[g] = pltpu.roll(logs, shift, 1) if shift else logs


def scan_forward(proj_ref, cw_ref, cb_ref, vec_ref, skip_ref, out_ref, sum_ref, start_ref,
                 shifted, act, state, dt_tab, log_tab, log_rows, *, inner, nstate, groups, per):
    first = pl.program_id(0) == 0
    conv = inner + 2 * nstate

    @pl.when(first)
    def _():
        shifted[0:8, :] = jnp.zeros((8, conv), F32)
        state[...] = jnp.zeros_like(state)

    shifted[8 : 8 + Q, :] = proj_ref[:, 0:conv]
    wide = 256
    for low in range(0, conv, wide):
        part = pl.ds(low, wide)
        total = cb_ref[0:1, part] + cw_ref[0:1, part] * shifted[5 : 5 + Q, part]
        for k in range(1, 4):
            total = total + cw_ref[k : k + 1, part] * shifted[5 + k : 5 + k + Q, part]
        sum_ref[:, part] = total
        act[:, part] = total * sigmoid(total)
    shifted[0:8, :] = shifted[Q : Q + 8, :]

    dt = softplus(proj_ref[:, conv : conv + LANES] + vec_ref[0:1, :])
    causal = tri_lower()
    logs = jnp.dot(causal.astype(F32), dt * vec_ref[1:2, :], precision=HI, preferred_element_type=F32)
    fill_tables(dt, logs, dt_tab, log_tab, log_rows, 0, groups, per)
    keys_b = act[:, inner : inner + nstate]
    keys_c = act[:, inner + nstate : conv].astype(BF16)
    b_cols = jnp.transpose(keys_b).astype(BF16)
    cross = mm(keys_c, b_cols)
    start_ref[...] = state[...].astype(BF16)
    span = per * HEAD
    low_half = lax.broadcasted_iota(jnp.int32, (Q, LANES), 1) < HEAD

    def group(g, carry):
        base = pl.multiple_of(g * span, span)
        dts, lgs = dt_tab[g], log_tab[g]
        carried = mm(keys_c, start_ref[:, pl.ds(base, span)])
        tails_all = []
        lasts = []
        for j in range(per // 2):
            cols = pl.ds(pl.multiple_of(base + j * LANES, LANES), LANES)
            h = g * per + 2 * j
            col0, col1 = spread(lgs, 2 * j), spread(lgs, 2 * j + 1)
            row0, row1 = log_rows[pl.ds(h, 1), :], log_rows[pl.ds(h + 1, 1), :]
            values = act[:, cols]
            stepped = (values * jnp.where(low_half, spread(dts, 2 * j), spread(dts, 2 * j + 1)))
            stepped_b = stepped.astype(BF16)
            mix0 = (jnp.exp(jnp.where(causal, col0 - row0, NEG)) * cross).astype(BF16)
            mix1 = (jnp.exp(jnp.where(causal, col1 - row1, NEG)) * cross).astype(BF16)
            zero = jnp.zeros_like(stepped_b)
            pairs = jnp.concatenate(
                [jnp.where(low_half, stepped_b, zero), jnp.where(low_half, zero, stepped_b)], axis=0)
            local = mm(jnp.concatenate([mix0, mix1], axis=1), pairs)
            both = jnp.where(low_half, col0, col1)
            last = both[Q - 1 : Q, :]
            out = local + carried[:, j * LANES : (j + 1) * LANES] * jnp.exp(both)
            out_ref[:, cols] = out + skip_ref[0:1, cols] * values
            tails_all.append((stepped * jnp.exp(last - both)).astype(BF16))
            lasts.append(jnp.exp(last))
        fresh = mm(b_cols, jnp.concatenate(tails_all, axis=1))
        cols = pl.ds(base, span)
        state[:, cols] = state[:, cols] * jnp.concatenate(lasts, axis=1) + fresh
        return carry

    lax.fori_loop(0, groups, group, 0)


def run_scan_forward(proj, cw, cb, vec, skip_cols, inner, nstate, groups, per):
    length = proj.shape[0]
    blocks = length // Q
    conv = inner + 2 * nstate
    whole = lambda shape: pl.BlockSpec(shape, lambda i: (0, 0))
    rows = lambda width: pl.BlockSpec((Q, width), lambda i: (i, 0))
    return pl.pallas_call(
        functools.partial(scan_forward, inner=inner, nstate=nstate, groups=groups, per=per),
        grid=(blocks,),
        in_specs=[rows(proj.shape[1]), whole(cw.shape), whole(cb.shape), whole(vec.shape), whole(skip_cols.shape)],
        out_specs=[rows(inner), rows(conv), pl.BlockSpec((nstate, inner), lambda i: (i, 0))],
        out_shape=[
            jax.ShapeDtypeStruct((length, inner), F32),
            jax.ShapeDtypeStruct((length, conv), F32),
            jax.ShapeDtypeStruct((blocks * nstate, inner), BF16),
        ],
        scratch_shapes=[
            pltpu.VMEM((Q + 8, conv), F32),
            pltpu.VMEM((Q, conv), F32),
            pltpu.VMEM((nstate, inner), F32),
            pltpu.VMEM((groups, Q, LANES), F32),
            pltpu.VMEM((groups, Q, LANES), F32),
            pltpu.VMEM((LANES, Q), F32),
        ],
        compiler_params=pltpu.CompilerParams(vmem_limit_bytes=60 << 20),
        cost_estimate=pl.CostEstimate(flops=12_000_000_000, bytes_accessed=60_000_000, transcendentals=20_000_000),
        name="scan_forward",
    )(proj, cw, cb, vec, skip_cols)


def piece_copies(place_ref, pieces, refs, target, sems):
    copies = []
    for index, (start, half, size, lane) in enumerate(pieces):
        rows, cols = refs[index].shape
        if half is not None:
            start = pl.multiple_of(start + jnp.bitwise_xor(place_ref[1], half) * size, 16)
        window = target.at[pl.ds(start, rows), pl.ds(lane, cols)]
        copies.append(pltpu.make_async_copy(refs[index], window, sems.at[index]))
    return copies


def load_pieces(*args):
    for copy in piece_copies(*args):
        copy.start()


def wait_pieces(*args):
    for copy in piece_copies(*args):
        copy.wait()


def columns_of(place_ref, position, order, width):
    return pl.ds(pl.multiple_of(jnp.bitwise_xor(place_ref[0], order[position]) * width, LANES), width)


def project_in(place_ref, tok_ref, gain_ref, *rest, pieces, order):
    refs, (normed_ref, proj_ref, weight, sems) = rest[: len(pieces)], rest[len(pieces) :]
    first = pl.program_id(0) == 0

    @pl.when(first)
    def _():
        load_pieces(place_ref, pieces, refs, weight, sems)

    width = tok_ref.shape[1] // len(order)
    tok = tok_ref[...].astype(F32)
    scale = lax.rsqrt(jnp.mean(tok * tok, axis=1, keepdims=True) + EPS)
    for position in range(len(order)):
        cols = columns_of(place_ref, position, order, width)
        value = tok_ref[:, cols].astype(F32) * scale * gain_ref[0:1, cols]
        normed_ref[:, position * width : (position + 1) * width] = value.astype(BF16)

    @pl.when(first)
    def _():
        wait_pieces(place_ref, pieces, refs, weight, sems)

    total = proj_ref.shape[1]
    step = 384
    for low in range(0, total, step):
        proj_ref[:, low : low + step] = mm_t(normed_ref[...], weight[low : low + step, :])


def grid_of(grid, in_specs, out_specs, scratch):
    return pltpu.PrefetchScalarGridSpec(
        num_scalar_prefetch=1, grid=grid, in_specs=in_specs, out_specs=out_specs, scratch_shapes=scratch)


def anywhere(count):
    return [pl.BlockSpec(memory_space=pl.ANY)] * count


def row_block(block, width):
    return pl.BlockSpec((block, width), lambda i, s: (i, 0))


def fixed(shape):
    return pl.BlockSpec(shape, lambda i, s: (0,) * len(shape))


def run_project_in(place, tok, gain, weight, total, order, block=256):
    pieces, arrays = weight
    length, width = tok.shape
    return pl.pallas_call(
        functools.partial(project_in, pieces=pieces, order=order),
        grid_spec=grid_of(
            (length // block,),
            [row_block(block, width), fixed(gain.shape)] + anywhere(len(pieces)),
            [row_block(block, width), row_block(block, total)],
            [pltpu.VMEM((total, width), BF16), pltpu.SemaphoreType.DMA((len(pieces),))],
        ),
        out_shape=[jax.ShapeDtypeStruct((length, width), BF16), jax.ShapeDtypeStruct((length, total), F32)],
        compiler_params=pltpu.CompilerParams(vmem_limit_bytes=50 << 20),
        cost_estimate=pl.CostEstimate(flops=20_000_000_000, bytes_accessed=30_000_000, transcendentals=1000),
        name="project_in",
    )(place, tok, gain, *arrays)


def gating(place_ref, normed_ref, cot_ref, scan_ref, gain_ref, *rest, wg_pieces, ow_pieces, order):
    n_g, n_o = len(wg_pieces), len(ow_pieces)
    wg_refs, ow_refs = rest[:n_g], rest[n_g : n_g + n_o]
    (mixed_ref, dscan_ref, dgate_ref, dgain_ref, wg, ow, gate_s, gated_s, scaled_s,
     g_sems, o_sems) = rest[n_g + n_o :]
    inner = wg.shape[0]
    parts = len(order)
    width = inner // parts
    first = pl.program_id(0) == 0

    @pl.when(first)
    def _():
        load_pieces(place_ref, wg_pieces, wg_refs, wg, g_sems)
        load_pieces(place_ref, ow_pieces, ow_refs, ow, o_sems)
        dgain_ref[...] = jnp.zeros_like(dgain_ref)
        wait_pieces(place_ref, wg_pieces, wg_refs, wg, g_sems)

    def fold(v):
        total = v[:, 0:LANES]
        for low in range(LANES, v.shape[1], LANES):
            total = total + v[:, low : low + LANES]
        return total

    power = None
    for p in range(parts):
        cols = slice(p * width, (p + 1) * width)
        gate = mm_t(normed_ref[...], wg[cols, :])
        gated = scan_ref[:, cols] * (gate * sigmoid(gate))
        gate_s[:, cols] = gate
        gated_s[:, cols] = gated
        term = fold(gated * gated)
        power = term if power is None else power + term
    scale = lax.rsqrt(jnp.sum(power, axis=1, keepdims=True) / inner + EPS)

    @pl.when(first)
    def _():
        wait_pieces(place_ref, ow_pieces, ow_refs, ow, o_sems)

    match = None
    for p in range(parts):
        true = columns_of(place_ref, p, order, width)
        rows = slice(p * width, (p + 1) * width)
        grad = mm_t(cot_ref[...], ow[rows, :])
        gated = gated_s[:, true]
        gain = gain_ref[0:1, true]
        unit = gated * scale
        mixed_ref[:, rows] = (unit * gain).astype(BF16)
        dgain_ref[0:1, true] += jnp.sum(grad * unit, axis=0, keepdims=True)
        scaled = grad * gain
        scaled_s[:, true] = scaled
        term = fold(scaled * gated)
        match = term if match is None else match + term
    pull = jnp.sum(match, axis=1, keepdims=True) * (scale * scale) / inner
    for p in range(parts):
        cols = slice(p * width, (p + 1) * width)
        gate = gate_s[:, cols]
        sig = sigmoid(gate)
        silu = gate * sig
        dgated = scale * (scaled_s[:, cols] - gated_s[:, cols] * pull)
        dscan_ref[:, cols] = dgated * silu
        dgate_ref[:, cols] = (dgated * scan_ref[:, cols] * (sig + silu * (1.0 - sig))).astype(BF16)


def run_gating(place, normed, gate_weight, out_weight, cot, scan_out, gain, order, block=256):
    wg_pieces, wg_arrays = gate_weight
    ow_pieces, ow_arrays = out_weight
    length, width = normed.shape
    inner = scan_out.shape[1]
    return pl.pallas_call(
        functools.partial(gating, wg_pieces=wg_pieces, ow_pieces=ow_pieces, order=order),
        grid_spec=grid_of(
            (length // block,),
            [row_block(block, width), row_block(block, width), row_block(block, inner), fixed((1, inner))]
            + anywhere(len(wg_pieces) + len(ow_pieces)),
            [row_block(block, inner), row_block(block, inner), row_block(block, inner), fixed((1, inner))],
            [pltpu.VMEM((inner, width), BF16), pltpu.VMEM((inner, width), BF16)]
            + [pltpu.VMEM((block, inner), F32)] * 3
            + [pltpu.SemaphoreType.DMA((len(wg_pieces),)), pltpu.SemaphoreType.DMA((len(ow_pieces),))],
        ),
        out_shape=[
            jax.ShapeDtypeStruct((length, inner), BF16),
            jax.ShapeDtypeStruct((length, inner), F32),
            jax.ShapeDtypeStruct((length, inner), BF16),
            jax.ShapeDtypeStruct((1, inner), F32),
        ],
        compiler_params=pltpu.CompilerParams(vmem_limit_bytes=62 << 20),
        cost_estimate=pl.CostEstimate(flops=40_000_000_000, bytes_accessed=70_000_000, transcendentals=10_000_000),
        name="gating",
    )(place, normed, cot, scan_out, gain, *wg_arrays, *ow_arrays)


def gate_back(place_ref, dgate_ref, *rest, pieces):
    refs, (grad_ref, weight, sems) = rest[: len(pieces)], rest[len(pieces) :]

    @pl.when(pl.program_id(0) == 0)
    def _():
        load_pieces(place_ref, pieces, refs, weight, sems)
        wait_pieces(place_ref, pieces, refs, weight, sems)

    step = 384
    for low in range(0, grad_ref.shape[1], step):
        grad_ref[:, low : low + step] = mm(dgate_ref[...], weight[:, low : low + step])


def run_gate_back(place, dgate, model, weight, block=256):
    pieces, arrays = weight
    length, inner = dgate.shape
    return pl.pallas_call(
        functools.partial(gate_back, pieces=pieces),
        grid_spec=grid_of(
            (length // block,),
            [row_block(block, inner)] + anywhere(len(pieces)),
            row_block(block, model),
            [pltpu.VMEM((inner, model), BF16), pltpu.SemaphoreType.DMA((len(pieces),))],
        ),
        out_shape=jax.ShapeDtypeStruct((length, model), F32),
        compiler_params=pltpu.CompilerParams(vmem_limit_bytes=40 << 20),
        cost_estimate=pl.CostEstimate(flops=16_000_000_000, bytes_accessed=22_000_000, transcendentals=0),
        name="gate_back",
    )(place, dgate, *arrays)


def input_back(place_ref, part_ref, tok_ref, cot_ref, gain_ref, *rest, count, pieces, order):
    dproj_refs, rest = rest[:count], rest[count:]
    refs, (grad_ref, dgain_ref, weight, dn, sems) = rest[: len(pieces)], rest[len(pieces) :]
    first = pl.program_id(0) == 0

    @pl.when(first)
    def _():
        load_pieces(place_ref, pieces, refs, weight, sems)
        dgain_ref[...] = jnp.zeros_like(dgain_ref)
        wait_pieces(place_ref, pieces, refs, weight, sems)

    model = tok_ref.shape[1]
    width = model // len(order)
    tok = tok_ref[...].astype(F32)
    scale = lax.rsqrt(jnp.mean(tok * tok, axis=1, keepdims=True) + EPS)
    match = None
    for position in range(len(order)):
        spot = slice(position * width, (position + 1) * width)
        true = columns_of(place_ref, position, order, width)
        grad, low = part_ref[:, spot], 0
        for ref in dproj_refs:
            grad = grad + mm(ref[...], weight[low : low + ref.shape[1], spot])
            low += ref.shape[1]
        value = tok_ref[:, true].astype(F32)
        dgain_ref[0:1, true] += jnp.sum(grad * (value * scale), axis=0, keepdims=True)
        grad = grad * gain_ref[0:1, true]
        dn[:, spot] = grad
        term = jnp.sum(grad * value, axis=1, keepdims=True)
        match = term if match is None else match + term
    pull = match * (scale * scale * scale) / model
    for position in range(len(order)):
        spot = slice(position * width, (position + 1) * width)
        true = columns_of(place_ref, position, order, width)
        value = tok_ref[:, true].astype(F32)
        grad_ref[:, true] = cot_ref[:, true].astype(F32) + (scale * dn[:, spot] - value * pull)


def run_input_back(place, part, dprojs, tok, cot, gain, weight, order, block=256):
    pieces, arrays = weight
    length, model = tok.shape
    widths = [d.shape[1] for d in dprojs]
    return pl.pallas_call(
        functools.partial(input_back, count=len(dprojs), pieces=pieces, order=order),
        grid_spec=grid_of(
            (length // block,),
            [row_block(block, model), row_block(block, model), row_block(block, model), fixed((1, model))]
            + [row_block(block, w) for w in widths] + anywhere(len(pieces)),
            [row_block(block, model), fixed((1, model))],
            [pltpu.VMEM((sum(widths), model), BF16), pltpu.VMEM((block, model), F32),
             pltpu.SemaphoreType.DMA((len(pieces),))],
        ),
        out_shape=[jax.ShapeDtypeStruct((length, model), F32), jax.ShapeDtypeStruct((1, model), F32)],
        compiler_params=pltpu.CompilerParams(vmem_limit_bytes=50 << 20),
        cost_estimate=pl.CostEstimate(flops=22_000_000_000, bytes_accessed=46_000_000, transcendentals=1000),
        name="input_back",
    )(place, part, tok, cot, gain, *dprojs, *arrays)


def project_out(place_ref, mixed_ref, tok_ref, *rest, pieces):
    refs, (out_ref, weight, sems) = rest[: len(pieces)], rest[len(pieces) :]

    @pl.when(pl.program_id(0) == 0)
    def _():
        load_pieces(place_ref, pieces, refs, weight, sems)
        wait_pieces(place_ref, pieces, refs, weight, sems)

    step = 384
    for low in range(0, out_ref.shape[1], step):
        cols = slice(low, low + step)
        out_ref[:, cols] = (tok_ref[:, cols].astype(F32) + mm(mixed_ref[...], weight[:, cols])).astype(BF16)


def run_project_out(place, mixed, tok, weight, block=256):
    pieces, arrays = weight
    length, model = tok.shape
    inner = mixed.shape[1]
    return pl.pallas_call(
        functools.partial(project_out, pieces=pieces),
        grid_spec=grid_of(
            (length // block,),
            [row_block(block, inner), row_block(block, model)] + anywhere(len(pieces)),
            row_block(block, model),
            [pltpu.VMEM((inner, model), BF16), pltpu.SemaphoreType.DMA((len(pieces),))],
        ),
        out_shape=jax.ShapeDtypeStruct((length, model), BF16),
        compiler_params=pltpu.CompilerParams(vmem_limit_bytes=40 << 20),
        cost_estimate=pl.CostEstimate(flops=14_000_000_000, bytes_accessed=20_000_000, transcendentals=0),
        name="project_out",
    )(place, mixed, tok, *arrays)


def scan_backward(proj_ref, tail_ref, sum_ref, keys_ref, out_ref, dout_ref, start_ref, cw_ref, cwk_ref, vec_ref,
                  skip_ref, pick_ref, *rest, nstate, low, groups, per, begin, last):
    if not begin:
        old_cross_ref, old_keys_ref, old_raw_ref = rest[:3]
        rest = rest[3:]
    dproj_ref, dcw_ref, dcb_ref, dskip_ref, dvec_ref = rest[:5]
    rest = rest[5:]
    if not last:
        cross_ref, keys_ref_out, raw_ref = rest[:3]
        rest = rest[3:]
    dsum, dstate, edge, logs_v, tails_v, steps_v, dt_tab, log_tab, log_rows, dcross, dkeys = rest
    first = pl.program_id(0) == 0
    span_all = groups * per * HEAD
    conv = dsum.shape[1]

    @pl.when(first)
    def _():
        dsum[Q : Q + 8, :] = jnp.zeros((8, conv), F32)
        dstate[...] = jnp.zeros_like(dstate)
        edge[...] = jnp.zeros_like(edge)
        dcw_ref[...] = jnp.zeros_like(dcw_ref)
        dcb_ref[...] = jnp.zeros_like(dcb_ref)
        dskip_ref[...] = jnp.zeros_like(dskip_ref)
        dvec_ref[...] = jnp.zeros_like(dvec_ref)

    raw = tail_ref[:, 2 * nstate : 2 * nstate + LANES] + vec_ref[0:1, :]
    dt = softplus(raw)
    lower = tri_lower()
    rate = vec_ref[1:2, :]
    logs = jnp.dot(lower.astype(F32), dt * rate, precision=HI, preferred_element_type=F32)
    fill_tables(dt, logs, dt_tab, log_tab, log_rows, low, groups, per)
    sum_b = keys_ref[:, 0:nstate]
    sum_c = keys_ref[:, nstate : 2 * nstate]
    sig_b, sig_c = sigmoid(sum_b), sigmoid(sum_c)
    keys_b32, keys_c32 = sum_b * sig_b, sum_c * sig_c
    keys_b, keys_c = keys_b32.astype(BF16), keys_c32.astype(BF16)
    c_cols = jnp.transpose(keys_c32).astype(BF16)
    cross = mm(keys_b, c_cols)
    span = per * HEAD
    low_half = lax.broadcasted_iota(jnp.int32, (Q, LANES), 1) < HEAD
    upper = lax.broadcasted_iota(jnp.int32, (Q, Q), 0) <= lax.broadcasted_iota(jnp.int32, (Q, Q), 1)
    if not begin:
        dcross[...] = old_cross_ref[...]
        dkeys[...] = old_keys_ref[...]
    else:
        dcross[...] = jnp.zeros_like(dcross)
        dkeys[...] = jnp.zeros_like(dkeys)

    def group(g, carry):
        base = pl.multiple_of(g * span, span)
        whole = pl.ds(base, span)
        dts, lgs = dt_tab[g], log_tab[g]
        dstate_b = dstate[:, whole].astype(BF16)
        from_state = mm(keys_b, dstate_b)
        tails_all, outs_all, lasts = [], [], []
        dcr = None
        for j in range(per // 2):
            cols = pl.ds(pl.multiple_of(base + j * LANES, LANES), LANES)
            h = (low + g) * per + 2 * j
            col0, col1 = spread(lgs, 2 * j), spread(lgs, 2 * j + 1)
            row0, row1 = log_rows[pl.ds(h, 1), :], log_rows[pl.ds(h + 1, 1), :]
            total = sum_ref[:, cols]
            sig = sigmoid(total)
            values = total * sig
            step = jnp.where(low_half, spread(dts, 2 * j), spread(dts, 2 * j + 1))
            stepped = values * step
            stepped_b = stepped.astype(BF16)
            dout = dout_ref[:, cols]
            dout_b = dout.astype(BF16)
            decay0 = jnp.exp(jnp.where(upper, row0 - col0, NEG))
            decay1 = jnp.exp(jnp.where(upper, row1 - col1, NEG))
            mix = jnp.concatenate([(decay0 * cross).astype(BF16), (decay1 * cross).astype(BF16)], axis=1)
            zero = jnp.zeros_like(dout_b)
            douts = jnp.concatenate(
                [jnp.where(low_half, dout_b, zero), jnp.where(low_half, zero, dout_b)], axis=0)
            local = mm(mix, douts)
            dmix = mm_t(stepped_b, douts)
            term = dmix[:, 0:Q] * decay0 + dmix[:, Q : 2 * Q] * decay1
            dcr = term if dcr is None else dcr + term
            both = jnp.where(low_half, col0, col1)
            last = both[Q - 1 : Q, :]
            tail = jnp.exp(last - both)
            passed = from_state[:, j * LANES : (j + 1) * LANES] * tail
            dstepped = local + passed
            skip = skip_ref[0:1, cols]
            scan = out_ref[:, cols] - skip * values
            logs_v[:, cols] = dout_b.astype(F32) * scan - stepped_b.astype(F32) * local
            tails_v[:, cols] = stepped * passed
            steps_v[:, cols] = dstepped * values
            dvalues = dstepped * step + dout * skip
            dskip_ref[0:1, cols] += jnp.sum(dout * values, axis=0, keepdims=True)
            dsum[0:Q, cols] = dvalues * (sig + values * (1.0 - sig))
            tails_all.append((stepped * tail).astype(BF16))
            outs_all.append((dout * jnp.exp(both)).astype(BF16))
            lasts.append(jnp.exp(last))
        dcross[...] += dcr
        outs = jnp.concatenate(outs_all, axis=1)
        starts = start_ref[:, whole]
        dkeys[:, nstate : 2 * nstate] += mm_t(outs, starts)
        dkeys[:, 0:nstate] += mm_t(jnp.concatenate(tails_all, axis=1), dstate_b)
        kept = dstate[:, whole] * jnp.concatenate(lasts, axis=1)
        edge[0:1, whole] = jnp.sum(kept * starts.astype(F32), axis=0, keepdims=True)
        dstate[:, whole] = kept + mm(c_cols, outs)
        return carry

    lax.fori_loop(0, groups, group, 0)

    if last:
        dcr = dcross[...]
        exact = lambda u, v: jnp.dot(u, v, precision=HI, preferred_element_type=F32)
        d_b = dkeys[:, 0:nstate] + exact(dcr, keys_c32)
        d_c = dkeys[:, nstate : 2 * nstate] + exact(jnp.transpose(dcr), keys_b32)
        dsum[0:Q, span_all : span_all + nstate] = d_b * (sig_b + keys_b32 * (1.0 - sig_b))
        dsum[0:Q, span_all + nstate : conv] = d_c * (sig_c + keys_c32 * (1.0 - sig_c))
    else:
        cross_ref[...] = dcross[...]
        keys_ref_out[...] = dkeys[...]

    def reduce_heads(v):
        high = v.astype(BF16)
        low = (v - high.astype(F32)).astype(BF16)
        return mm(high, pick_ref[...]) + mm(low, pick_ref[...])

    dlogs = reduce_heads(logs_v[...])
    dtails = reduce_heads(tails_v[...])
    dlogit = (
        jnp.dot(upper.astype(F32), dlogs, precision=HI, preferred_element_type=F32)
        + jnp.dot(1.0 - upper.astype(F32), dtails, precision=HI, preferred_element_type=F32)
        + reduce_heads(edge[...])[0:1, :]
    )
    dstep = reduce_heads(steps_v[...]) + dlogit * rate
    draw = dstep * sigmoid(raw)
    dvec_ref[0:1, :] += jnp.sum(draw, axis=0, keepdims=True)
    dvec_ref[1:2, :] += jnp.sum(dlogit * dt * rate, axis=0, keepdims=True)
    if last:
        dproj_ref[:, conv : conv + LANES] = (draw + old_raw_ref[...]).astype(BF16)
    elif begin:
        raw_ref[...] = draw
    else:
        raw_ref[...] = draw + old_raw_ref[...]

    wide = 256
    for start in range(0, conv, wide):
        part = pl.ds(start, wide)
        if start < span_all:
            source, taps_ref, local = proj_ref, cw_ref, part
        else:
            source, taps_ref, local = tail_ref, cwk_ref, pl.ds(start - span_all, wide)
        taken = source[:, local]
        total = None
        for k in range(4):
            moved = dsum[3 - k : 3 - k + Q, part]
            dcw_ref[k : k + 1, part] += jnp.sum(taken * moved, axis=0, keepdims=True)
            term = taps_ref[k : k + 1, local] * moved
            total = term if total is None else total + term
            if k == 3:
                dcb_ref[0:1, part] += jnp.sum(moved, axis=0, keepdims=True)
        dproj_ref[:, part] = total.astype(BF16)
    dsum[Q : Q + 8, :] = dsum[0:8, :]


def run_scan_backward(proj, sums, scan_out, dscan, starts, cw, vec, skip_cols, pick, inner, nstate, low, groups, per,
                      previous, last):
    length = proj.shape[0]
    blocks = length // Q
    span = groups * per * HEAD
    begin = previous is None
    conv = span + (2 * nstate if last else 0)
    where = low * per * HEAD // span
    whole = lambda shape: pl.BlockSpec(shape, lambda i: (0, 0))
    rows = lambda width, col=0: pl.BlockSpec((Q, width), lambda i: (blocks - 1 - i, col))
    part = lambda height: pl.BlockSpec((height, span), lambda i: (0, where))
    tail = 2 * nstate + LANES
    out_specs = [rows(conv + (LANES if last else 0)), whole((4, conv)), whole((1, conv)), whole((1, span)),
                 whole((8, LANES))]
    out_shape = [
        jax.ShapeDtypeStruct((length, conv + (LANES if last else 0)), BF16),
        jax.ShapeDtypeStruct((4, conv), F32),
        jax.ShapeDtypeStruct((1, conv), F32),
        jax.ShapeDtypeStruct((1, span), F32),
        jax.ShapeDtypeStruct((8, LANES), F32),
    ]
    carried = [rows(Q), rows(2 * nstate), rows(LANES)]
    if not last:
        out_specs += carried
        out_shape += [jax.ShapeDtypeStruct((length, w), F32) for w in (Q, 2 * nstate, LANES)]
    return pl.pallas_call(
        functools.partial(scan_backward, nstate=nstate, low=low, groups=groups, per=per, begin=begin, last=last),
        grid=(blocks,),
        in_specs=[
            rows(span, where), rows(tail, inner // tail), rows(span, where), rows(2 * nstate, inner // (2 * nstate)),
            rows(span, where), rows(span, where),
            pl.BlockSpec((nstate, span), lambda i: (blocks - 1 - i, where)),
            part(4), pl.BlockSpec((4, 2 * nstate), lambda i: (0, inner // (2 * nstate))),
            whole(vec.shape), part(1), pl.BlockSpec((span, LANES), lambda i: (where, 0)),
        ] + ([] if begin else carried),
        out_specs=out_specs,
        out_shape=out_shape,
        scratch_shapes=[
            pltpu.VMEM((Q + 8, conv), F32),
            pltpu.VMEM((nstate, span), F32),
            pltpu.VMEM((8, span), F32),
            pltpu.VMEM((Q, span), F32),
            pltpu.VMEM((Q, span), F32),
            pltpu.VMEM((Q, span), F32),
            pltpu.VMEM((groups, Q, LANES), F32),
            pltpu.VMEM((groups, Q, LANES), F32),
            pltpu.VMEM((LANES, Q), F32),
            pltpu.VMEM((Q, Q), F32),
            pltpu.VMEM((Q, 2 * nstate), F32),
        ],
        compiler_params=pltpu.CompilerParams(vmem_limit_bytes=50 << 20),
        cost_estimate=pl.CostEstimate(flops=40_000_000_000, bytes_accessed=40_000_000, transcendentals=15_000_000),
        name="scan_backward",
    )(proj, proj, sums, sums, scan_out, dscan, starts, cw, cw, vec, skip_cols, pick, *(previous or ()))


def bits_of(size):
    return [1 << b for b in range(size.bit_length() - 1)]


def swap(value, axis, bit, size):
    return lax.ppermute(value, axis, [(i, i ^ bit) for i in range(size)])


def after(value, *deps):
    return lax.optimization_barrier((value,) + deps)[0] if deps else value


def order_of(size):
    flipped = []
    for index in range(size):
        value = 0
        for low, high in zip(bits_of(size), reversed(bits_of(size))):
            value |= high if index & low else 0
        flipped.append(value)
    return flipped


class Gather:
    def __init__(self, shard, order, rep_index, groups, copies, lanes, chunks):
        self.order, self.groups, self.copies = order, groups, copies
        self.size = shard.shape
        self.lanes = lanes
        self.half = shard.shape[0] // 2
        self.rows = self.half // chunks
        self.shard = shard
        parity = rep_index & 1
        self.mine = [lax.dynamic_slice_in_dim(shard, parity * self.half + c * self.rows, self.rows, 0)
                     for c in range(chunks)]
        self.there, self.across = [None] * chunks, [None] * chunks

    def far(self, chunk, *deps):
        value = after(self.mine[chunk], *deps)
        self.there[chunk] = swap(value, "shard", 2, self.groups)

    def side(self, chunk):
        self.across[chunk] = swap(self.there[chunk], "rep", 1, self.copies)

    def finish(self):
        have = {0: [(0, None, 0, self.shard)]}
        have[2] = [(c * self.rows, h, self.half, v) for h, vs in ((0, self.there), (1, self.across))
                   for c, v in enumerate(vs)]
        for source in (0, 2):
            have[source ^ 1] = [(r, h, s, swap(v, "shard", 1, self.groups)) for r, h, s, v in have[source]]
        pieces, arrays = [], []
        for position, source in enumerate(self.order):
            for row, half, size, value in have[source]:
                if self.lanes:
                    pieces.append((row, half, size, position * self.size[1]))
                else:
                    pieces.append((row + position * self.size[0], half, size, 0))
                arrays.append(value)
        return tuple(pieces), tuple(arrays)


class Total:
    def __init__(self, kept, sent, axis, rep_index, groups, copies):
        self.axis, self.rep_index = axis, rep_index
        self.stages = [("shard", bit, groups) for bit in bits_of(groups)]
        self.stages += [("rep", bit, copies) for bit in bits_of(copies)]
        self.back = list(reversed(self.stages[len(bits_of(groups)) :]))
        self.value, self.out = kept, sent
        self.fly()

    def fly(self):
        self.coming = swap(self.out, *self.stages[0])

    def step(self, *deps):
        coming = after(self.coming, *deps)
        self.stages.pop(0)
        value = self.value
        if not self.stages:
            self.value = (value.astype(F32) + coming.astype(F32)).astype(BF16)
            self.out = self.value
            return self.out
        name, bit, _ = self.stages[0]
        if name == "shard":
            half = value.shape[self.axis] // 2
            low, high = 0, half
            axis = self.axis
        else:
            half = value.shape[0] // 2
            turn = (self.rep_index & bit) != 0
            low = jnp.where(turn, half, 0)
            high = half - low
            axis = 0
        cut = lambda v, start: lax.dynamic_slice_in_dim(v, start, half, axis).astype(F32)
        self.out = (cut(value, high) + cut(coming, high)).astype(BF16)
        self.value = cut(value, low) + cut(coming, low)
        self.fly()
        return self.out

    def widen(self, *deps):
        name, bit, size = self.back.pop(0)
        other = swap(after(self.value, *deps), name, bit, size)
        turn = (self.rep_index & bit) != 0
        low, high = jnp.where(turn, other, self.value), jnp.where(turn, self.value, other)
        if self.back:
            self.value = jnp.concatenate([low, high])
        else:
            self.value = [low.astype(F32), high.astype(F32)]
        return self.value


def outer(left, right):
    return lax.dot_general(left, right, (((0,), (0,)), ((), ())), preferred_element_type=F32).astype(BF16)


def on_device(groups, copies, tokens, norm_gain, in_weight, conv_weight, conv_bias, dt_bias, a_log, skip, gate_gain,
              out_weight, cotangent):
    if tokens.shape[0] != 1 or groups != 4:
        raise ValueError("unexpected sizes")
    order = order_of(groups)
    shard_index = lax.axis_index("shard")
    rep_index = lax.axis_index("rep")
    tok, cot = tokens[0], cotangent[0]
    inner = gate_gain.shape[0] * groups
    conv = conv_bias.shape[0] * groups
    heads = dt_bias.shape[0] * groups
    nstate = (conv - inner) // 2
    model = tok.shape[1]
    taps = conv_weight.shape[0]
    outputs_all = in_weight.shape[1]
    place = jnp.stack([shard_index, rep_index & 1]).astype(jnp.int32)

    turned = in_weight.T
    total = conv + LANES
    conv_part = jnp.pad(turned[inner:], ((0, total + inner - outputs_all), (0, 0)))
    make = lambda shard, lanes, chunks: Gather(shard, order, rep_index, groups, copies, lanes, chunks)
    wc = make(conv_part, True, 2)
    wg = make(turned[:inner], True, 1)
    ow = make(out_weight, False, 1)

    small = (norm_gain, conv_bias, dt_bias, a_log, skip, gate_gain, conv_weight)
    packed = jnp.concatenate([v.reshape(-1) for v in small])
    wc.far(0)
    wc.far(1, wc.there[0])
    wc.side(0)
    wc.side(1)
    wg.far(0, wc.there[1])
    ow.far(0, wc.across[1])
    wg.side(0)
    ow.side(0)
    rows = [packed, swap(packed, "shard", 1, groups)]
    far = swap(packed, "shard", 2, groups)
    rows += [far, swap(far, "shard", 1, groups)]
    for bit in bits_of(groups):
        turn = (shard_index & bit) != 0
        rows = [jnp.where(turn, rows[j ^ bit], rows[j]) for j in range(groups)]
    everyone = jnp.stack(rows).astype(F32)
    parts, low = [], 0
    for v in small:
        parts.append(everyone[:, low : low + v.size])
        low += v.size
    gain, cb, db, al, sk, gg = (v.reshape(-1) for v in parts[:6])
    cw = parts[6].reshape(groups, taps, -1).transpose(1, 0, 2).reshape(taps, conv)
    gain, cb, gg = gain[None], cb[None], gg[None]
    vec = jnp.pad(jnp.stack([db, -jnp.exp(al)]), ((0, 6), (0, LANES - heads)))
    skip_cols = jnp.repeat(sk, inner // heads)[None]
    pick = (jnp.arange(inner)[:, None] // (inner // heads) == jnp.arange(LANES)[None]).astype(BF16)

    wc, wg, ow = wc.finish(), wg.finish(), ow.finish()
    normed, proj = run_project_in(place, tok, gain, wc, total, order)
    per = 8
    scan_out, sums, starts = run_scan_forward(proj, cw, cb, vec, skip_cols, inner, nstate, heads // per, per)
    mixed, dscan, dgate, dgg = run_gating(place, normed, wg, ow, cot, scan_out, gg, order)

    chain = lambda kept, sent, axis: Total(kept, sent, axis, rep_index, groups, copies)
    half = inner // 2
    out_sent = outer(mixed[:, half:], cot)
    o = chain(outer(mixed[:, :half], cot), out_sent, 0)
    half = model // 2
    left, right = normed[:, :half], normed[:, half:]
    gate_sent = outer(dgate, right)
    g = chain(outer(dgate, left), gate_sent, 1)

    blocks = heads // per
    cuts = [blocks * v // 3 for v in range(4)]
    marks = [o.step(g.value)]
    marks.append(g.step(*marks))
    chains, grads, carried = [o, g], [], None
    for index in range(3):
        low, high = cuts[index], cuts[index + 1]
        last = index == 2
        found = run_scan_backward(
            proj, sums, scan_out, after(dscan, *marks), starts, cw, vec, skip_cols, pick, inner, nstate, low,
            high - low, per, carried, last)
        grads.append(found[:5])
        carried = tuple(found[5:])
        marks = []
        for old in chains[: 1 if index == 0 else None]:
            marks.append(old.step(found[0], *marks))
        dproj = after(found[0], *marks)
        sent = outer(dproj, right)
        kept = outer(dproj, left)
        new = chain(kept, sent, 1)
        marks.append(new.step(kept))
        chains.append(new)

    def exchange(value):
        for axis, size in (("shard", groups), ("rep", copies)):
            for bit in bits_of(size):
                value = value + swap(value, axis, bit, size)
        return value

    def advance(*fence):
        moved = []
        for old in chains:
            if old.stages:
                moved.append(old.step(*fence, *moved))
            elif old.back:
                old.widen(*fence)
        return moved

    output = run_project_out(place, after(mixed, *marks), tok, ow)
    marks = advance(output)
    part = run_gate_back(place, after(dgate, *marks), model, wg)
    marks = advance(part)
    input_grad, dgain = run_input_back(place, after(part, *marks), [v[0] for v in grads], tok, cot, gain, wc, order)
    advance(dgain)
    while any(old.stages or old.back for old in chains):
        advance()

    in_total = jnp.concatenate([v for old in chains[1:] for v in old.value])[:outputs_all].T
    out_total = jnp.concatenate(o.value)

    dcw = jnp.concatenate([v[1] for v in grads], axis=1)
    dcb = jnp.concatenate([v[2][0] for v in grads])
    dskip = jnp.concatenate([v[3][0] for v in grads]).reshape(heads, -1).sum(1)
    dvec = sum(v[4] for v in grads)
    pieces = (dcb, dvec[0, :heads], dvec[1, :heads], dskip, dgg[0])
    flat = jnp.concatenate([v.reshape(groups, -1) for v in pieces]
                           + [dcw.reshape(taps, groups, -1).transpose(1, 0, 2).reshape(groups, -1)], axis=1)
    flat = exchange(jnp.concatenate([dgain[0].reshape(groups, -1), flat], axis=1))
    own = lax.dynamic_slice_in_dim(flat, shard_index, 1, 0)[0]
    shares, low = [], 0
    for v in small:
        shares.append(own[low : low + v.size].reshape(v.shape))
        low += v.size
    d_gain, d_cb, d_db, d_al, d_sk, d_gg, d_cw = shares
    return (output[None], input_grad[None], d_gain, in_total, d_cw, d_cb, d_db, d_al, d_sk, d_gg, out_total)


def solution(mesh):
    whole = P(("shard", "rep"), None, None)
    row, matrix, cols = P("shard"), P("shard", None), P(None, "shard")
    return jax.shard_map(
        functools.partial(on_device, mesh.shape["shard"], mesh.shape["rep"]),
        mesh=mesh,
        in_specs=(whole, row, matrix, cols, row, row, row, row, row, matrix, whole),
        out_specs=(whole, whole, row, matrix, cols, row, row, row, row, row, matrix),
        check_vma=False,
    )
```

```python
import functools

import jax
import jax.numpy as jnp
from jax import lax
from jax.experimental import pallas as pl
from jax.experimental.pallas import tpu as pltpu
from jax.sharding import PartitionSpec as P

Q = 128
LANES = 128
HEAD = 64
EPS = 1e-05
F32 = jnp.float32
BF16 = jnp.bfloat16
HI = lax.Precision.HIGHEST
NEG = -1e30


def mm(a, b):
    return jnp.dot(a, b, preferred_element_type=F32)


def mm_t(a, b):
    return lax.dot_general(a, b, (((1,), (1,)), ((), ())), preferred_element_type=F32)


def softplus(v):
    return jnp.maximum(v, 0.0) + jnp.log1p(jnp.exp(-jnp.abs(v)))


def sigmoid(v):
    return 1.0 / (1.0 + jnp.exp(-v))


def tri_lower():
    rows = lax.broadcasted_iota(jnp.int32, (Q, Q), 0)
    cols = lax.broadcasted_iota(jnp.int32, (Q, Q), 1)
    return rows >= cols


def spread(table, lane):
    return jnp.broadcast_to(table[:, lane : lane + 1], (Q, LANES))


def fill_tables(dt, logs, dt_tab, log_tab, log_rows, low, groups, per):
    log_rows[...] = jnp.transpose(logs)
    for g in range(groups):
        shift = (LANES - (low + g) * per) % LANES
        dt_tab[g] = pltpu.roll(dt, shift, 1) if shift else dt
        log_tab[g] = pltpu.roll(logs, shift, 1) if shift else logs


def scan_forward(proj_ref, cw_ref, cb_ref, vec_ref, skip_ref, out_ref, sum_ref, start_ref,
                 shifted, act, state, dt_tab, log_tab, log_rows, *, inner, nstate, groups, per):
    first = pl.program_id(0) == 0
    conv = inner + 2 * nstate

    @pl.when(first)
    def _():
        shifted[0:8, :] = jnp.zeros((8, conv), F32)
        state[...] = jnp.zeros_like(state)

    shifted[8 : 8 + Q, :] = proj_ref[:, 0:conv]
    wide = 256
    for low in range(0, conv, wide):
        part = pl.ds(low, wide)
        total = cb_ref[0:1, part] + cw_ref[0:1, part] * shifted[5 : 5 + Q, part]
        for k in range(1, 4):
            total = total + cw_ref[k : k + 1, part] * shifted[5 + k : 5 + k + Q, part]
        sum_ref[:, part] = total
        act[:, part] = total * sigmoid(total)
    shifted[0:8, :] = shifted[Q : Q + 8, :]

    dt = softplus(proj_ref[:, conv : conv + LANES] + vec_ref[0:1, :])
    causal = tri_lower()
    logs = jnp.dot(causal.astype(F32), dt * vec_ref[1:2, :], precision=HI, preferred_element_type=F32)
    fill_tables(dt, logs, dt_tab, log_tab, log_rows, 0, groups, per)
    keys_b = act[:, inner : inner + nstate]
    keys_c = act[:, inner + nstate : conv].astype(BF16)
    b_cols = jnp.transpose(keys_b).astype(BF16)
    cross = mm(keys_c, b_cols)
    start_ref[...] = state[...].astype(BF16)
    span = per * HEAD
    low_half = lax.broadcasted_iota(jnp.int32, (Q, LANES), 1) < HEAD

    def group(g, carry):
        base = pl.multiple_of(g * span, span)
        dts, lgs = dt_tab[g], log_tab[g]
        carried = mm(keys_c, start_ref[:, pl.ds(base, span)])
        tails_all = []
        lasts = []
        for j in range(per // 2):
            cols = pl.ds(pl.multiple_of(base + j * LANES, LANES), LANES)
            h = g * per + 2 * j
            col0, col1 = spread(lgs, 2 * j), spread(lgs, 2 * j + 1)
            row0, row1 = log_rows[pl.ds(h, 1), :], log_rows[pl.ds(h + 1, 1), :]
            values = act[:, cols]
            stepped = (values * jnp.where(low_half, spread(dts, 2 * j), spread(dts, 2 * j + 1)))
            stepped_b = stepped.astype(BF16)
            mix0 = (jnp.exp(jnp.where(causal, col0 - row0, NEG)) * cross).astype(BF16)
            mix1 = (jnp.exp(jnp.where(causal, col1 - row1, NEG)) * cross).astype(BF16)
            zero = jnp.zeros_like(stepped_b)
            pairs = jnp.concatenate(
                [jnp.where(low_half, stepped_b, zero), jnp.where(low_half, zero, stepped_b)], axis=0)
            local = mm(jnp.concatenate([mix0, mix1], axis=1), pairs)
            both = jnp.where(low_half, col0, col1)
            last = both[Q - 1 : Q, :]
            out = local + carried[:, j * LANES : (j + 1) * LANES] * jnp.exp(both)
            out_ref[:, cols] = out + skip_ref[0:1, cols] * values
            tails_all.append((stepped * jnp.exp(last - both)).astype(BF16))
            lasts.append(jnp.exp(last))
        fresh = mm(b_cols, jnp.concatenate(tails_all, axis=1))
        cols = pl.ds(base, span)
        state[:, cols] = state[:, cols] * jnp.concatenate(lasts, axis=1) + fresh
        return carry

    lax.fori_loop(0, groups, group, 0)


def run_scan_forward(proj, cw, cb, vec, skip_cols, inner, nstate, groups, per):
    length = proj.shape[0]
    blocks = length // Q
    conv = inner + 2 * nstate
    whole = lambda shape: pl.BlockSpec(shape, lambda i: (0, 0))
    rows = lambda width: pl.BlockSpec((Q, width), lambda i: (i, 0))
    return pl.pallas_call(
        functools.partial(scan_forward, inner=inner, nstate=nstate, groups=groups, per=per),
        grid=(blocks,),
        in_specs=[rows(proj.shape[1]), whole(cw.shape), whole(cb.shape), whole(vec.shape), whole(skip_cols.shape)],
        out_specs=[rows(inner), rows(conv), pl.BlockSpec((nstate, inner), lambda i: (i, 0))],
        out_shape=[
            jax.ShapeDtypeStruct((length, inner), F32),
            jax.ShapeDtypeStruct((length, conv), F32),
            jax.ShapeDtypeStruct((blocks * nstate, inner), BF16),
        ],
        scratch_shapes=[
            pltpu.VMEM((Q + 8, conv), F32),
            pltpu.VMEM((Q, conv), F32),
            pltpu.VMEM((nstate, inner), F32),
            pltpu.VMEM((groups, Q, LANES), F32),
            pltpu.VMEM((groups, Q, LANES), F32),
            pltpu.VMEM((LANES, Q), F32),
        ],
        compiler_params=pltpu.CompilerParams(vmem_limit_bytes=60 << 20),
        cost_estimate=pl.CostEstimate(flops=12_000_000_000, bytes_accessed=60_000_000, transcendentals=20_000_000),
        name="scan_forward",
    )(proj, cw, cb, vec, skip_cols)


def piece_copies(place_ref, pieces, refs, target, sems):
    copies = []
    for index, (start, half, size, lane) in enumerate(pieces):
        rows, cols = refs[index].shape
        if half is not None:
            start = pl.multiple_of(start + jnp.bitwise_xor(place_ref[1], half) * size, 16)
        window = target.at[pl.ds(start, rows), pl.ds(lane, cols)]
        copies.append(pltpu.make_async_copy(refs[index], window, sems.at[index]))
    return copies


def load_pieces(*args):
    for copy in piece_copies(*args):
        copy.start()


def wait_pieces(*args):
    for copy in piece_copies(*args):
        copy.wait()


def columns_of(place_ref, position, order, width):
    return pl.ds(pl.multiple_of(jnp.bitwise_xor(place_ref[0], order[position]) * width, LANES), width)


def project_in(place_ref, tok_ref, gain_ref, *rest, pieces, order):
    refs, (normed_ref, proj_ref, weight, sems) = rest[: len(pieces)], rest[len(pieces) :]
    first = pl.program_id(0) == 0

    @pl.when(first)
    def _():
        load_pieces(place_ref, pieces, refs, weight, sems)

    width = tok_ref.shape[1] // len(order)
    tok = tok_ref[...].astype(F32)
    scale = lax.rsqrt(jnp.mean(tok * tok, axis=1, keepdims=True) + EPS)
    for position in range(len(order)):
        cols = columns_of(place_ref, position, order, width)
        value = tok_ref[:, cols].astype(F32) * scale * gain_ref[0:1, cols]
        normed_ref[:, position * width : (position + 1) * width] = value.astype(BF16)

    @pl.when(first)
    def _():
        wait_pieces(place_ref, pieces, refs, weight, sems)

    total = proj_ref.shape[1]
    step = 384
    for low in range(0, total, step):
        proj_ref[:, low : low + step] = mm_t(normed_ref[...], weight[low : low + step, :])


def grid_of(grid, in_specs, out_specs, scratch):
    return pltpu.PrefetchScalarGridSpec(
        num_scalar_prefetch=1, grid=grid, in_specs=in_specs, out_specs=out_specs, scratch_shapes=scratch)


def anywhere(count):
    return [pl.BlockSpec(memory_space=pl.ANY)] * count


def row_block(block, width):
    return pl.BlockSpec((block, width), lambda i, s: (i, 0))


def fixed(shape):
    return pl.BlockSpec(shape, lambda i, s: (0,) * len(shape))


def run_project_in(place, tok, gain, weight, total, order, block=256):
    pieces, arrays = weight
    length, width = tok.shape
    return pl.pallas_call(
        functools.partial(project_in, pieces=pieces, order=order),
        grid_spec=grid_of(
            (length // block,),
            [row_block(block, width), fixed(gain.shape)] + anywhere(len(pieces)),
            [row_block(block, width), row_block(block, total)],
            [pltpu.VMEM((total, width), BF16), pltpu.SemaphoreType.DMA((len(pieces),))],
        ),
        out_shape=[jax.ShapeDtypeStruct((length, width), BF16), jax.ShapeDtypeStruct((length, total), F32)],
        compiler_params=pltpu.CompilerParams(vmem_limit_bytes=50 << 20),
        cost_estimate=pl.CostEstimate(flops=20_000_000_000, bytes_accessed=30_000_000, transcendentals=1000),
        name="project_in",
    )(place, tok, gain, *arrays)


def gating(place_ref, normed_ref, cot_ref, scan_ref, gain_ref, *rest, wg_pieces, ow_pieces, order):
    n_g, n_o = len(wg_pieces), len(ow_pieces)
    wg_refs, ow_refs = rest[:n_g], rest[n_g : n_g + n_o]
    (mixed_ref, dscan_ref, dgate_ref, dgain_ref, wg, ow, gate_s, gated_s, scaled_s,
     g_sems, o_sems) = rest[n_g + n_o :]
    inner = wg.shape[0]
    parts = len(order)
    width = inner // parts
    first = pl.program_id(0) == 0

    @pl.when(first)
    def _():
        load_pieces(place_ref, wg_pieces, wg_refs, wg, g_sems)
        load_pieces(place_ref, ow_pieces, ow_refs, ow, o_sems)
        dgain_ref[...] = jnp.zeros_like(dgain_ref)
        wait_pieces(place_ref, wg_pieces, wg_refs, wg, g_sems)

    def fold(v):
        total = v[:, 0:LANES]
        for low in range(LANES, v.shape[1], LANES):
            total = total + v[:, low : low + LANES]
        return total

    power = None
    for p in range(parts):
        cols = slice(p * width, (p + 1) * width)
        gate = mm_t(normed_ref[...], wg[cols, :])
        gated = scan_ref[:, cols] * (gate * sigmoid(gate))
        gate_s[:, cols] = gate
        gated_s[:, cols] = gated
        term = fold(gated * gated)
        power = term if power is None else power + term
    scale = lax.rsqrt(jnp.sum(power, axis=1, keepdims=True) / inner + EPS)

    @pl.when(first)
    def _():
        wait_pieces(place_ref, ow_pieces, ow_refs, ow, o_sems)

    match = None
    for p in range(parts):
        true = columns_of(place_ref, p, order, width)
        rows = slice(p * width, (p + 1) * width)
        grad = mm_t(cot_ref[...], ow[rows, :])
        gated = gated_s[:, true]
        gain = gain_ref[0:1, true]
        unit = gated * scale
        mixed_ref[:, rows] = (unit * gain).astype(BF16)
        dgain_ref[0:1, true] += jnp.sum(grad * unit, axis=0, keepdims=True)
        scaled = grad * gain
        scaled_s[:, true] = scaled
        term = fold(scaled * gated)
        match = term if match is None else match + term
    pull = jnp.sum(match, axis=1, keepdims=True) * (scale * scale) / inner
    for p in range(parts):
        cols = slice(p * width, (p + 1) * width)
        gate = gate_s[:, cols]
        sig = sigmoid(gate)
        silu = gate * sig
        dgated = scale * (scaled_s[:, cols] - gated_s[:, cols] * pull)
        dscan_ref[:, cols] = dgated * silu
        dgate_ref[:, cols] = (dgated * scan_ref[:, cols] * (sig + silu * (1.0 - sig))).astype(BF16)


def run_gating(place, normed, gate_weight, out_weight, cot, scan_out, gain, order, block=256):
    wg_pieces, wg_arrays = gate_weight
    ow_pieces, ow_arrays = out_weight
    length, width = normed.shape
    inner = scan_out.shape[1]
    return pl.pallas_call(
        functools.partial(gating, wg_pieces=wg_pieces, ow_pieces=ow_pieces, order=order),
        grid_spec=grid_of(
            (length // block,),
            [row_block(block, width), row_block(block, width), row_block(block, inner), fixed((1, inner))]
            + anywhere(len(wg_pieces) + len(ow_pieces)),
            [row_block(block, inner), row_block(block, inner), row_block(block, inner), fixed((1, inner))],
            [pltpu.VMEM((inner, width), BF16), pltpu.VMEM((inner, width), BF16)]
            + [pltpu.VMEM((block, inner), F32)] * 3
            + [pltpu.SemaphoreType.DMA((len(wg_pieces),)), pltpu.SemaphoreType.DMA((len(ow_pieces),))],
        ),
        out_shape=[
            jax.ShapeDtypeStruct((length, inner), BF16),
            jax.ShapeDtypeStruct((length, inner), F32),
            jax.ShapeDtypeStruct((length, inner), BF16),
            jax.ShapeDtypeStruct((1, inner), F32),
        ],
        compiler_params=pltpu.CompilerParams(vmem_limit_bytes=62 << 20),
        cost_estimate=pl.CostEstimate(flops=40_000_000_000, bytes_accessed=70_000_000, transcendentals=10_000_000),
        name="gating",
    )(place, normed, cot, scan_out, gain, *wg_arrays, *ow_arrays)


def gate_back(place_ref, dgate_ref, *rest, pieces):
    refs, (grad_ref, weight, sems) = rest[: len(pieces)], rest[len(pieces) :]

    @pl.when(pl.program_id(0) == 0)
    def _():
        load_pieces(place_ref, pieces, refs, weight, sems)
        wait_pieces(place_ref, pieces, refs, weight, sems)

    step = 384
    for low in range(0, grad_ref.shape[1], step):
        grad_ref[:, low : low + step] = mm(dgate_ref[...], weight[:, low : low + step])


def run_gate_back(place, dgate, model, weight, block=256):
    pieces, arrays = weight
    length, inner = dgate.shape
    return pl.pallas_call(
        functools.partial(gate_back, pieces=pieces),
        grid_spec=grid_of(
            (length // block,),
            [row_block(block, inner)] + anywhere(len(pieces)),
            row_block(block, model),
            [pltpu.VMEM((inner, model), BF16), pltpu.SemaphoreType.DMA((len(pieces),))],
        ),
        out_shape=jax.ShapeDtypeStruct((length, model), F32),
        compiler_params=pltpu.CompilerParams(vmem_limit_bytes=40 << 20),
        cost_estimate=pl.CostEstimate(flops=16_000_000_000, bytes_accessed=22_000_000, transcendentals=0),
        name="gate_back",
    )(place, dgate, *arrays)


def input_back(place_ref, part_ref, tok_ref, cot_ref, gain_ref, *rest, count, pieces, order):
    dproj_refs, rest = rest[:count], rest[count:]
    refs, (grad_ref, dgain_ref, weight, dn, sems) = rest[: len(pieces)], rest[len(pieces) :]
    first = pl.program_id(0) == 0

    @pl.when(first)
    def _():
        load_pieces(place_ref, pieces, refs, weight, sems)
        dgain_ref[...] = jnp.zeros_like(dgain_ref)
        wait_pieces(place_ref, pieces, refs, weight, sems)

    model = tok_ref.shape[1]
    width = model // len(order)
    tok = tok_ref[...].astype(F32)
    scale = lax.rsqrt(jnp.mean(tok * tok, axis=1, keepdims=True) + EPS)
    match = None
    for position in range(len(order)):
        spot = slice(position * width, (position + 1) * width)
        true = columns_of(place_ref, position, order, width)
        grad, low = part_ref[:, spot], 0
        for ref in dproj_refs:
            grad = grad + mm(ref[...], weight[low : low + ref.shape[1], spot])
            low += ref.shape[1]
        value = tok_ref[:, true].astype(F32)
        dgain_ref[0:1, true] += jnp.sum(grad * (value * scale), axis=0, keepdims=True)
        grad = grad * gain_ref[0:1, true]
        dn[:, spot] = grad
        term = jnp.sum(grad * value, axis=1, keepdims=True)
        match = term if match is None else match + term
    pull = match * (scale * scale * scale) / model
    for position in range(len(order)):
        spot = slice(position * width, (position + 1) * width)
        true = columns_of(place_ref, position, order, width)
        value = tok_ref[:, true].astype(F32)
        grad_ref[:, true] = cot_ref[:, true].astype(F32) + (scale * dn[:, spot] - value * pull)


def run_input_back(place, part, dprojs, tok, cot, gain, weight, order, block=256):
    pieces, arrays = weight
    length, model = tok.shape
    widths = [d.shape[1] for d in dprojs]
    return pl.pallas_call(
        functools.partial(input_back, count=len(dprojs), pieces=pieces, order=order),
        grid_spec=grid_of(
            (length // block,),
            [row_block(block, model), row_block(block, model), row_block(block, model), fixed((1, model))]
            + [row_block(block, w) for w in widths] + anywhere(len(pieces)),
            [row_block(block, model), fixed((1, model))],
            [pltpu.VMEM((sum(widths), model), BF16), pltpu.VMEM((block, model), F32),
             pltpu.SemaphoreType.DMA((len(pieces),))],
        ),
        out_shape=[jax.ShapeDtypeStruct((length, model), F32), jax.ShapeDtypeStruct((1, model), F32)],
        compiler_params=pltpu.CompilerParams(vmem_limit_bytes=50 << 20),
        cost_estimate=pl.CostEstimate(flops=22_000_000_000, bytes_accessed=46_000_000, transcendentals=1000),
        name="input_back",
    )(place, part, tok, cot, gain, *dprojs, *arrays)


def project_out(place_ref, mixed_ref, tok_ref, *rest, pieces):
    refs, (out_ref, weight, sems) = rest[: len(pieces)], rest[len(pieces) :]

    @pl.when(pl.program_id(0) == 0)
    def _():
        load_pieces(place_ref, pieces, refs, weight, sems)
        wait_pieces(place_ref, pieces, refs, weight, sems)

    step = 384
    for low in range(0, out_ref.shape[1], step):
        cols = slice(low, low + step)
        out_ref[:, cols] = (tok_ref[:, cols].astype(F32) + mm(mixed_ref[...], weight[:, cols])).astype(BF16)


def run_project_out(place, mixed, tok, weight, block=256):
    pieces, arrays = weight
    length, model = tok.shape
    inner = mixed.shape[1]
    return pl.pallas_call(
        functools.partial(project_out, pieces=pieces),
        grid_spec=grid_of(
            (length // block,),
            [row_block(block, inner), row_block(block, model)] + anywhere(len(pieces)),
            row_block(block, model),
            [pltpu.VMEM((inner, model), BF16), pltpu.SemaphoreType.DMA((len(pieces),))],
        ),
        out_shape=jax.ShapeDtypeStruct((length, model), BF16),
        compiler_params=pltpu.CompilerParams(vmem_limit_bytes=40 << 20),
        cost_estimate=pl.CostEstimate(flops=14_000_000_000, bytes_accessed=20_000_000, transcendentals=0),
        name="project_out",
    )(place, mixed, tok, *arrays)


def scan_backward(proj_ref, tail_ref, sum_ref, keys_ref, out_ref, dout_ref, start_ref, cw_ref, cwk_ref, vec_ref,
                  skip_ref, pick_ref, *rest, nstate, low, groups, per, begin, last):
    if not begin:
        old_cross_ref, old_keys_ref, old_raw_ref = rest[:3]
        rest = rest[3:]
    dproj_ref, dcw_ref, dcb_ref, dskip_ref, dvec_ref = rest[:5]
    rest = rest[5:]
    if not last:
        cross_ref, keys_ref_out, raw_ref = rest[:3]
        rest = rest[3:]
    dsum, dstate, edge, logs_v, tails_v, steps_v, dt_tab, log_tab, log_rows, dcross, dkeys = rest
    first = pl.program_id(0) == 0
    span_all = groups * per * HEAD
    conv = dsum.shape[1]

    @pl.when(first)
    def _():
        dsum[Q : Q + 8, :] = jnp.zeros((8, conv), F32)
        dstate[...] = jnp.zeros_like(dstate)
        edge[...] = jnp.zeros_like(edge)
        dcw_ref[...] = jnp.zeros_like(dcw_ref)
        dcb_ref[...] = jnp.zeros_like(dcb_ref)
        dskip_ref[...] = jnp.zeros_like(dskip_ref)
        dvec_ref[...] = jnp.zeros_like(dvec_ref)

    raw = tail_ref[:, 2 * nstate : 2 * nstate + LANES] + vec_ref[0:1, :]
    dt = softplus(raw)
    lower = tri_lower()
    rate = vec_ref[1:2, :]
    logs = jnp.dot(lower.astype(F32), dt * rate, precision=HI, preferred_element_type=F32)
    fill_tables(dt, logs, dt_tab, log_tab, log_rows, low, groups, per)
    sum_b = keys_ref[:, 0:nstate]
    sum_c = keys_ref[:, nstate : 2 * nstate]
    sig_b, sig_c = sigmoid(sum_b), sigmoid(sum_c)
    keys_b32, keys_c32 = sum_b * sig_b, sum_c * sig_c
    keys_b, keys_c = keys_b32.astype(BF16), keys_c32.astype(BF16)
    c_cols = jnp.transpose(keys_c32).astype(BF16)
    cross = mm(keys_b, c_cols)
    span = per * HEAD
    low_half = lax.broadcasted_iota(jnp.int32, (Q, LANES), 1) < HEAD
    upper = lax.broadcasted_iota(jnp.int32, (Q, Q), 0) <= lax.broadcasted_iota(jnp.int32, (Q, Q), 1)
    if not begin:
        dcross[...] = old_cross_ref[...]
        dkeys[...] = old_keys_ref[...]
    else:
        dcross[...] = jnp.zeros_like(dcross)
        dkeys[...] = jnp.zeros_like(dkeys)

    def group(g, carry):
        base = pl.multiple_of(g * span, span)
        whole = pl.ds(base, span)
        dts, lgs = dt_tab[g], log_tab[g]
        dstate_b = dstate[:, whole].astype(BF16)
        from_state = mm(keys_b, dstate_b)
        tails_all, outs_all, lasts = [], [], []
        dcr = None
        for j in range(per // 2):
            cols = pl.ds(pl.multiple_of(base + j * LANES, LANES), LANES)
            h = (low + g) * per + 2 * j
            col0, col1 = spread(lgs, 2 * j), spread(lgs, 2 * j + 1)
            row0, row1 = log_rows[pl.ds(h, 1), :], log_rows[pl.ds(h + 1, 1), :]
            total = sum_ref[:, cols]
            sig = sigmoid(total)
            values = total * sig
            step = jnp.where(low_half, spread(dts, 2 * j), spread(dts, 2 * j + 1))
            stepped = values * step
            stepped_b = stepped.astype(BF16)
            dout = dout_ref[:, cols]
            dout_b = dout.astype(BF16)
            decay0 = jnp.exp(jnp.where(upper, row0 - col0, NEG))
            decay1 = jnp.exp(jnp.where(upper, row1 - col1, NEG))
            mix = jnp.concatenate([(decay0 * cross).astype(BF16), (decay1 * cross).astype(BF16)], axis=1)
            zero = jnp.zeros_like(dout_b)
            douts = jnp.concatenate(
                [jnp.where(low_half, dout_b, zero), jnp.where(low_half, zero, dout_b)], axis=0)
            local = mm(mix, douts)
            dmix = mm_t(stepped_b, douts)
            term = dmix[:, 0:Q] * decay0 + dmix[:, Q : 2 * Q] * decay1
            dcr = term if dcr is None else dcr + term
            both = jnp.where(low_half, col0, col1)
            last = both[Q - 1 : Q, :]
            tail = jnp.exp(last - both)
            passed = from_state[:, j * LANES : (j + 1) * LANES] * tail
            dstepped = local + passed
            skip = skip_ref[0:1, cols]
            scan = out_ref[:, cols] - skip * values
            logs_v[:, cols] = dout_b.astype(F32) * scan - stepped_b.astype(F32) * local
            tails_v[:, cols] = stepped * passed
            steps_v[:, cols] = dstepped * values
            dvalues = dstepped * step + dout * skip
            dskip_ref[0:1, cols] += jnp.sum(dout * values, axis=0, keepdims=True)
            dsum[0:Q, cols] = dvalues * (sig + values * (1.0 - sig))
            tails_all.append((stepped * tail).astype(BF16))
            outs_all.append((dout * jnp.exp(both)).astype(BF16))
            lasts.append(jnp.exp(last))
        dcross[...] += dcr
        outs = jnp.concatenate(outs_all, axis=1)
        starts = start_ref[:, whole]
        dkeys[:, nstate : 2 * nstate] += mm_t(outs, starts)
        dkeys[:, 0:nstate] += mm_t(jnp.concatenate(tails_all, axis=1), dstate_b)
        kept = dstate[:, whole] * jnp.concatenate(lasts, axis=1)
        edge[0:1, whole] = jnp.sum(kept * starts.astype(F32), axis=0, keepdims=True)
        dstate[:, whole] = kept + mm(c_cols, outs)
        return carry

    lax.fori_loop(0, groups, group, 0)

    if last:
        dcr = dcross[...]
        exact = lambda u, v: jnp.dot(u, v, precision=HI, preferred_element_type=F32)
        d_b = dkeys[:, 0:nstate] + exact(dcr, keys_c32)
        d_c = dkeys[:, nstate : 2 * nstate] + exact(jnp.transpose(dcr), keys_b32)
        dsum[0:Q, span_all : span_all + nstate] = d_b * (sig_b + keys_b32 * (1.0 - sig_b))
        dsum[0:Q, span_all + nstate : conv] = d_c * (sig_c + keys_c32 * (1.0 - sig_c))
    else:
        cross_ref[...] = dcross[...]
        keys_ref_out[...] = dkeys[...]

    def reduce_heads(v):
        high = v.astype(BF16)
        low = (v - high.astype(F32)).astype(BF16)
        return mm(high, pick_ref[...]) + mm(low, pick_ref[...])

    dlogs = reduce_heads(logs_v[...])
    dtails = reduce_heads(tails_v[...])
    dlogit = (
        jnp.dot(upper.astype(F32), dlogs, precision=HI, preferred_element_type=F32)
        + jnp.dot(1.0 - upper.astype(F32), dtails, precision=HI, preferred_element_type=F32)
        + reduce_heads(edge[...])[0:1, :]
    )
    dstep = reduce_heads(steps_v[...]) + dlogit * rate
    draw = dstep * sigmoid(raw)
    dvec_ref[0:1, :] += jnp.sum(draw, axis=0, keepdims=True)
    dvec_ref[1:2, :] += jnp.sum(dlogit * dt * rate, axis=0, keepdims=True)
    if last:
        dproj_ref[:, conv : conv + LANES] = (draw + old_raw_ref[...]).astype(BF16)
    elif begin:
        raw_ref[...] = draw
    else:
        raw_ref[...] = draw + old_raw_ref[...]

    wide = 256
    for start in range(0, conv, wide):
        part = pl.ds(start, wide)
        if start < span_all:
            source, taps_ref, local = proj_ref, cw_ref, part
        else:
            source, taps_ref, local = tail_ref, cwk_ref, pl.ds(start - span_all, wide)
        taken = source[:, local]
        total = None
        for k in range(4):
            moved = dsum[3 - k : 3 - k + Q, part]
            dcw_ref[k : k + 1, part] += jnp.sum(taken * moved, axis=0, keepdims=True)
            term = taps_ref[k : k + 1, local] * moved
            total = term if total is None else total + term
            if k == 3:
                dcb_ref[0:1, part] += jnp.sum(moved, axis=0, keepdims=True)
        dproj_ref[:, part] = total.astype(BF16)
    dsum[Q : Q + 8, :] = dsum[0:8, :]


def run_scan_backward(proj, sums, scan_out, dscan, starts, cw, vec, skip_cols, pick, inner, nstate, low, groups, per,
                      previous, last):
    length = proj.shape[0]
    blocks = length // Q
    span = groups * per * HEAD
    begin = previous is None
    conv = span + (2 * nstate if last else 0)
    where = low * per * HEAD // span
    whole = lambda shape: pl.BlockSpec(shape, lambda i: (0, 0))
    rows = lambda width, col=0: pl.BlockSpec((Q, width), lambda i: (blocks - 1 - i, col))
    part = lambda height: pl.BlockSpec((height, span), lambda i: (0, where))
    tail = 2 * nstate + LANES
    out_specs = [rows(conv + (LANES if last else 0)), whole((4, conv)), whole((1, conv)), whole((1, span)),
                 whole((8, LANES))]
    out_shape = [
        jax.ShapeDtypeStruct((length, conv + (LANES if last else 0)), BF16),
        jax.ShapeDtypeStruct((4, conv), F32),
        jax.ShapeDtypeStruct((1, conv), F32),
        jax.ShapeDtypeStruct((1, span), F32),
        jax.ShapeDtypeStruct((8, LANES), F32),
    ]
    carried = [rows(Q), rows(2 * nstate), rows(LANES)]
    if not last:
        out_specs += carried
        out_shape += [jax.ShapeDtypeStruct((length, w), F32) for w in (Q, 2 * nstate, LANES)]
    return pl.pallas_call(
        functools.partial(scan_backward, nstate=nstate, low=low, groups=groups, per=per, begin=begin, last=last),
        grid=(blocks,),
        in_specs=[
            rows(span, where), rows(tail, inner // tail), rows(span, where), rows(2 * nstate, inner // (2 * nstate)),
            rows(span, where), rows(span, where),
            pl.BlockSpec((nstate, span), lambda i: (blocks - 1 - i, where)),
            part(4), pl.BlockSpec((4, 2 * nstate), lambda i: (0, inner // (2 * nstate))),
            whole(vec.shape), part(1), pl.BlockSpec((span, LANES), lambda i: (where, 0)),
        ] + ([] if begin else carried),
        out_specs=out_specs,
        out_shape=out_shape,
        scratch_shapes=[
            pltpu.VMEM((Q + 8, conv), F32),
            pltpu.VMEM((nstate, span), F32),
            pltpu.VMEM((8, span), F32),
            pltpu.VMEM((Q, span), F32),
            pltpu.VMEM((Q, span), F32),
            pltpu.VMEM((Q, span), F32),
            pltpu.VMEM((groups, Q, LANES), F32),
            pltpu.VMEM((groups, Q, LANES), F32),
            pltpu.VMEM((LANES, Q), F32),
            pltpu.VMEM((Q, Q), F32),
            pltpu.VMEM((Q, 2 * nstate), F32),
        ],
        compiler_params=pltpu.CompilerParams(vmem_limit_bytes=50 << 20),
        cost_estimate=pl.CostEstimate(flops=40_000_000_000, bytes_accessed=40_000_000, transcendentals=15_000_000),
        name="scan_backward",
    )(proj, proj, sums, sums, scan_out, dscan, starts, cw, cw, vec, skip_cols, pick, *(previous or ()))


def bits_of(size):
    return [1 << b for b in range(size.bit_length() - 1)]


def swap(value, axis, bit, size):
    return lax.ppermute(value, axis, [(i, i ^ bit) for i in range(size)])


def after(value, *deps):
    return lax.optimization_barrier((value,) + deps)[0] if deps else value


def order_of(size):
    flipped = []
    for index in range(size):
        value = 0
        for low, high in zip(bits_of(size), reversed(bits_of(size))):
            value |= high if index & low else 0
        flipped.append(value)
    return flipped


class Gather:
    def __init__(self, shard, order, rep_index, groups, copies, lanes, chunks):
        self.order, self.groups, self.copies = order, groups, copies
        self.size = shard.shape
        self.lanes = lanes
        self.half = shard.shape[0] // 2
        self.rows = self.half // chunks
        self.shard = shard
        parity = rep_index & 1
        self.mine = [lax.dynamic_slice_in_dim(shard, parity * self.half + c * self.rows, self.rows, 0)
                     for c in range(chunks)]
        self.there, self.across = [None] * chunks, [None] * chunks

    def far(self, chunk, *deps):
        value = after(self.mine[chunk], *deps)
        self.there[chunk] = swap(value, "shard", 2, self.groups)

    def side(self, chunk):
        self.across[chunk] = swap(self.there[chunk], "rep", 1, self.copies)

    def finish(self, *deps):
        have = {0: [(0, None, 0, self.shard)]}
        have[2] = [(c * self.rows, h, self.half, v) for h, vs in ((0, self.there), (1, self.across))
                   for c, v in enumerate(vs)]
        for source in (0, 2):
            have[source ^ 1] = [(r, h, s, swap(after(v, *deps) if v is self.across[-1] else v, "shard", 1, self.groups))
                                for r, h, s, v in have[source]]
        pieces, arrays = [], []
        for position, source in enumerate(self.order):
            for row, half, size, value in have[source]:
                if self.lanes:
                    pieces.append((row, half, size, position * self.size[1]))
                else:
                    pieces.append((row + position * self.size[0], half, size, 0))
                arrays.append(value)
        return tuple(pieces), tuple(arrays)


class Total:
    def __init__(self, kept, sent, axis, rep_index, groups, copies, narrow=False):
        self.axis, self.rep_index = axis, rep_index
        self.sizes = {"shard": groups, "rep": copies}
        self.stages = [("shard", index, 1) for index in range(len(bits_of(groups)))]
        count = len(bits_of(copies))
        over = [("rep", 0, 1)] + [("rep", index, min(2, count - index)) for index in range(1, count, 2)]
        self.stages += over
        self.back = list(reversed(over))
        if narrow:
            self.back = [(name, shift + bit, 1) for name, shift, width in self.back for bit in range(width)]
        self.value, self.out = kept, [sent]
        self.fly()

    @classmethod
    def join(cls, chains):
        first = chains[0]
        new = object.__new__(cls)
        new.axis, new.rep_index, new.sizes = first.axis, first.rep_index, first.sizes
        new.stages, new.back = first.stages, first.back
        new.value = jnp.concatenate([v.value for v in chains])
        new.coming = [jnp.concatenate(v) for v in zip(*(c.coming for c in chains))]
        return new

    def fly(self):
        name, shift, _ = self.stages[0]
        self.coming = [swap(v, name, (k + 1) << shift, self.sizes[name]) for k, v in enumerate(self.out)]

    def done(self):
        return not self.stages and not self.back

    def step(self, *deps):
        coming = [after(v, *deps) for v in self.coming]
        if not self.stages:
            return self.widen(coming)
        self.stages.pop(0)
        terms = [self.value] + coming
        if not self.stages:
            self.value = sum(v.astype(F32) for v in terms).astype(BF16)
            self.fly_back()
            return [self.value]
        name, shift, width = self.stages[0]
        parts = 1 << width
        axis = self.axis if name == "shard" else 0
        size = self.value.shape[axis] // parts
        mine = 0 if name == "shard" else (self.rep_index >> shift) & (parts - 1)
        cut = lambda start: sum(lax.dynamic_slice_in_dim(v, start, size, axis).astype(F32) for v in terms)
        self.out = [cut((mine ^ k) * size).astype(BF16) for k in range(1, parts)]
        self.value = cut(mine * size)
        self.fly()
        return self.out

    def fly_back(self):
        name, shift, width = self.back[0]
        self.coming = [swap(self.value, name, k << shift, self.sizes[name]) for k in range(1, 1 << width)]

    def widen(self, coming):
        name, shift, width = self.back.pop(0)
        parts = [self.value] + coming
        for bit in range(width):
            turn = ((self.rep_index >> (shift + bit)) & 1) != 0
            parts = [jnp.where(turn, parts[k ^ (1 << bit)], parts[k]) for k in range(len(parts))]
        if not self.back:
            self.value = [v.astype(F32) for v in parts]
            return self.value
        self.value = jnp.concatenate(parts)
        self.fly_back()
        return [self.value]


def outer(left, right):
    return lax.dot_general(left, right, (((0,), (0,)), ((), ())), preferred_element_type=F32).astype(BF16)


def on_device(groups, copies, tokens, norm_gain, in_weight, conv_weight, conv_bias, dt_bias, a_log, skip, gate_gain,
              out_weight, cotangent):
    if tokens.shape[0] != 1 or groups != 4:
        raise ValueError("unexpected sizes")
    order = order_of(groups)
    shard_index = lax.axis_index("shard")
    rep_index = lax.axis_index("rep")
    tok, cot = tokens[0], cotangent[0]
    inner = gate_gain.shape[0] * groups
    conv = conv_bias.shape[0] * groups
    heads = dt_bias.shape[0] * groups
    nstate = (conv - inner) // 2
    model = tok.shape[1]
    taps = conv_weight.shape[0]
    outputs_all = in_weight.shape[1]
    place = jnp.stack([shard_index, rep_index & 1]).astype(jnp.int32)

    turned = in_weight.T
    total = conv + LANES
    conv_part = jnp.pad(turned[inner:], ((0, total + inner - outputs_all), (0, 0)))
    make = lambda shard, lanes, chunks: Gather(shard, order, rep_index, groups, copies, lanes, chunks)
    wc = make(conv_part, True, 2)
    wg = make(turned[:inner], True, 1)
    ow = make(out_weight, False, 1)

    small = (norm_gain, conv_bias, dt_bias, a_log, skip, gate_gain, conv_weight)
    packed = jnp.concatenate([v.reshape(-1) for v in small])
    wc.far(0)
    wc.far(1)
    wc.side(0)
    wc.side(1)
    wg.far(0, wc.there[1])
    ow.far(0, wc.there[1])
    rows = [packed, swap(packed, "shard", 1, groups)]
    far = swap(packed, "shard", 2, groups)
    rows += [far, swap(far, "shard", 1, groups)]
    for bit in bits_of(groups):
        turn = (shard_index & bit) != 0
        rows = [jnp.where(turn, rows[j ^ bit], rows[j]) for j in range(groups)]
    everyone = jnp.stack(rows).astype(F32)
    parts, low = [], 0
    for v in small:
        parts.append(everyone[:, low : low + v.size])
        low += v.size
    gain, cb, db, al, sk, gg = (v.reshape(-1) for v in parts[:6])
    cw = parts[6].reshape(groups, taps, -1).transpose(1, 0, 2).reshape(taps, conv)
    gain, cb, gg = gain[None], cb[None], gg[None]
    vec = jnp.pad(jnp.stack([db, -jnp.exp(al)]), ((0, 6), (0, LANES - heads)))
    skip_cols = jnp.repeat(sk, inner // heads)[None]
    pick = (jnp.arange(inner)[:, None] // (inner // heads) == jnp.arange(LANES)[None]).astype(BF16)

    wc = wc.finish(gain, cb, gg, cw, vec, skip_cols, pick)
    normed, proj = run_project_in(place, tok, gain, wc, total, order)
    for weight in (wg, ow):
        weight.there[0] = after(weight.there[0], normed)
        weight.side(0)
    proj = after(proj, wg.there[0], ow.there[0])
    per = 8
    scan_out, sums, starts = run_scan_forward(proj, cw, cb, vec, skip_cols, inner, nstate, heads // per, per)
    wg, ow = wg.finish(scan_out), ow.finish(scan_out)
    mixed, dscan, dgate, dgg = run_gating(place, normed, wg, ow, cot, scan_out, gg, order)

    chain = lambda kept, sent, axis, *way: Total(kept, sent, axis, rep_index, groups, copies, *way)
    half = inner // 2
    out_sent = outer(mixed[:, half:], cot)
    o = chain(outer(mixed[:, :half], cot), out_sent, 0)
    half = model // 2
    left, right = normed[:, :half], normed[:, half:]
    gate_sent = outer(dgate, right)
    marks = o.step(gate_sent)
    g = chain(outer(after(dgate, *marks), left), gate_sent, 1, True)
    marks = marks + g.step(g.value)

    blocks = heads // per
    cuts = [blocks * v // 3 for v in range(4)]
    chains, grads, carried = [o, g], [], None
    for index in range(3):
        low, high = cuts[index], cuts[index + 1]
        found = run_scan_backward(
            proj, sums, scan_out, after(dscan, *marks), starts, cw, vec, skip_cols, pick, inner, nstate, low,
            high - low, per, carried, index == 2)
        grads.append(found[:5])
        carried = tuple(found[5:])
        dproj, marks = found[0], []
        if index == 1:
            marks = o.step(dproj)
        if index == 2:
            ab = Total.join(chains[2:])
            marks = o.coming + g.step(dproj, *o.coming)
            marks = marks + ab.step(dproj, *marks)
        dproj = after(dproj, *marks)
        sent = outer(dproj, right)
        kept = outer(dproj, left)
        new = chain(kept, sent, 1)
        marks = marks + new.step(kept)
        if index < 2:
            marks = marks + (o, g)[index].step(kept, *marks)
        chains.append(new)
    c = chains[4]

    part = run_gate_back(place, after(dgate, *marks), model, wg)
    marks = g.coming + ab.coming
    marks = marks + o.step(part, *marks)
    marks = marks + c.step(part, *marks)
    input_grad, dgain = run_input_back(place, after(part, *marks), [v[0] for v in grads], tok, cot, gain, wc, order)

    dcw = jnp.concatenate([v[1] for v in grads], axis=1)
    dcb = jnp.concatenate([v[2][0] for v in grads])
    dskip = jnp.concatenate([v[3][0] for v in grads]).reshape(heads, -1).sum(1)
    dvec = sum(v[4] for v in grads)
    pieces = (dcb, dvec[0, :heads], dvec[1, :heads], dskip, dgg[0])
    flat = jnp.concatenate([v.reshape(groups, -1) for v in pieces]
                           + [dcw.reshape(taps, groups, -1).transpose(1, 0, 2).reshape(groups, -1)], axis=1)
    flat = jnp.concatenate([dgain[0].reshape(groups, -1), flat], axis=1)
    abc = Total.join([ab, c])
    marks = abc.step(dgain, *o.coming)
    marks = marks + g.step(*marks)
    marks = marks + o.step(*marks)
    flat = after(flat, *marks)
    for bit in bits_of(groups):
        flat = flat + swap(flat, "shard", bit, groups)
    output = run_project_out(place, after(mixed, flat, *marks), tok, ow)
    marks = o.coming + abc.coming
    marks = marks + g.step(output, *marks)
    marks = marks + abc.step(output, *marks)
    flat = after(flat, *marks)
    for bit in bits_of(copies):
        flat = flat + swap(flat, "rep", bit, copies)
    chains = [o, g, abc]
    while not all(old.done() for old in chains):
        for old in (g, abc, o):
            if not old.done():
                old.step()

    cut = ab.value.shape[0]
    halves = [v[:cut] for v in abc.value] + [v[cut:] for v in abc.value]
    in_total = jnp.concatenate(g.value + halves)[:outputs_all].T
    out_total = jnp.concatenate(o.value)

    own = lax.dynamic_slice_in_dim(flat, shard_index, 1, 0)[0]
    shares, low = [], 0
    for v in small:
        shares.append(own[low : low + v.size].reshape(v.shape))
        low += v.size
    d_gain, d_cb, d_db, d_al, d_sk, d_gg, d_cw = shares
    return (output[None], input_grad[None], d_gain, in_total, d_cw, d_cb, d_db, d_al, d_sk, d_gg, out_total)


def solution(mesh):
    whole = P(("shard", "rep"), None, None)
    row, matrix, cols = P("shard"), P("shard", None), P(None, "shard")
    return jax.shard_map(
        functools.partial(on_device, mesh.shape["shard"], mesh.shape["rep"]),
        mesh=mesh,
        in_specs=(whole, row, matrix, cols, row, row, row, row, row, matrix, whole),
        out_specs=(whole, whole, row, matrix, cols, row, row, row, row, row, matrix),
        check_vma=False,
    )
```

```python
import functools

import jax
import jax.numpy as jnp
from jax import lax
from jax.experimental import pallas as pl
from jax.experimental.pallas import tpu as pltpu
from jax.sharding import PartitionSpec as P

Q = 128
LANES = 128
HEAD = 64
EPS = 1e-05
F32 = jnp.float32
BF16 = jnp.bfloat16
HI = lax.Precision.HIGHEST
NEG = -1e30


def mm(a, b):
    return jnp.dot(a, b, preferred_element_type=F32)


def mm_t(a, b):
    return lax.dot_general(a, b, (((1,), (1,)), ((), ())), preferred_element_type=F32)


def softplus(v):
    return jnp.maximum(v, 0.0) + jnp.log1p(jnp.exp(-jnp.abs(v)))


def sigmoid(v):
    return 1.0 / (1.0 + jnp.exp(-v))


def tri_lower():
    rows = lax.broadcasted_iota(jnp.int32, (Q, Q), 0)
    cols = lax.broadcasted_iota(jnp.int32, (Q, Q), 1)
    return rows >= cols


def spread(table, lane):
    return jnp.broadcast_to(table[:, lane : lane + 1], (Q, LANES))


def fill_tables(dt, logs, dt_tab, log_tab, log_rows, low, groups, per):
    log_rows[...] = jnp.transpose(logs)
    for g in range(groups):
        shift = (LANES - (low + g) * per) % LANES
        dt_tab[g] = pltpu.roll(dt, shift, 1) if shift else dt
        log_tab[g] = pltpu.roll(logs, shift, 1) if shift else logs


def scan_forward(proj_ref, cw_ref, cb_ref, vec_ref, skip_ref, out_ref, sum_ref, start_ref,
                 shifted, act, state, dt_tab, log_tab, log_rows, *, inner, nstate, groups, per):
    first = pl.program_id(0) == 0
    conv = inner + 2 * nstate

    @pl.when(first)
    def _():
        shifted[0:8, :] = jnp.zeros((8, conv), F32)
        state[...] = jnp.zeros_like(state)

    shifted[8 : 8 + Q, :] = proj_ref[:, 0:conv]
    wide = 256
    for low in range(0, conv, wide):
        part = pl.ds(low, wide)
        total = cb_ref[0:1, part] + cw_ref[0:1, part] * shifted[5 : 5 + Q, part]
        for k in range(1, 4):
            total = total + cw_ref[k : k + 1, part] * shifted[5 + k : 5 + k + Q, part]
        sum_ref[:, part] = total
        act[:, part] = total * sigmoid(total)
    shifted[0:8, :] = shifted[Q : Q + 8, :]

    dt = softplus(proj_ref[:, conv : conv + LANES] + vec_ref[0:1, :])
    causal = tri_lower()
    logs = jnp.dot(causal.astype(F32), dt * vec_ref[1:2, :], precision=HI, preferred_element_type=F32)
    fill_tables(dt, logs, dt_tab, log_tab, log_rows, 0, groups, per)
    keys_b = act[:, inner : inner + nstate]
    keys_c = act[:, inner + nstate : conv].astype(BF16)
    b_cols = jnp.transpose(keys_b).astype(BF16)
    cross = mm(keys_c, b_cols)
    start_ref[...] = state[...].astype(BF16)
    span = per * HEAD
    low_half = lax.broadcasted_iota(jnp.int32, (Q, LANES), 1) < HEAD

    def group(g, carry):
        base = pl.multiple_of(g * span, span)
        dts, lgs = dt_tab[g], log_tab[g]
        carried = mm(keys_c, start_ref[:, pl.ds(base, span)])
        tails_all = []
        lasts = []
        for j in range(per // 2):
            cols = pl.ds(pl.multiple_of(base + j * LANES, LANES), LANES)
            h = g * per + 2 * j
            col0, col1 = spread(lgs, 2 * j), spread(lgs, 2 * j + 1)
            row0, row1 = log_rows[pl.ds(h, 1), :], log_rows[pl.ds(h + 1, 1), :]
            values = act[:, cols]
            stepped = (values * jnp.where(low_half, spread(dts, 2 * j), spread(dts, 2 * j + 1)))
            stepped_b = stepped.astype(BF16)
            mix0 = (jnp.exp(jnp.where(causal, col0 - row0, NEG)) * cross).astype(BF16)
            mix1 = (jnp.exp(jnp.where(causal, col1 - row1, NEG)) * cross).astype(BF16)
            zero = jnp.zeros_like(stepped_b)
            pairs = jnp.concatenate(
                [jnp.where(low_half, stepped_b, zero), jnp.where(low_half, zero, stepped_b)], axis=0)
            local = mm(jnp.concatenate([mix0, mix1], axis=1), pairs)
            both = jnp.where(low_half, col0, col1)
            last = both[Q - 1 : Q, :]
            out = local + carried[:, j * LANES : (j + 1) * LANES] * jnp.exp(both)
            out_ref[:, cols] = out + skip_ref[0:1, cols] * values
            tails_all.append((stepped * jnp.exp(last - both)).astype(BF16))
            lasts.append(jnp.exp(last))
        fresh = mm(b_cols, jnp.concatenate(tails_all, axis=1))
        cols = pl.ds(base, span)
        state[:, cols] = state[:, cols] * jnp.concatenate(lasts, axis=1) + fresh
        return carry

    lax.fori_loop(0, groups, group, 0)


def run_scan_forward(proj, cw, cb, vec, skip_cols, inner, nstate, groups, per):
    length = proj.shape[0]
    blocks = length // Q
    conv = inner + 2 * nstate
    whole = lambda shape: pl.BlockSpec(shape, lambda i: (0, 0))
    rows = lambda width: pl.BlockSpec((Q, width), lambda i: (i, 0))
    return pl.pallas_call(
        functools.partial(scan_forward, inner=inner, nstate=nstate, groups=groups, per=per),
        grid=(blocks,),
        in_specs=[rows(proj.shape[1]), whole(cw.shape), whole(cb.shape), whole(vec.shape), whole(skip_cols.shape)],
        out_specs=[rows(inner), rows(conv), pl.BlockSpec((nstate, inner), lambda i: (i, 0))],
        out_shape=[
            jax.ShapeDtypeStruct((length, inner), F32),
            jax.ShapeDtypeStruct((length, conv), F32),
            jax.ShapeDtypeStruct((blocks * nstate, inner), BF16),
        ],
        scratch_shapes=[
            pltpu.VMEM((Q + 8, conv), F32),
            pltpu.VMEM((Q, conv), F32),
            pltpu.VMEM((nstate, inner), F32),
            pltpu.VMEM((groups, Q, LANES), F32),
            pltpu.VMEM((groups, Q, LANES), F32),
            pltpu.VMEM((LANES, Q), F32),
        ],
        compiler_params=pltpu.CompilerParams(vmem_limit_bytes=60 << 20),
        cost_estimate=pl.CostEstimate(flops=12_000_000_000, bytes_accessed=60_000_000, transcendentals=20_000_000),
        name="scan_forward",
    )(proj, cw, cb, vec, skip_cols)


def piece_copies(place_ref, pieces, refs, target, sems):
    copies = []
    for index, (start, half, size, lane) in enumerate(pieces):
        rows, cols = refs[index].shape
        if half is not None:
            start = pl.multiple_of(start + jnp.bitwise_xor(place_ref[1], half) * size, 16)
        window = target.at[pl.ds(start, rows), pl.ds(lane, cols)]
        copies.append(pltpu.make_async_copy(refs[index], window, sems.at[index]))
    return copies


def load_pieces(*args):
    for copy in piece_copies(*args):
        copy.start()


def wait_pieces(*args):
    for copy in piece_copies(*args):
        copy.wait()


def columns_of(place_ref, position, order, width):
    return pl.ds(pl.multiple_of(jnp.bitwise_xor(place_ref[0], order[position]) * width, LANES), width)


def project_in(place_ref, tok_ref, gain_ref, *rest, pieces, order):
    refs, (normed_ref, proj_ref, weight, sems) = rest[: len(pieces)], rest[len(pieces) :]
    first = pl.program_id(0) == 0

    @pl.when(first)
    def _():
        load_pieces(place_ref, pieces, refs, weight, sems)

    width = tok_ref.shape[1] // len(order)
    tok = tok_ref[...].astype(F32)
    scale = lax.rsqrt(jnp.mean(tok * tok, axis=1, keepdims=True) + EPS)
    for position in range(len(order)):
        cols = columns_of(place_ref, position, order, width)
        value = tok_ref[:, cols].astype(F32) * scale * gain_ref[0:1, cols]
        normed_ref[:, position * width : (position + 1) * width] = value.astype(BF16)

    @pl.when(first)
    def _():
        wait_pieces(place_ref, pieces, refs, weight, sems)

    total = proj_ref.shape[1]
    step = 384
    for low in range(0, total, step):
        proj_ref[:, low : low + step] = mm_t(normed_ref[...], weight[low : low + step, :])


def grid_of(grid, in_specs, out_specs, scratch):
    return pltpu.PrefetchScalarGridSpec(
        num_scalar_prefetch=1, grid=grid, in_specs=in_specs, out_specs=out_specs, scratch_shapes=scratch)


def anywhere(count):
    return [pl.BlockSpec(memory_space=pl.ANY)] * count


def row_block(block, width):
    return pl.BlockSpec((block, width), lambda i, s: (i, 0))


def fixed(shape):
    return pl.BlockSpec(shape, lambda i, s: (0,) * len(shape))


def run_project_in(place, tok, gain, weight, total, order, block=256):
    pieces, arrays = weight
    length, width = tok.shape
    return pl.pallas_call(
        functools.partial(project_in, pieces=pieces, order=order),
        grid_spec=grid_of(
            (length // block,),
            [row_block(block, width), fixed(gain.shape)] + anywhere(len(pieces)),
            [row_block(block, width), row_block(block, total)],
            [pltpu.VMEM((total, width), BF16), pltpu.SemaphoreType.DMA((len(pieces),))],
        ),
        out_shape=[jax.ShapeDtypeStruct((length, width), BF16), jax.ShapeDtypeStruct((length, total), F32)],
        compiler_params=pltpu.CompilerParams(vmem_limit_bytes=50 << 20),
        cost_estimate=pl.CostEstimate(flops=20_000_000_000, bytes_accessed=30_000_000, transcendentals=1000),
        name="project_in",
    )(place, tok, gain, *arrays)


def gating(place_ref, normed_ref, cot_ref, scan_ref, gain_ref, *rest, wg_pieces, ow_pieces, order):
    n_g, n_o = len(wg_pieces), len(ow_pieces)
    wg_refs, ow_refs = rest[:n_g], rest[n_g : n_g + n_o]
    (mixed_ref, dscan_ref, dgate_ref, dgain_ref, wg, ow, gate_s, gated_s, scaled_s,
     g_sems, o_sems) = rest[n_g + n_o :]
    inner = wg.shape[0]
    parts = len(order)
    width = inner // parts
    first = pl.program_id(0) == 0

    @pl.when(first)
    def _():
        load_pieces(place_ref, wg_pieces, wg_refs, wg, g_sems)
        load_pieces(place_ref, ow_pieces, ow_refs, ow, o_sems)
        dgain_ref[...] = jnp.zeros_like(dgain_ref)
        wait_pieces(place_ref, wg_pieces, wg_refs, wg, g_sems)

    def fold(v):
        total = v[:, 0:LANES]
        for low in range(LANES, v.shape[1], LANES):
            total = total + v[:, low : low + LANES]
        return total

    power = None
    for p in range(parts):
        cols = slice(p * width, (p + 1) * width)
        gate = mm_t(normed_ref[...], wg[cols, :])
        gated = scan_ref[:, cols] * (gate * sigmoid(gate))
        gate_s[:, cols] = gate
        gated_s[:, cols] = gated
        term = fold(gated * gated)
        power = term if power is None else power + term
    scale = lax.rsqrt(jnp.sum(power, axis=1, keepdims=True) / inner + EPS)

    @pl.when(first)
    def _():
        wait_pieces(place_ref, ow_pieces, ow_refs, ow, o_sems)

    match = None
    for p in range(parts):
        true = columns_of(place_ref, p, order, width)
        rows = slice(p * width, (p + 1) * width)
        grad = mm_t(cot_ref[...], ow[rows, :])
        gated = gated_s[:, true]
        gain = gain_ref[0:1, true]
        unit = gated * scale
        mixed_ref[:, rows] = (unit * gain).astype(BF16)
        dgain_ref[0:1, true] += jnp.sum(grad * unit, axis=0, keepdims=True)
        scaled = grad * gain
        scaled_s[:, true] = scaled
        term = fold(scaled * gated)
        match = term if match is None else match + term
    pull = jnp.sum(match, axis=1, keepdims=True) * (scale * scale) / inner
    for p in range(parts):
        cols = slice(p * width, (p + 1) * width)
        gate = gate_s[:, cols]
        sig = sigmoid(gate)
        silu = gate * sig
        dgated = scale * (scaled_s[:, cols] - gated_s[:, cols] * pull)
        dscan_ref[:, cols] = dgated * silu
        dgate_ref[:, cols] = (dgated * scan_ref[:, cols] * (sig + silu * (1.0 - sig))).astype(BF16)


def run_gating(place, normed, gate_weight, out_weight, cot, scan_out, gain, order, block=256):
    wg_pieces, wg_arrays = gate_weight
    ow_pieces, ow_arrays = out_weight
    length, width = normed.shape
    inner = scan_out.shape[1]
    return pl.pallas_call(
        functools.partial(gating, wg_pieces=wg_pieces, ow_pieces=ow_pieces, order=order),
        grid_spec=grid_of(
            (length // block,),
            [row_block(block, width), row_block(block, width), row_block(block, inner), fixed((1, inner))]
            + anywhere(len(wg_pieces) + len(ow_pieces)),
            [row_block(block, inner), row_block(block, inner), row_block(block, inner), fixed((1, inner))],
            [pltpu.VMEM((inner, width), BF16), pltpu.VMEM((inner, width), BF16)]
            + [pltpu.VMEM((block, inner), F32)] * 3
            + [pltpu.SemaphoreType.DMA((len(wg_pieces),)), pltpu.SemaphoreType.DMA((len(ow_pieces),))],
        ),
        out_shape=[
            jax.ShapeDtypeStruct((length, inner), BF16),
            jax.ShapeDtypeStruct((length, inner), F32),
            jax.ShapeDtypeStruct((length, inner), BF16),
            jax.ShapeDtypeStruct((1, inner), F32),
        ],
        compiler_params=pltpu.CompilerParams(vmem_limit_bytes=62 << 20),
        cost_estimate=pl.CostEstimate(flops=40_000_000_000, bytes_accessed=70_000_000, transcendentals=10_000_000),
        name="gating",
    )(place, normed, cot, scan_out, gain, *wg_arrays, *ow_arrays)


def gate_back(place_ref, dgate_ref, *rest, pieces):
    refs, (grad_ref, weight, sems) = rest[: len(pieces)], rest[len(pieces) :]

    @pl.when(pl.program_id(0) == 0)
    def _():
        load_pieces(place_ref, pieces, refs, weight, sems)
        wait_pieces(place_ref, pieces, refs, weight, sems)

    step = 384
    for low in range(0, grad_ref.shape[1], step):
        grad_ref[:, low : low + step] = mm(dgate_ref[...], weight[:, low : low + step])


def run_gate_back(place, dgate, model, weight, block=256):
    pieces, arrays = weight
    length, inner = dgate.shape
    return pl.pallas_call(
        functools.partial(gate_back, pieces=pieces),
        grid_spec=grid_of(
            (length // block,),
            [row_block(block, inner)] + anywhere(len(pieces)),
            row_block(block, model),
            [pltpu.VMEM((inner, model), BF16), pltpu.SemaphoreType.DMA((len(pieces),))],
        ),
        out_shape=jax.ShapeDtypeStruct((length, model), F32),
        compiler_params=pltpu.CompilerParams(vmem_limit_bytes=40 << 20),
        cost_estimate=pl.CostEstimate(flops=16_000_000_000, bytes_accessed=22_000_000, transcendentals=0),
        name="gate_back",
    )(place, dgate, *arrays)


def input_back(place_ref, part_ref, tok_ref, cot_ref, gain_ref, *rest, count, pieces, order):
    dproj_refs, rest = rest[:count], rest[count:]
    refs, (grad_ref, dgain_ref, weight, dn, sems) = rest[: len(pieces)], rest[len(pieces) :]
    first = pl.program_id(0) == 0

    @pl.when(first)
    def _():
        load_pieces(place_ref, pieces, refs, weight, sems)
        dgain_ref[...] = jnp.zeros_like(dgain_ref)
        wait_pieces(place_ref, pieces, refs, weight, sems)

    model = tok_ref.shape[1]
    width = model // len(order)
    tok = tok_ref[...].astype(F32)
    scale = lax.rsqrt(jnp.mean(tok * tok, axis=1, keepdims=True) + EPS)
    match = None
    for position in range(len(order)):
        spot = slice(position * width, (position + 1) * width)
        true = columns_of(place_ref, position, order, width)
        grad, low = part_ref[:, spot], 0
        for ref in dproj_refs:
            grad = grad + mm(ref[...], weight[low : low + ref.shape[1], spot])
            low += ref.shape[1]
        value = tok_ref[:, true].astype(F32)
        dgain_ref[0:1, true] += jnp.sum(grad * (value * scale), axis=0, keepdims=True)
        grad = grad * gain_ref[0:1, true]
        dn[:, spot] = grad
        term = jnp.sum(grad * value, axis=1, keepdims=True)
        match = term if match is None else match + term
    pull = match * (scale * scale * scale) / model
    for position in range(len(order)):
        spot = slice(position * width, (position + 1) * width)
        true = columns_of(place_ref, position, order, width)
        value = tok_ref[:, true].astype(F32)
        grad_ref[:, true] = cot_ref[:, true].astype(F32) + (scale * dn[:, spot] - value * pull)


def run_input_back(place, part, dprojs, tok, cot, gain, weight, order, block=256):
    pieces, arrays = weight
    length, model = tok.shape
    widths = [d.shape[1] for d in dprojs]
    return pl.pallas_call(
        functools.partial(input_back, count=len(dprojs), pieces=pieces, order=order),
        grid_spec=grid_of(
            (length // block,),
            [row_block(block, model), row_block(block, model), row_block(block, model), fixed((1, model))]
            + [row_block(block, w) for w in widths] + anywhere(len(pieces)),
            [row_block(block, model), fixed((1, model))],
            [pltpu.VMEM((sum(widths), model), BF16), pltpu.VMEM((block, model), F32),
             pltpu.SemaphoreType.DMA((len(pieces),))],
        ),
        out_shape=[jax.ShapeDtypeStruct((length, model), F32), jax.ShapeDtypeStruct((1, model), F32)],
        compiler_params=pltpu.CompilerParams(vmem_limit_bytes=50 << 20),
        cost_estimate=pl.CostEstimate(flops=22_000_000_000, bytes_accessed=46_000_000, transcendentals=1000),
        name="input_back",
    )(place, part, tok, cot, gain, *dprojs, *arrays)


def project_out(place_ref, mixed_ref, tok_ref, *rest, pieces):
    refs, (out_ref, weight, sems) = rest[: len(pieces)], rest[len(pieces) :]

    @pl.when(pl.program_id(0) == 0)
    def _():
        load_pieces(place_ref, pieces, refs, weight, sems)
        wait_pieces(place_ref, pieces, refs, weight, sems)

    step = 384
    for low in range(0, out_ref.shape[1], step):
        cols = slice(low, low + step)
        out_ref[:, cols] = (tok_ref[:, cols].astype(F32) + mm(mixed_ref[...], weight[:, cols])).astype(BF16)


def run_project_out(place, mixed, tok, weight, block=256):
    pieces, arrays = weight
    length, model = tok.shape
    inner = mixed.shape[1]
    return pl.pallas_call(
        functools.partial(project_out, pieces=pieces),
        grid_spec=grid_of(
            (length // block,),
            [row_block(block, inner), row_block(block, model)] + anywhere(len(pieces)),
            row_block(block, model),
            [pltpu.VMEM((inner, model), BF16), pltpu.SemaphoreType.DMA((len(pieces),))],
        ),
        out_shape=jax.ShapeDtypeStruct((length, model), BF16),
        compiler_params=pltpu.CompilerParams(vmem_limit_bytes=40 << 20),
        cost_estimate=pl.CostEstimate(flops=14_000_000_000, bytes_accessed=20_000_000, transcendentals=0),
        name="project_out",
    )(place, mixed, tok, *arrays)


def scan_backward(proj_ref, tail_ref, sum_ref, keys_ref, out_ref, dout_ref, start_ref, cw_ref, cwk_ref, vec_ref,
                  skip_ref, pick_ref, *rest, nstate, low, groups, per, begin, last):
    if not begin:
        old_cross_ref, old_keys_ref, old_raw_ref = rest[:3]
        rest = rest[3:]
    dproj_ref, dcw_ref, dcb_ref, dskip_ref, dvec_ref = rest[:5]
    rest = rest[5:]
    if not last:
        cross_ref, keys_ref_out, raw_ref = rest[:3]
        rest = rest[3:]
    dsum, dstate, edge, logs_v, tails_v, steps_v, dt_tab, log_tab, log_rows, dcross, dkeys = rest
    first = pl.program_id(0) == 0
    span_all = groups * per * HEAD
    conv = dsum.shape[1]

    @pl.when(first)
    def _():
        dsum[Q : Q + 8, :] = jnp.zeros((8, conv), F32)
        dstate[...] = jnp.zeros_like(dstate)
        edge[...] = jnp.zeros_like(edge)
        dcw_ref[...] = jnp.zeros_like(dcw_ref)
        dcb_ref[...] = jnp.zeros_like(dcb_ref)
        dskip_ref[...] = jnp.zeros_like(dskip_ref)
        dvec_ref[...] = jnp.zeros_like(dvec_ref)

    raw = tail_ref[:, 2 * nstate : 2 * nstate + LANES] + vec_ref[0:1, :]
    dt = softplus(raw)
    lower = tri_lower()
    rate = vec_ref[1:2, :]
    logs = jnp.dot(lower.astype(F32), dt * rate, precision=HI, preferred_element_type=F32)
    fill_tables(dt, logs, dt_tab, log_tab, log_rows, low, groups, per)
    sum_b = keys_ref[:, 0:nstate]
    sum_c = keys_ref[:, nstate : 2 * nstate]
    sig_b, sig_c = sigmoid(sum_b), sigmoid(sum_c)
    keys_b32, keys_c32 = sum_b * sig_b, sum_c * sig_c
    keys_b, keys_c = keys_b32.astype(BF16), keys_c32.astype(BF16)
    c_cols = jnp.transpose(keys_c32).astype(BF16)
    cross = mm(keys_b, c_cols)
    span = per * HEAD
    low_half = lax.broadcasted_iota(jnp.int32, (Q, LANES), 1) < HEAD
    upper = lax.broadcasted_iota(jnp.int32, (Q, Q), 0) <= lax.broadcasted_iota(jnp.int32, (Q, Q), 1)
    if not begin:
        dcross[...] = old_cross_ref[...]
        dkeys[...] = old_keys_ref[...]
    else:
        dcross[...] = jnp.zeros_like(dcross)
        dkeys[...] = jnp.zeros_like(dkeys)

    def group(g, carry):
        base = pl.multiple_of(g * span, span)
        whole = pl.ds(base, span)
        dts, lgs = dt_tab[g], log_tab[g]
        dstate_b = dstate[:, whole].astype(BF16)
        from_state = mm(keys_b, dstate_b)
        tails_all, outs_all, lasts = [], [], []
        dcr = None
        for j in range(per // 2):
            cols = pl.ds(pl.multiple_of(base + j * LANES, LANES), LANES)
            h = (low + g) * per + 2 * j
            col0, col1 = spread(lgs, 2 * j), spread(lgs, 2 * j + 1)
            row0, row1 = log_rows[pl.ds(h, 1), :], log_rows[pl.ds(h + 1, 1), :]
            total = sum_ref[:, cols]
            sig = sigmoid(total)
            values = total * sig
            step = jnp.where(low_half, spread(dts, 2 * j), spread(dts, 2 * j + 1))
            stepped = values * step
            stepped_b = stepped.astype(BF16)
            dout = dout_ref[:, cols]
            dout_b = dout.astype(BF16)
            decay0 = jnp.exp(jnp.where(upper, row0 - col0, NEG))
            decay1 = jnp.exp(jnp.where(upper, row1 - col1, NEG))
            mix = jnp.concatenate([(decay0 * cross).astype(BF16), (decay1 * cross).astype(BF16)], axis=1)
            zero = jnp.zeros_like(dout_b)
            douts = jnp.concatenate(
                [jnp.where(low_half, dout_b, zero), jnp.where(low_half, zero, dout_b)], axis=0)
            local = mm(mix, douts)
            dmix = mm_t(stepped_b, douts)
            term = dmix[:, 0:Q] * decay0 + dmix[:, Q : 2 * Q] * decay1
            dcr = term if dcr is None else dcr + term
            both = jnp.where(low_half, col0, col1)
            last = both[Q - 1 : Q, :]
            tail = jnp.exp(last - both)
            passed = from_state[:, j * LANES : (j + 1) * LANES] * tail
            dstepped = local + passed
            skip = skip_ref[0:1, cols]
            scan = out_ref[:, cols] - skip * values
            logs_v[:, cols] = dout_b.astype(F32) * scan - stepped_b.astype(F32) * local
            tails_v[:, cols] = stepped * passed
            steps_v[:, cols] = dstepped * values
            dvalues = dstepped * step + dout * skip
            dskip_ref[0:1, cols] += jnp.sum(dout * values, axis=0, keepdims=True)
            dsum[0:Q, cols] = dvalues * (sig + values * (1.0 - sig))
            tails_all.append((stepped * tail).astype(BF16))
            outs_all.append((dout * jnp.exp(both)).astype(BF16))
            lasts.append(jnp.exp(last))
        dcross[...] += dcr
        outs = jnp.concatenate(outs_all, axis=1)
        starts = start_ref[:, whole]
        dkeys[:, nstate : 2 * nstate] += mm_t(outs, starts)
        dkeys[:, 0:nstate] += mm_t(jnp.concatenate(tails_all, axis=1), dstate_b)
        kept = dstate[:, whole] * jnp.concatenate(lasts, axis=1)
        edge[0:1, whole] = jnp.sum(kept * starts.astype(F32), axis=0, keepdims=True)
        dstate[:, whole] = kept + mm(c_cols, outs)
        return carry

    lax.fori_loop(0, groups, group, 0)

    if last:
        dcr = dcross[...]
        exact = lambda u, v: jnp.dot(u, v, precision=HI, preferred_element_type=F32)
        d_b = dkeys[:, 0:nstate] + exact(dcr, keys_c32)
        d_c = dkeys[:, nstate : 2 * nstate] + exact(jnp.transpose(dcr), keys_b32)
        dsum[0:Q, span_all : span_all + nstate] = d_b * (sig_b + keys_b32 * (1.0 - sig_b))
        dsum[0:Q, span_all + nstate : conv] = d_c * (sig_c + keys_c32 * (1.0 - sig_c))
    else:
        cross_ref[...] = dcross[...]
        keys_ref_out[...] = dkeys[...]

    def reduce_heads(v):
        high = v.astype(BF16)
        low = (v - high.astype(F32)).astype(BF16)
        return mm(high, pick_ref[...]) + mm(low, pick_ref[...])

    dlogs = reduce_heads(logs_v[...])
    dtails = reduce_heads(tails_v[...])
    dlogit = (
        jnp.dot(upper.astype(F32), dlogs, precision=HI, preferred_element_type=F32)
        + jnp.dot(1.0 - upper.astype(F32), dtails, precision=HI, preferred_element_type=F32)
        + reduce_heads(edge[...])[0:1, :]
    )
    dstep = reduce_heads(steps_v[...]) + dlogit * rate
    draw = dstep * sigmoid(raw)
    dvec_ref[0:1, :] += jnp.sum(draw, axis=0, keepdims=True)
    dvec_ref[1:2, :] += jnp.sum(dlogit * dt * rate, axis=0, keepdims=True)
    if last:
        dproj_ref[:, conv : conv + LANES] = (draw + old_raw_ref[...]).astype(BF16)
    elif begin:
        raw_ref[...] = draw
    else:
        raw_ref[...] = draw + old_raw_ref[...]

    wide = 256
    for start in range(0, conv, wide):
        part = pl.ds(start, wide)
        if start < span_all:
            source, taps_ref, local = proj_ref, cw_ref, part
        else:
            source, taps_ref, local = tail_ref, cwk_ref, pl.ds(start - span_all, wide)
        taken = source[:, local]
        total = None
        for k in range(4):
            moved = dsum[3 - k : 3 - k + Q, part]
            dcw_ref[k : k + 1, part] += jnp.sum(taken * moved, axis=0, keepdims=True)
            term = taps_ref[k : k + 1, local] * moved
            total = term if total is None else total + term
            if k == 3:
                dcb_ref[0:1, part] += jnp.sum(moved, axis=0, keepdims=True)
        dproj_ref[:, part] = total.astype(BF16)
    dsum[Q : Q + 8, :] = dsum[0:8, :]


def run_scan_backward(proj, sums, scan_out, dscan, starts, cw, vec, skip_cols, pick, inner, nstate, low, groups, per,
                      previous, last):
    length = proj.shape[0]
    blocks = length // Q
    span = groups * per * HEAD
    begin = previous is None
    conv = span + (2 * nstate if last else 0)
    where = low * per * HEAD // span
    whole = lambda shape: pl.BlockSpec(shape, lambda i: (0, 0))
    rows = lambda width, col=0: pl.BlockSpec((Q, width), lambda i: (blocks - 1 - i, col))
    part = lambda height: pl.BlockSpec((height, span), lambda i: (0, where))
    tail = 2 * nstate + LANES
    out_specs = [rows(conv + (LANES if last else 0)), whole((4, conv)), whole((1, conv)), whole((1, span)),
                 whole((8, LANES))]
    out_shape = [
        jax.ShapeDtypeStruct((length, conv + (LANES if last else 0)), BF16),
        jax.ShapeDtypeStruct((4, conv), F32),
        jax.ShapeDtypeStruct((1, conv), F32),
        jax.ShapeDtypeStruct((1, span), F32),
        jax.ShapeDtypeStruct((8, LANES), F32),
    ]
    carried = [rows(Q), rows(2 * nstate), rows(LANES)]
    if not last:
        out_specs += carried
        out_shape += [jax.ShapeDtypeStruct((length, w), F32) for w in (Q, 2 * nstate, LANES)]
    return pl.pallas_call(
        functools.partial(scan_backward, nstate=nstate, low=low, groups=groups, per=per, begin=begin, last=last),
        grid=(blocks,),
        in_specs=[
            rows(span, where), rows(tail, inner // tail), rows(span, where), rows(2 * nstate, inner // (2 * nstate)),
            rows(span, where), rows(span, where),
            pl.BlockSpec((nstate, span), lambda i: (blocks - 1 - i, where)),
            part(4), pl.BlockSpec((4, 2 * nstate), lambda i: (0, inner // (2 * nstate))),
            whole(vec.shape), part(1), pl.BlockSpec((span, LANES), lambda i: (where, 0)),
        ] + ([] if begin else carried),
        out_specs=out_specs,
        out_shape=out_shape,
        scratch_shapes=[
            pltpu.VMEM((Q + 8, conv), F32),
            pltpu.VMEM((nstate, span), F32),
            pltpu.VMEM((8, span), F32),
            pltpu.VMEM((Q, span), F32),
            pltpu.VMEM((Q, span), F32),
            pltpu.VMEM((Q, span), F32),
            pltpu.VMEM((groups, Q, LANES), F32),
            pltpu.VMEM((groups, Q, LANES), F32),
            pltpu.VMEM((LANES, Q), F32),
            pltpu.VMEM((Q, Q), F32),
            pltpu.VMEM((Q, 2 * nstate), F32),
        ],
        compiler_params=pltpu.CompilerParams(vmem_limit_bytes=50 << 20),
        cost_estimate=pl.CostEstimate(flops=40_000_000_000, bytes_accessed=40_000_000, transcendentals=15_000_000),
        name="scan_backward",
    )(proj, proj, sums, sums, scan_out, dscan, starts, cw, cw, vec, skip_cols, pick, *(previous or ()))


def bits_of(size):
    return [1 << b for b in range(size.bit_length() - 1)]


def swap(value, axis, bit, size):
    return lax.ppermute(value, axis, [(i, i ^ bit) for i in range(size)])


def after(value, *deps):
    return lax.optimization_barrier((value,) + deps)[0] if deps else value


def order_of(size):
    flipped = []
    for index in range(size):
        value = 0
        for low, high in zip(bits_of(size), reversed(bits_of(size))):
            value |= high if index & low else 0
        flipped.append(value)
    return flipped


class Gather:
    def __init__(self, shard, order, rep_index, groups, copies, lanes, chunks):
        self.order, self.groups, self.copies = order, groups, copies
        self.size = shard.shape
        self.lanes = lanes
        self.half = shard.shape[0] // 2
        self.rows = self.half // chunks
        self.shard = shard
        parity = rep_index & 1
        self.mine = [lax.dynamic_slice_in_dim(shard, parity * self.half + c * self.rows, self.rows, 0)
                     for c in range(chunks)]
        self.there, self.across = [None] * chunks, [None] * chunks

    def far(self, chunk, *deps):
        value = after(self.mine[chunk], *deps)
        self.there[chunk] = swap(value, "shard", 2, self.groups)

    def side(self, chunk):
        self.across[chunk] = swap(self.there[chunk], "rep", 1, self.copies)

    def finish(self, *deps):
        have = {0: [(0, None, 0, self.shard)]}
        have[2] = [(c * self.rows, h, self.half, v) for h, vs in ((0, self.there), (1, self.across))
                   for c, v in enumerate(vs)]
        for source in (0, 2):
            have[source ^ 1] = [(r, h, s, swap(after(v, *deps) if v is self.across[-1] else v, "shard", 1, self.groups))
                                for r, h, s, v in have[source]]
        pieces, arrays = [], []
        for position, source in enumerate(self.order):
            for row, half, size, value in have[source]:
                if self.lanes:
                    pieces.append((row, half, size, position * self.size[1]))
                else:
                    pieces.append((row + position * self.size[0], half, size, 0))
                arrays.append(value)
        return tuple(pieces), tuple(arrays)


class Total:
    def __init__(self, kept, sent, axis, rep_index, groups, copies):
        self.axis, self.rep_index = axis, rep_index
        self.sizes = {"shard": groups, "rep": copies}
        self.stages = [("shard", index, 1) for index in range(len(bits_of(groups)))]
        count = len(bits_of(copies))
        over = [("rep", 0, 1)] + [("rep", index, min(2, count - index)) for index in range(1, count, 2)]
        self.stages += over
        self.back = list(reversed(over))
        self.value, self.out = kept, [sent]
        self.fly()

    @classmethod
    def join(cls, chains):
        first = chains[0]
        new = object.__new__(cls)
        new.axis, new.rep_index, new.sizes = first.axis, first.rep_index, first.sizes
        new.stages, new.back = first.stages, first.back
        new.value = jnp.concatenate([v.value for v in chains])
        new.coming = [jnp.concatenate(v) for v in zip(*(c.coming for c in chains))]
        return new

    def fly(self):
        name, shift, _ = self.stages[0]
        self.coming = [swap(v, name, (k + 1) << shift, self.sizes[name]) for k, v in enumerate(self.out)]

    def done(self):
        return not self.stages and not self.back

    def step(self, *deps):
        coming = [after(v, *deps) for v in self.coming]
        if not self.stages:
            return self.widen(coming)
        self.stages.pop(0)
        terms = [self.value] + coming
        if not self.stages:
            self.value = sum(v.astype(F32) for v in terms).astype(BF16)
            self.fly_back()
            return [self.value]
        name, shift, width = self.stages[0]
        parts = 1 << width
        axis = self.axis if name == "shard" else 0
        size = self.value.shape[axis] // parts
        mine = 0 if name == "shard" else (self.rep_index >> shift) & (parts - 1)
        cut = lambda start: sum(lax.dynamic_slice_in_dim(v, start, size, axis).astype(F32) for v in terms)
        self.out = [cut((mine ^ k) * size).astype(BF16) for k in range(1, parts)]
        self.value = cut(mine * size)
        self.fly()
        return self.out

    def reduce(self, *deps):
        terms = [self.value] + [after(v, *deps) for v in self.coming]
        mine = sum(v.astype(F32) for v in terms).astype(BF16)
        self.value = [lax.psum(mine, "rep")]
        self.stages, self.back = [], []
        return [mine]

    def fly_back(self):
        name, shift, width = self.back[0]
        self.coming = [swap(self.value, name, k << shift, self.sizes[name]) for k in range(1, 1 << width)]

    def widen(self, coming):
        name, shift, width = self.back.pop(0)
        parts = [self.value] + coming
        for bit in range(width):
            turn = ((self.rep_index >> (shift + bit)) & 1) != 0
            parts = [jnp.where(turn, parts[k ^ (1 << bit)], parts[k]) for k in range(len(parts))]
        if not self.back:
            self.value = [v.astype(F32) for v in parts]
            return self.value
        self.value = jnp.concatenate(parts)
        self.fly_back()
        return [self.value]


def outer(left, right):
    return lax.dot_general(left, right, (((0,), (0,)), ((), ())), preferred_element_type=F32).astype(BF16)


def on_device(groups, copies, tokens, norm_gain, in_weight, conv_weight, conv_bias, dt_bias, a_log, skip, gate_gain,
              out_weight, cotangent):
    if tokens.shape[0] != 1 or groups != 4:
        raise ValueError("unexpected sizes")
    order = order_of(groups)
    shard_index = lax.axis_index("shard")
    rep_index = lax.axis_index("rep")
    tok, cot = tokens[0], cotangent[0]
    inner = gate_gain.shape[0] * groups
    conv = conv_bias.shape[0] * groups
    heads = dt_bias.shape[0] * groups
    nstate = (conv - inner) // 2
    model = tok.shape[1]
    taps = conv_weight.shape[0]
    outputs_all = in_weight.shape[1]
    place = jnp.stack([shard_index, rep_index & 1]).astype(jnp.int32)

    turned = in_weight.T
    total = conv + LANES
    conv_part = jnp.pad(turned[inner:], ((0, total + inner - outputs_all), (0, 0)))
    make = lambda shard, lanes, chunks: Gather(shard, order, rep_index, groups, copies, lanes, chunks)
    wc = make(conv_part, True, 2)
    wg = make(turned[:inner], True, 1)
    ow = make(out_weight, False, 1)

    small = (norm_gain, conv_bias, dt_bias, a_log, skip, gate_gain, conv_weight)
    packed = jnp.concatenate([v.reshape(-1) for v in small])
    wc.far(0)
    wc.far(1, wg.mine[0], ow.mine[0])
    wc.side(0)
    wc.side(1)
    wg.far(0, wc.there[1])
    ow.far(0, wc.there[1])
    rows = [packed, swap(packed, "shard", 1, groups)]
    far = swap(packed, "shard", 2, groups)
    rows += [far, swap(far, "shard", 1, groups)]
    for bit in bits_of(groups):
        turn = (shard_index & bit) != 0
        rows = [jnp.where(turn, rows[j ^ bit], rows[j]) for j in range(groups)]
    everyone = jnp.stack(rows).astype(F32)
    parts, low = [], 0
    for v in small:
        parts.append(everyone[:, low : low + v.size])
        low += v.size
    gain, cb, db, al, sk, gg = (v.reshape(-1) for v in parts[:6])
    cw = parts[6].reshape(groups, taps, -1).transpose(1, 0, 2).reshape(taps, conv)
    gain, cb, gg = gain[None], cb[None], gg[None]
    vec = jnp.pad(jnp.stack([db, -jnp.exp(al)]), ((0, 6), (0, LANES - heads)))
    skip_cols = jnp.repeat(sk, inner // heads)[None]
    pick = (jnp.arange(inner)[:, None] // (inner // heads) == jnp.arange(LANES)[None]).astype(BF16)

    wc = wc.finish(gain, cb, gg, cw, vec, skip_cols, pick)
    normed, proj = run_project_in(place, tok, gain, wc, total, order)
    for weight in (wg, ow):
        weight.there[0] = after(weight.there[0], normed)
        weight.side(0)
    proj = after(proj, wg.there[0], ow.there[0])
    per = 8
    scan_out, sums, starts = run_scan_forward(proj, cw, cb, vec, skip_cols, inner, nstate, heads // per, per)
    wg, ow = wg.finish(scan_out), ow.finish(scan_out)
    mixed, dscan, dgate, dgg = run_gating(place, normed, wg, ow, cot, scan_out, gg, order)

    chain = lambda kept, sent, axis: Total(kept, sent, axis, rep_index, groups, copies)
    half = inner // 2
    out_sent = outer(mixed[:, half:], cot)
    o = chain(outer(mixed[:, :half], cot), out_sent, 0)
    half = model // 2
    left, right = normed[:, :half], normed[:, half:]
    gate_sent = outer(dgate, right)
    marks = o.step(gate_sent)
    g = chain(outer(after(dgate, *marks), left), gate_sent, 1)
    marks = marks + g.step(g.value)

    blocks = heads // per
    cuts = [blocks * v // 3 for v in range(4)]
    chains, grads, carried = [o, g], [], None
    for index in range(3):
        low, high = cuts[index], cuts[index + 1]
        found = run_scan_backward(
            proj, sums, scan_out, after(dscan, *marks), starts, cw, vec, skip_cols, pick, inner, nstate, low,
            high - low, per, carried, index == 2)
        grads.append(found[:5])
        carried = tuple(found[5:])
        dproj, marks = found[0], []
        if index == 2:
            ab = Total.join(chains[2:])
            marks = g.step(dproj)
            marks = marks + ab.step(dproj, *marks)
        dproj = after(dproj, *marks)
        sent = outer(dproj, right)
        kept = outer(dproj, left)
        new = chain(kept, sent, 1)
        marks = marks + new.step(kept)
        if index == 0:
            marks = marks + o.reduce(kept, *marks)
        if index == 1:
            marks = marks + g.step(kept, *marks)
        chains.append(new)
    c = chains[4]

    part = run_gate_back(place, after(dgate, *marks), model, wg)
    marks = ab.coming + g.step(part, *ab.coming)
    marks = marks + c.step(part, *marks)
    input_grad, dgain = run_input_back(place, after(part, *marks), [v[0] for v in grads], tok, cot, gain, wc, order)

    dcw = jnp.concatenate([v[1] for v in grads], axis=1)
    dcb = jnp.concatenate([v[2][0] for v in grads])
    dskip = jnp.concatenate([v[3][0] for v in grads]).reshape(heads, -1).sum(1)
    dvec = sum(v[4] for v in grads)
    pieces = (dcb, dvec[0, :heads], dvec[1, :heads], dskip, dgg[0])
    flat = jnp.concatenate([v.reshape(groups, -1) for v in pieces]
                           + [dcw.reshape(taps, groups, -1).transpose(1, 0, 2).reshape(groups, -1)], axis=1)
    flat = jnp.concatenate([dgain[0].reshape(groups, -1), flat], axis=1)
    abc = Total.join([ab, c])
    marks = abc.step(dgain, *g.coming, *o.value)
    marks = marks + g.step(*marks)
    output = run_project_out(place, after(mixed, *marks), tok, ow)
    marks = abc.step(output, *g.coming)
    flat = after(flat, output, *marks)
    for axis, size in (("shard", groups), ("rep", copies)):
        for bit in bits_of(size):
            flat = flat + swap(flat, axis, bit, size)
    while not all(old.done() for old in (g, abc)):
        for old in (g, abc):
            if not old.done():
                old.step()

    cut = ab.value.shape[0]
    halves = [v[:cut] for v in abc.value] + [v[cut:] for v in abc.value]
    in_total = jnp.concatenate(g.value + halves)[:outputs_all].T
    out_total = o.value[0].astype(F32)

    own = lax.dynamic_slice_in_dim(flat, shard_index, 1, 0)[0]
    shares, low = [], 0
    for v in small:
        shares.append(own[low : low + v.size].reshape(v.shape))
        low += v.size
    d_gain, d_cb, d_db, d_al, d_sk, d_gg, d_cw = shares
    return (output[None], input_grad[None], d_gain, in_total, d_cw, d_cb, d_db, d_al, d_sk, d_gg, out_total)


def solution(mesh):
    whole = P(("shard", "rep"), None, None)
    row, matrix, cols = P("shard"), P("shard", None), P(None, "shard")
    return jax.shard_map(
        functools.partial(on_device, mesh.shape["shard"], mesh.shape["rep"]),
        mesh=mesh,
        in_specs=(whole, row, matrix, cols, row, row, row, row, row, matrix, whole),
        out_specs=(whole, whole, row, matrix, cols, row, row, row, row, row, matrix),
        check_vma=False,
    )
```

```python
import functools

import jax
import jax.numpy as jnp
from jax import lax
from jax.experimental import pallas as pl
from jax.experimental.pallas import tpu as pltpu
from jax.sharding import PartitionSpec as P

Q = 128
LANES = 128
HEAD = 64
EPS = 1e-05
F32 = jnp.float32
BF16 = jnp.bfloat16
HI = lax.Precision.HIGHEST
NEG = -1e30


def mm(a, b):
    return jnp.dot(a, b, preferred_element_type=F32)


def mm_t(a, b):
    return lax.dot_general(a, b, (((1,), (1,)), ((), ())), preferred_element_type=F32)


def softplus(v):
    return jnp.maximum(v, 0.0) + jnp.log1p(jnp.exp(-jnp.abs(v)))


def sigmoid(v):
    return 1.0 / (1.0 + jnp.exp(-v))


def tri_lower():
    rows = lax.broadcasted_iota(jnp.int32, (Q, Q), 0)
    cols = lax.broadcasted_iota(jnp.int32, (Q, Q), 1)
    return rows >= cols


def spread(table, lane):
    return jnp.broadcast_to(table[:, lane : lane + 1], (Q, LANES))


def fill_tables(dt, logs, dt_tab, log_tab, log_rows, low, groups, per):
    log_rows[...] = jnp.transpose(logs)
    for g in range(groups):
        shift = (LANES - (low + g) * per) % LANES
        dt_tab[g] = pltpu.roll(dt, shift, 1) if shift else dt
        log_tab[g] = pltpu.roll(logs, shift, 1) if shift else logs


def scan_forward(proj_ref, cw_ref, cb_ref, vec_ref, skip_ref, out_ref, sum_ref, start_ref,
                 shifted, act, state, dt_tab, log_tab, log_rows, *, inner, nstate, groups, per):
    first = pl.program_id(0) == 0
    conv = inner + 2 * nstate

    @pl.when(first)
    def _():
        shifted[0:8, :] = jnp.zeros((8, conv), F32)
        state[...] = jnp.zeros_like(state)

    shifted[8 : 8 + Q, :] = proj_ref[:, 0:conv]
    wide = 256
    for low in range(0, conv, wide):
        part = pl.ds(low, wide)
        total = cb_ref[0:1, part] + cw_ref[0:1, part] * shifted[5 : 5 + Q, part]
        for k in range(1, 4):
            total = total + cw_ref[k : k + 1, part] * shifted[5 + k : 5 + k + Q, part]
        sum_ref[:, part] = total
        act[:, part] = total * sigmoid(total)
    shifted[0:8, :] = shifted[Q : Q + 8, :]

    dt = softplus(proj_ref[:, conv : conv + LANES] + vec_ref[0:1, :])
    causal = tri_lower()
    logs = jnp.dot(causal.astype(F32), dt * vec_ref[1:2, :], precision=HI, preferred_element_type=F32)
    fill_tables(dt, logs, dt_tab, log_tab, log_rows, 0, groups, per)
    keys_b = act[:, inner : inner + nstate]
    keys_c = act[:, inner + nstate : conv].astype(BF16)
    b_cols = jnp.transpose(keys_b).astype(BF16)
    cross = mm(keys_c, b_cols)
    start_ref[...] = state[...].astype(BF16)
    span = per * HEAD
    low_half = lax.broadcasted_iota(jnp.int32, (Q, LANES), 1) < HEAD

    def group(g, carry):
        base = pl.multiple_of(g * span, span)
        dts, lgs = dt_tab[g], log_tab[g]
        carried = mm(keys_c, start_ref[:, pl.ds(base, span)])
        tails_all = []
        lasts = []
        for j in range(per // 2):
            cols = pl.ds(pl.multiple_of(base + j * LANES, LANES), LANES)
            h = g * per + 2 * j
            col0, col1 = spread(lgs, 2 * j), spread(lgs, 2 * j + 1)
            row0, row1 = log_rows[pl.ds(h, 1), :], log_rows[pl.ds(h + 1, 1), :]
            values = act[:, cols]
            stepped = (values * jnp.where(low_half, spread(dts, 2 * j), spread(dts, 2 * j + 1)))
            stepped_b = stepped.astype(BF16)
            mix0 = (jnp.exp(jnp.where(causal, col0 - row0, NEG)) * cross).astype(BF16)
            mix1 = (jnp.exp(jnp.where(causal, col1 - row1, NEG)) * cross).astype(BF16)
            zero = jnp.zeros_like(stepped_b)
            pairs = jnp.concatenate(
                [jnp.where(low_half, stepped_b, zero), jnp.where(low_half, zero, stepped_b)], axis=0)
            local = mm(jnp.concatenate([mix0, mix1], axis=1), pairs)
            both = jnp.where(low_half, col0, col1)
            last = both[Q - 1 : Q, :]
            out = local + carried[:, j * LANES : (j + 1) * LANES] * jnp.exp(both)
            out_ref[:, cols] = out + skip_ref[0:1, cols] * values
            tails_all.append((stepped * jnp.exp(last - both)).astype(BF16))
            lasts.append(jnp.exp(last))
        fresh = mm(b_cols, jnp.concatenate(tails_all, axis=1))
        cols = pl.ds(base, span)
        state[:, cols] = state[:, cols] * jnp.concatenate(lasts, axis=1) + fresh
        return carry

    lax.fori_loop(0, groups, group, 0)


def run_scan_forward(proj, cw, cb, vec, skip_cols, inner, nstate, groups, per):
    length = proj.shape[0]
    blocks = length // Q
    conv = inner + 2 * nstate
    whole = lambda shape: pl.BlockSpec(shape, lambda i: (0, 0))
    rows = lambda width: pl.BlockSpec((Q, width), lambda i: (i, 0))
    return pl.pallas_call(
        functools.partial(scan_forward, inner=inner, nstate=nstate, groups=groups, per=per),
        grid=(blocks,),
        in_specs=[rows(proj.shape[1]), whole(cw.shape), whole(cb.shape), whole(vec.shape), whole(skip_cols.shape)],
        out_specs=[rows(inner), rows(conv), pl.BlockSpec((nstate, inner), lambda i: (i, 0))],
        out_shape=[
            jax.ShapeDtypeStruct((length, inner), F32),
            jax.ShapeDtypeStruct((length, conv), F32),
            jax.ShapeDtypeStruct((blocks * nstate, inner), BF16),
        ],
        scratch_shapes=[
            pltpu.VMEM((Q + 8, conv), F32),
            pltpu.VMEM((Q, conv), F32),
            pltpu.VMEM((nstate, inner), F32),
            pltpu.VMEM((groups, Q, LANES), F32),
            pltpu.VMEM((groups, Q, LANES), F32),
            pltpu.VMEM((LANES, Q), F32),
        ],
        compiler_params=pltpu.CompilerParams(vmem_limit_bytes=60 << 20),
        cost_estimate=pl.CostEstimate(flops=12_000_000_000, bytes_accessed=60_000_000, transcendentals=20_000_000),
        name="scan_forward",
    )(proj, cw, cb, vec, skip_cols)


def piece_copies(place_ref, pieces, refs, target, sems):
    copies = []
    for index, (start, half, size, lane) in enumerate(pieces):
        rows, cols = refs[index].shape
        if half is not None:
            start = pl.multiple_of(start + jnp.bitwise_xor(place_ref[1], half) * size, 16)
        window = target.at[pl.ds(start, rows), pl.ds(lane, cols)]
        copies.append(pltpu.make_async_copy(refs[index], window, sems.at[index]))
    return copies


def load_pieces(*args):
    for copy in piece_copies(*args):
        copy.start()


def wait_pieces(*args):
    for copy in piece_copies(*args):
        copy.wait()


def columns_of(place_ref, position, order, width):
    return pl.ds(pl.multiple_of(jnp.bitwise_xor(place_ref[0], order[position]) * width, LANES), width)


def project_in(place_ref, tok_ref, gain_ref, *rest, pieces, order):
    refs, (normed_ref, proj_ref, weight, sems) = rest[: len(pieces)], rest[len(pieces) :]
    first = pl.program_id(0) == 0

    @pl.when(first)
    def _():
        load_pieces(place_ref, pieces, refs, weight, sems)

    width = tok_ref.shape[1] // len(order)
    tok = tok_ref[...].astype(F32)
    scale = lax.rsqrt(jnp.mean(tok * tok, axis=1, keepdims=True) + EPS)
    for position in range(len(order)):
        cols = columns_of(place_ref, position, order, width)
        value = tok_ref[:, cols].astype(F32) * scale * gain_ref[0:1, cols]
        normed_ref[:, position * width : (position + 1) * width] = value.astype(BF16)

    @pl.when(first)
    def _():
        wait_pieces(place_ref, pieces, refs, weight, sems)

    total = proj_ref.shape[1]
    step = 384
    for low in range(0, total, step):
        proj_ref[:, low : low + step] = mm_t(normed_ref[...], weight[low : low + step, :])


def grid_of(grid, in_specs, out_specs, scratch):
    return pltpu.PrefetchScalarGridSpec(
        num_scalar_prefetch=1, grid=grid, in_specs=in_specs, out_specs=out_specs, scratch_shapes=scratch)


def anywhere(count):
    return [pl.BlockSpec(memory_space=pl.ANY)] * count


def row_block(block, width):
    return pl.BlockSpec((block, width), lambda i, s: (i, 0))


def fixed(shape):
    return pl.BlockSpec(shape, lambda i, s: (0,) * len(shape))


def run_project_in(place, tok, gain, weight, total, order, block=256):
    pieces, arrays = weight
    length, width = tok.shape
    return pl.pallas_call(
        functools.partial(project_in, pieces=pieces, order=order),
        grid_spec=grid_of(
            (length // block,),
            [row_block(block, width), fixed(gain.shape)] + anywhere(len(pieces)),
            [row_block(block, width), row_block(block, total)],
            [pltpu.VMEM((total, width), BF16), pltpu.SemaphoreType.DMA((len(pieces),))],
        ),
        out_shape=[jax.ShapeDtypeStruct((length, width), BF16), jax.ShapeDtypeStruct((length, total), F32)],
        compiler_params=pltpu.CompilerParams(vmem_limit_bytes=50 << 20),
        cost_estimate=pl.CostEstimate(flops=20_000_000_000, bytes_accessed=30_000_000, transcendentals=1000),
        name="project_in",
    )(place, tok, gain, *arrays)


def gating(place_ref, normed_ref, cot_ref, scan_ref, gain_ref, *rest, wg_pieces, ow_pieces, order):
    n_g, n_o = len(wg_pieces), len(ow_pieces)
    wg_refs, ow_refs = rest[:n_g], rest[n_g : n_g + n_o]
    (mixed_ref, dscan_ref, dgate_ref, dgain_ref, wg, ow, gate_s, gated_s, scaled_s,
     g_sems, o_sems) = rest[n_g + n_o :]
    inner = wg.shape[0]
    parts = len(order)
    width = inner // parts
    first = pl.program_id(0) == 0

    @pl.when(first)
    def _():
        load_pieces(place_ref, wg_pieces, wg_refs, wg, g_sems)
        load_pieces(place_ref, ow_pieces, ow_refs, ow, o_sems)
        dgain_ref[...] = jnp.zeros_like(dgain_ref)
        wait_pieces(place_ref, wg_pieces, wg_refs, wg, g_sems)

    def fold(v):
        total = v[:, 0:LANES]
        for low in range(LANES, v.shape[1], LANES):
            total = total + v[:, low : low + LANES]
        return total

    power = None
    for p in range(parts):
        cols = slice(p * width, (p + 1) * width)
        gate = mm_t(normed_ref[...], wg[cols, :])
        gated = scan_ref[:, cols] * (gate * sigmoid(gate))
        gate_s[:, cols] = gate
        gated_s[:, cols] = gated
        term = fold(gated * gated)
        power = term if power is None else power + term
    scale = lax.rsqrt(jnp.sum(power, axis=1, keepdims=True) / inner + EPS)

    @pl.when(first)
    def _():
        wait_pieces(place_ref, ow_pieces, ow_refs, ow, o_sems)

    match = None
    for p in range(parts):
        true = columns_of(place_ref, p, order, width)
        rows = slice(p * width, (p + 1) * width)
        grad = mm_t(cot_ref[...], ow[rows, :])
        gated = gated_s[:, true]
        gain = gain_ref[0:1, true]
        unit = gated * scale
        mixed_ref[:, rows] = (unit * gain).astype(BF16)
        dgain_ref[0:1, true] += jnp.sum(grad * unit, axis=0, keepdims=True)
        scaled = grad * gain
        scaled_s[:, true] = scaled
        term = fold(scaled * gated)
        match = term if match is None else match + term
    pull = jnp.sum(match, axis=1, keepdims=True) * (scale * scale) / inner
    for p in range(parts):
        cols = slice(p * width, (p + 1) * width)
        gate = gate_s[:, cols]
        sig = sigmoid(gate)
        silu = gate * sig
        dgated = scale * (scaled_s[:, cols] - gated_s[:, cols] * pull)
        dscan_ref[:, cols] = dgated * silu
        dgate_ref[:, cols] = (dgated * scan_ref[:, cols] * (sig + silu * (1.0 - sig))).astype(BF16)


def run_gating(place, normed, gate_weight, out_weight, cot, scan_out, gain, order, block=256):
    wg_pieces, wg_arrays = gate_weight
    ow_pieces, ow_arrays = out_weight
    length, width = normed.shape
    inner = scan_out.shape[1]
    return pl.pallas_call(
        functools.partial(gating, wg_pieces=wg_pieces, ow_pieces=ow_pieces, order=order),
        grid_spec=grid_of(
            (length // block,),
            [row_block(block, width), row_block(block, width), row_block(block, inner), fixed((1, inner))]
            + anywhere(len(wg_pieces) + len(ow_pieces)),
            [row_block(block, inner), row_block(block, inner), row_block(block, inner), fixed((1, inner))],
            [pltpu.VMEM((inner, width), BF16), pltpu.VMEM((inner, width), BF16)]
            + [pltpu.VMEM((block, inner), F32)] * 3
            + [pltpu.SemaphoreType.DMA((len(wg_pieces),)), pltpu.SemaphoreType.DMA((len(ow_pieces),))],
        ),
        out_shape=[
            jax.ShapeDtypeStruct((length, inner), BF16),
            jax.ShapeDtypeStruct((length, inner), F32),
            jax.ShapeDtypeStruct((length, inner), BF16),
            jax.ShapeDtypeStruct((1, inner), F32),
        ],
        compiler_params=pltpu.CompilerParams(vmem_limit_bytes=62 << 20),
        cost_estimate=pl.CostEstimate(flops=40_000_000_000, bytes_accessed=70_000_000, transcendentals=10_000_000),
        name="gating",
    )(place, normed, cot, scan_out, gain, *wg_arrays, *ow_arrays)


def gate_back(place_ref, dgate_ref, *rest, pieces):
    refs, (grad_ref, weight, sems) = rest[: len(pieces)], rest[len(pieces) :]

    @pl.when(pl.program_id(0) == 0)
    def _():
        load_pieces(place_ref, pieces, refs, weight, sems)
        wait_pieces(place_ref, pieces, refs, weight, sems)

    step = 384
    for low in range(0, grad_ref.shape[1], step):
        grad_ref[:, low : low + step] = mm(dgate_ref[...], weight[:, low : low + step])


def run_gate_back(place, dgate, model, weight, block=256):
    pieces, arrays = weight
    length, inner = dgate.shape
    return pl.pallas_call(
        functools.partial(gate_back, pieces=pieces),
        grid_spec=grid_of(
            (length // block,),
            [row_block(block, inner)] + anywhere(len(pieces)),
            row_block(block, model),
            [pltpu.VMEM((inner, model), BF16), pltpu.SemaphoreType.DMA((len(pieces),))],
        ),
        out_shape=jax.ShapeDtypeStruct((length, model), F32),
        compiler_params=pltpu.CompilerParams(vmem_limit_bytes=40 << 20),
        cost_estimate=pl.CostEstimate(flops=16_000_000_000, bytes_accessed=22_000_000, transcendentals=0),
        name="gate_back",
    )(place, dgate, *arrays)


def input_back(place_ref, part_ref, tok_ref, cot_ref, gain_ref, *rest, count, pieces, order):
    dproj_refs, rest = rest[:count], rest[count:]
    refs, (grad_ref, dgain_ref, weight, dn, sems) = rest[: len(pieces)], rest[len(pieces) :]
    first = pl.program_id(0) == 0

    @pl.when(first)
    def _():
        load_pieces(place_ref, pieces, refs, weight, sems)
        dgain_ref[...] = jnp.zeros_like(dgain_ref)
        wait_pieces(place_ref, pieces, refs, weight, sems)

    model = tok_ref.shape[1]
    width = model // len(order)
    tok = tok_ref[...].astype(F32)
    scale = lax.rsqrt(jnp.mean(tok * tok, axis=1, keepdims=True) + EPS)
    match = None
    for position in range(len(order)):
        spot = slice(position * width, (position + 1) * width)
        true = columns_of(place_ref, position, order, width)
        grad, low = part_ref[:, spot], 0
        for ref in dproj_refs:
            grad = grad + mm(ref[...], weight[low : low + ref.shape[1], spot])
            low += ref.shape[1]
        value = tok_ref[:, true].astype(F32)
        dgain_ref[0:1, true] += jnp.sum(grad * (value * scale), axis=0, keepdims=True)
        grad = grad * gain_ref[0:1, true]
        dn[:, spot] = grad
        term = jnp.sum(grad * value, axis=1, keepdims=True)
        match = term if match is None else match + term
    pull = match * (scale * scale * scale) / model
    for position in range(len(order)):
        spot = slice(position * width, (position + 1) * width)
        true = columns_of(place_ref, position, order, width)
        value = tok_ref[:, true].astype(F32)
        grad_ref[:, true] = cot_ref[:, true].astype(F32) + (scale * dn[:, spot] - value * pull)


def run_input_back(place, part, dprojs, tok, cot, gain, weight, order, block=256):
    pieces, arrays = weight
    length, model = tok.shape
    widths = [d.shape[1] for d in dprojs]
    return pl.pallas_call(
        functools.partial(input_back, count=len(dprojs), pieces=pieces, order=order),
        grid_spec=grid_of(
            (length // block,),
            [row_block(block, model), row_block(block, model), row_block(block, model), fixed((1, model))]
            + [row_block(block, w) for w in widths] + anywhere(len(pieces)),
            [row_block(block, model), fixed((1, model))],
            [pltpu.VMEM((sum(widths), model), BF16), pltpu.VMEM((block, model), F32),
             pltpu.SemaphoreType.DMA((len(pieces),))],
        ),
        out_shape=[jax.ShapeDtypeStruct((length, model), F32), jax.ShapeDtypeStruct((1, model), F32)],
        compiler_params=pltpu.CompilerParams(vmem_limit_bytes=50 << 20),
        cost_estimate=pl.CostEstimate(flops=22_000_000_000, bytes_accessed=46_000_000, transcendentals=1000),
        name="input_back",
    )(place, part, tok, cot, gain, *dprojs, *arrays)


def project_out(place_ref, mixed_ref, tok_ref, *rest, pieces):
    refs, (out_ref, weight, sems) = rest[: len(pieces)], rest[len(pieces) :]

    @pl.when(pl.program_id(0) == 0)
    def _():
        load_pieces(place_ref, pieces, refs, weight, sems)
        wait_pieces(place_ref, pieces, refs, weight, sems)

    step = 384
    for low in range(0, out_ref.shape[1], step):
        cols = slice(low, low + step)
        out_ref[:, cols] = (tok_ref[:, cols].astype(F32) + mm(mixed_ref[...], weight[:, cols])).astype(BF16)


def run_project_out(place, mixed, tok, weight, block=256):
    pieces, arrays = weight
    length, model = tok.shape
    inner = mixed.shape[1]
    return pl.pallas_call(
        functools.partial(project_out, pieces=pieces),
        grid_spec=grid_of(
            (length // block,),
            [row_block(block, inner), row_block(block, model)] + anywhere(len(pieces)),
            row_block(block, model),
            [pltpu.VMEM((inner, model), BF16), pltpu.SemaphoreType.DMA((len(pieces),))],
        ),
        out_shape=jax.ShapeDtypeStruct((length, model), BF16),
        compiler_params=pltpu.CompilerParams(vmem_limit_bytes=40 << 20),
        cost_estimate=pl.CostEstimate(flops=14_000_000_000, bytes_accessed=20_000_000, transcendentals=0),
        name="project_out",
    )(place, mixed, tok, *arrays)


def scan_backward(proj_ref, tail_ref, sum_ref, keys_ref, out_ref, dout_ref, start_ref, cw_ref, cwk_ref, vec_ref,
                  skip_ref, pick_ref, *rest, nstate, low, groups, per, begin, last):
    if not begin:
        old_cross_ref, old_keys_ref, old_raw_ref = rest[:3]
        rest = rest[3:]
    dproj_ref, dcw_ref, dcb_ref, dskip_ref, dvec_ref = rest[:5]
    rest = rest[5:]
    if not last:
        cross_ref, keys_ref_out, raw_ref = rest[:3]
        rest = rest[3:]
    dsum, dstate, edge, logs_v, tails_v, steps_v, dt_tab, log_tab, log_rows, dcross, dkeys = rest
    first = pl.program_id(0) == 0
    span_all = groups * per * HEAD
    conv = dsum.shape[1]

    @pl.when(first)
    def _():
        dsum[Q : Q + 8, :] = jnp.zeros((8, conv), F32)
        dstate[...] = jnp.zeros_like(dstate)
        edge[...] = jnp.zeros_like(edge)
        dcw_ref[...] = jnp.zeros_like(dcw_ref)
        dcb_ref[...] = jnp.zeros_like(dcb_ref)
        dskip_ref[...] = jnp.zeros_like(dskip_ref)
        dvec_ref[...] = jnp.zeros_like(dvec_ref)

    raw = tail_ref[:, 2 * nstate : 2 * nstate + LANES] + vec_ref[0:1, :]
    dt = softplus(raw)
    lower = tri_lower()
    rate = vec_ref[1:2, :]
    logs = jnp.dot(lower.astype(F32), dt * rate, precision=HI, preferred_element_type=F32)
    fill_tables(dt, logs, dt_tab, log_tab, log_rows, low, groups, per)
    sum_b = keys_ref[:, 0:nstate]
    sum_c = keys_ref[:, nstate : 2 * nstate]
    sig_b, sig_c = sigmoid(sum_b), sigmoid(sum_c)
    keys_b32, keys_c32 = sum_b * sig_b, sum_c * sig_c
    keys_b, keys_c = keys_b32.astype(BF16), keys_c32.astype(BF16)
    c_cols = jnp.transpose(keys_c32).astype(BF16)
    cross = mm(keys_b, c_cols)
    span = per * HEAD
    low_half = lax.broadcasted_iota(jnp.int32, (Q, LANES), 1) < HEAD
    upper = lax.broadcasted_iota(jnp.int32, (Q, Q), 0) <= lax.broadcasted_iota(jnp.int32, (Q, Q), 1)
    if not begin:
        dcross[...] = old_cross_ref[...]
        dkeys[...] = old_keys_ref[...]
    else:
        dcross[...] = jnp.zeros_like(dcross)
        dkeys[...] = jnp.zeros_like(dkeys)

    def group(g, carry):
        base = pl.multiple_of(g * span, span)
        whole = pl.ds(base, span)
        dts, lgs = dt_tab[g], log_tab[g]
        dstate_b = dstate[:, whole].astype(BF16)
        from_state = mm(keys_b, dstate_b)
        tails_all, outs_all, lasts = [], [], []
        dcr = None
        for j in range(per // 2):
            cols = pl.ds(pl.multiple_of(base + j * LANES, LANES), LANES)
            h = (low + g) * per + 2 * j
            col0, col1 = spread(lgs, 2 * j), spread(lgs, 2 * j + 1)
            row0, row1 = log_rows[pl.ds(h, 1), :], log_rows[pl.ds(h + 1, 1), :]
            total = sum_ref[:, cols]
            sig = sigmoid(total)
            values = total * sig
            step = jnp.where(low_half, spread(dts, 2 * j), spread(dts, 2 * j + 1))
            stepped = values * step
            stepped_b = stepped.astype(BF16)
            dout = dout_ref[:, cols]
            dout_b = dout.astype(BF16)
            decay0 = jnp.exp(jnp.where(upper, row0 - col0, NEG))
            decay1 = jnp.exp(jnp.where(upper, row1 - col1, NEG))
            mix = jnp.concatenate([(decay0 * cross).astype(BF16), (decay1 * cross).astype(BF16)], axis=1)
            zero = jnp.zeros_like(dout_b)
            douts = jnp.concatenate(
                [jnp.where(low_half, dout_b, zero), jnp.where(low_half, zero, dout_b)], axis=0)
            local = mm(mix, douts)
            dmix = mm_t(stepped_b, douts)
            term = dmix[:, 0:Q] * decay0 + dmix[:, Q : 2 * Q] * decay1
            dcr = term if dcr is None else dcr + term
            both = jnp.where(low_half, col0, col1)
            last = both[Q - 1 : Q, :]
            tail = jnp.exp(last - both)
            passed = from_state[:, j * LANES : (j + 1) * LANES] * tail
            dstepped = local + passed
            skip = skip_ref[0:1, cols]
            scan = out_ref[:, cols] - skip * values
            logs_v[:, cols] = dout_b.astype(F32) * scan - stepped_b.astype(F32) * local
            tails_v[:, cols] = stepped * passed
            steps_v[:, cols] = dstepped * values
            dvalues = dstepped * step + dout * skip
            dskip_ref[0:1, cols] += jnp.sum(dout * values, axis=0, keepdims=True)
            dsum[0:Q, cols] = dvalues * (sig + values * (1.0 - sig))
            tails_all.append((stepped * tail).astype(BF16))
            outs_all.append((dout * jnp.exp(both)).astype(BF16))
            lasts.append(jnp.exp(last))
        dcross[...] += dcr
        outs = jnp.concatenate(outs_all, axis=1)
        starts = start_ref[:, whole]
        dkeys[:, nstate : 2 * nstate] += mm_t(outs, starts)
        dkeys[:, 0:nstate] += mm_t(jnp.concatenate(tails_all, axis=1), dstate_b)
        kept = dstate[:, whole] * jnp.concatenate(lasts, axis=1)
        edge[0:1, whole] = jnp.sum(kept * starts.astype(F32), axis=0, keepdims=True)
        dstate[:, whole] = kept + mm(c_cols, outs)
        return carry

    lax.fori_loop(0, groups, group, 0)

    if last:
        dcr = dcross[...]
        exact = lambda u, v: jnp.dot(u, v, precision=HI, preferred_element_type=F32)
        d_b = dkeys[:, 0:nstate] + exact(dcr, keys_c32)
        d_c = dkeys[:, nstate : 2 * nstate] + exact(jnp.transpose(dcr), keys_b32)
        dsum[0:Q, span_all : span_all + nstate] = d_b * (sig_b + keys_b32 * (1.0 - sig_b))
        dsum[0:Q, span_all + nstate : conv] = d_c * (sig_c + keys_c32 * (1.0 - sig_c))
    else:
        cross_ref[...] = dcross[...]
        keys_ref_out[...] = dkeys[...]

    def reduce_heads(v):
        high = v.astype(BF16)
        low = (v - high.astype(F32)).astype(BF16)
        return mm(high, pick_ref[...]) + mm(low, pick_ref[...])

    dlogs = reduce_heads(logs_v[...])
    dtails = reduce_heads(tails_v[...])
    dlogit = (
        jnp.dot(upper.astype(F32), dlogs, precision=HI, preferred_element_type=F32)
        + jnp.dot(1.0 - upper.astype(F32), dtails, precision=HI, preferred_element_type=F32)
        + reduce_heads(edge[...])[0:1, :]
    )
    dstep = reduce_heads(steps_v[...]) + dlogit * rate
    draw = dstep * sigmoid(raw)
    dvec_ref[0:1, :] += jnp.sum(draw, axis=0, keepdims=True)
    dvec_ref[1:2, :] += jnp.sum(dlogit * dt * rate, axis=0, keepdims=True)
    if last:
        dproj_ref[:, conv : conv + LANES] = (draw + old_raw_ref[...]).astype(BF16)
    elif begin:
        raw_ref[...] = draw
    else:
        raw_ref[...] = draw + old_raw_ref[...]

    wide = 256
    for start in range(0, conv, wide):
        part = pl.ds(start, wide)
        if start < span_all:
            source, taps_ref, local = proj_ref, cw_ref, part
        else:
            source, taps_ref, local = tail_ref, cwk_ref, pl.ds(start - span_all, wide)
        taken = source[:, local]
        total = None
        for k in range(4):
            moved = dsum[3 - k : 3 - k + Q, part]
            dcw_ref[k : k + 1, part] += jnp.sum(taken * moved, axis=0, keepdims=True)
            term = taps_ref[k : k + 1, local] * moved
            total = term if total is None else total + term
            if k == 3:
                dcb_ref[0:1, part] += jnp.sum(moved, axis=0, keepdims=True)
        dproj_ref[:, part] = total.astype(BF16)
    dsum[Q : Q + 8, :] = dsum[0:8, :]


def run_scan_backward(proj, sums, scan_out, dscan, starts, cw, vec, skip_cols, pick, inner, nstate, low, groups, per,
                      previous, last):
    length = proj.shape[0]
    blocks = length // Q
    span = groups * per * HEAD
    begin = previous is None
    conv = span + (2 * nstate if last else 0)
    where = low * per * HEAD // span
    whole = lambda shape: pl.BlockSpec(shape, lambda i: (0, 0))
    rows = lambda width, col=0: pl.BlockSpec((Q, width), lambda i: (blocks - 1 - i, col))
    part = lambda height: pl.BlockSpec((height, span), lambda i: (0, where))
    tail = 2 * nstate + LANES
    out_specs = [rows(conv + (LANES if last else 0)), whole((4, conv)), whole((1, conv)), whole((1, span)),
                 whole((8, LANES))]
    out_shape = [
        jax.ShapeDtypeStruct((length, conv + (LANES if last else 0)), BF16),
        jax.ShapeDtypeStruct((4, conv), F32),
        jax.ShapeDtypeStruct((1, conv), F32),
        jax.ShapeDtypeStruct((1, span), F32),
        jax.ShapeDtypeStruct((8, LANES), F32),
    ]
    carried = [rows(Q), rows(2 * nstate), rows(LANES)]
    if not last:
        out_specs += carried
        out_shape += [jax.ShapeDtypeStruct((length, w), F32) for w in (Q, 2 * nstate, LANES)]
    return pl.pallas_call(
        functools.partial(scan_backward, nstate=nstate, low=low, groups=groups, per=per, begin=begin, last=last),
        grid=(blocks,),
        in_specs=[
            rows(span, where), rows(tail, inner // tail), rows(span, where), rows(2 * nstate, inner // (2 * nstate)),
            rows(span, where), rows(span, where),
            pl.BlockSpec((nstate, span), lambda i: (blocks - 1 - i, where)),
            part(4), pl.BlockSpec((4, 2 * nstate), lambda i: (0, inner // (2 * nstate))),
            whole(vec.shape), part(1), pl.BlockSpec((span, LANES), lambda i: (where, 0)),
        ] + ([] if begin else carried),
        out_specs=out_specs,
        out_shape=out_shape,
        scratch_shapes=[
            pltpu.VMEM((Q + 8, conv), F32),
            pltpu.VMEM((nstate, span), F32),
            pltpu.VMEM((8, span), F32),
            pltpu.VMEM((Q, span), F32),
            pltpu.VMEM((Q, span), F32),
            pltpu.VMEM((Q, span), F32),
            pltpu.VMEM((groups, Q, LANES), F32),
            pltpu.VMEM((groups, Q, LANES), F32),
            pltpu.VMEM((LANES, Q), F32),
            pltpu.VMEM((Q, Q), F32),
            pltpu.VMEM((Q, 2 * nstate), F32),
        ],
        compiler_params=pltpu.CompilerParams(vmem_limit_bytes=50 << 20),
        cost_estimate=pl.CostEstimate(flops=40_000_000_000, bytes_accessed=40_000_000, transcendentals=15_000_000),
        name="scan_backward",
    )(proj, proj, sums, sums, scan_out, dscan, starts, cw, cw, vec, skip_cols, pick, *(previous or ()))


def bits_of(size):
    return [1 << b for b in range(size.bit_length() - 1)]


def swap(value, axis, bit, size):
    return lax.ppermute(value, axis, [(i, i ^ bit) for i in range(size)])


def after(value, *deps):
    return lax.optimization_barrier((value,) + deps)[0] if deps else value


def order_of(size):
    flipped = []
    for index in range(size):
        value = 0
        for low, high in zip(bits_of(size), reversed(bits_of(size))):
            value |= high if index & low else 0
        flipped.append(value)
    return flipped


class Gather:
    def __init__(self, shard, order, rep_index, groups, copies, lanes, chunks):
        self.order, self.groups, self.copies = order, groups, copies
        self.size = shard.shape
        self.lanes = lanes
        self.half = shard.shape[0] // 2
        self.rows = self.half // chunks
        self.shard = shard
        parity = rep_index & 1
        self.mine = [lax.dynamic_slice_in_dim(shard, parity * self.half + c * self.rows, self.rows, 0)
                     for c in range(chunks)]
        self.there, self.across = [None] * chunks, [None] * chunks
        self.own, self.early = None, []

    def far(self, chunk, *deps):
        value = after(self.mine[chunk], *deps)
        self.there[chunk] = swap(value, "shard", 2, self.groups)

    def whole(self, *deps):
        self.there = [swap(after(self.shard, *deps), "shard", 2, self.groups)]
        self.across = []

    def side(self, chunk):
        self.across[chunk] = swap(self.there[chunk], "rep", 1, self.copies)

    def core(self, value, *deps):
        return swap(after(value, *deps), "shard", 1, self.groups)

    def finish(self, *deps):
        own = self.own if self.own is not None else self.core(self.shard)
        have = {0: [(0, None, 0, self.shard)], 1: [(0, None, 0, own)]}
        if self.across:
            have[2] = [(c * self.rows, h, self.half, v) for h, vs in ((0, self.there), (1, self.across))
                       for c, v in enumerate(vs)]
        else:
            have[2] = [(0, None, 0, self.there[0])]
        have[3] = []
        for index, (row, half, size, value) in enumerate(have[2]):
            if index < len(self.early):
                partner = self.early[index]
            else:
                partner = self.core(value, *(deps if index == len(have[2]) - 1 else ()))
            have[3].append((row, half, size, partner))
        pieces, arrays = [], []
        for position, source in enumerate(self.order):
            for row, half, size, value in have[source]:
                if self.lanes:
                    pieces.append((row, half, size, position * self.size[1]))
                else:
                    pieces.append((row + position * self.size[0], half, size, 0))
                arrays.append(value)
        return tuple(pieces), tuple(arrays)


class Total:
    def __init__(self, kept, sent, axis, rep_index, groups, copies, narrow=False):
        self.axis, self.rep_index = axis, rep_index
        self.sizes = {"shard": groups, "rep": copies}
        self.stages = [("shard", index, 1) for index in range(len(bits_of(groups)))]
        count = len(bits_of(copies))
        over = [("rep", 0, 1)] + [("rep", index, min(2, count - index)) for index in range(1, count, 2)]
        self.stages += over
        self.back = list(reversed(over))
        if narrow:
            self.back = [(name, shift + bit, 1) for name, shift, width in self.back for bit in range(width)]
        self.value, self.out = kept, [sent]
        self.fly()

    @classmethod
    def join(cls, chains):
        first = chains[0]
        new = object.__new__(cls)
        new.axis, new.rep_index, new.sizes = first.axis, first.rep_index, first.sizes
        new.stages, new.back = first.stages, first.back
        new.value = jnp.concatenate([v.value for v in chains])
        new.coming = [jnp.concatenate(v) for v in zip(*(c.coming for c in chains))]
        return new

    def fly(self):
        name, shift, _ = self.stages[0]
        self.coming = [swap(v, name, (k + 1) << shift, self.sizes[name]) for k, v in enumerate(self.out)]

    def done(self):
        return not self.stages and not self.back

    def step(self, *deps):
        coming = [after(v, *deps) for v in self.coming]
        if not self.stages:
            return self.widen(coming)
        self.stages.pop(0)
        terms = [self.value] + coming
        if not self.stages:
            self.value = sum(v.astype(F32) for v in terms).astype(BF16)
            self.fly_back()
            return [self.value]
        name, shift, width = self.stages[0]
        parts = 1 << width
        axis = self.axis if name == "shard" else 0
        size = self.value.shape[axis] // parts
        mine = 0 if name == "shard" else (self.rep_index >> shift) & (parts - 1)
        cut = lambda start: sum(lax.dynamic_slice_in_dim(v, start, size, axis).astype(F32) for v in terms)
        self.out = [cut((mine ^ k) * size).astype(BF16) for k in range(1, parts)]
        self.value = cut(mine * size)
        self.fly()
        return self.out

    def fly_back(self):
        name, shift, width = self.back[0]
        self.coming = [swap(self.value, name, k << shift, self.sizes[name]) for k in range(1, 1 << width)]

    def widen(self, coming):
        name, shift, width = self.back.pop(0)
        parts = [self.value] + coming
        for bit in range(width):
            turn = ((self.rep_index >> (shift + bit)) & 1) != 0
            parts = [jnp.where(turn, parts[k ^ (1 << bit)], parts[k]) for k in range(len(parts))]
        if not self.back:
            self.value = [v.astype(F32) for v in parts]
            return self.value
        self.value = jnp.concatenate(parts)
        self.fly_back()
        return [self.value]


def outer(left, right):
    return lax.dot_general(left, right, (((0,), (0,)), ((), ())), preferred_element_type=F32).astype(BF16)


def on_device(groups, copies, tokens, norm_gain, in_weight, conv_weight, conv_bias, dt_bias, a_log, skip, gate_gain,
              out_weight, cotangent):
    if tokens.shape[0] != 1 or groups != 4:
        raise ValueError("unexpected sizes")
    order = order_of(groups)
    shard_index = lax.axis_index("shard")
    rep_index = lax.axis_index("rep")
    tok, cot = tokens[0], cotangent[0]
    inner = gate_gain.shape[0] * groups
    conv = conv_bias.shape[0] * groups
    heads = dt_bias.shape[0] * groups
    nstate = (conv - inner) // 2
    model = tok.shape[1]
    taps = conv_weight.shape[0]
    outputs_all = in_weight.shape[1]
    place = jnp.stack([shard_index, rep_index & 1]).astype(jnp.int32)

    turned = in_weight.T
    total = conv + LANES
    conv_part = jnp.pad(turned[inner:], ((0, total + inner - outputs_all), (0, 0)))
    make = lambda shard, lanes, chunks: Gather(shard, order, rep_index, groups, copies, lanes, chunks)
    wc = make(conv_part, True, 2)
    wg = make(turned[:inner], True, 1)
    ow = make(out_weight, False, 1)

    small = (norm_gain, conv_bias, dt_bias, a_log, skip, gate_gain, conv_weight)
    packed = jnp.concatenate([v.reshape(-1) for v in small])
    wc.far(0)
    wc.far(1)
    wc.side(0)
    wc.side(1)
    wc.own = wc.core(wc.shard)
    wc.early = [wc.core(wc.there[0])]
    wg.far(0, wc.there[1], wc.own, wc.early[0])
    ow.whole(wc.there[1], wc.own, wc.early[0])
    rows = [packed, swap(packed, "shard", 1, groups)]
    far = swap(packed, "shard", 2, groups)
    rows += [far, swap(far, "shard", 1, groups)]
    for bit in bits_of(groups):
        turn = (shard_index & bit) != 0
        rows = [jnp.where(turn, rows[j ^ bit], rows[j]) for j in range(groups)]
    everyone = jnp.stack(rows).astype(F32)
    parts, low = [], 0
    for v in small:
        parts.append(everyone[:, low : low + v.size])
        low += v.size
    gain, cb, db, al, sk, gg = (v.reshape(-1) for v in parts[:6])
    cw = parts[6].reshape(groups, taps, -1).transpose(1, 0, 2).reshape(taps, conv)
    gain, cb, gg = gain[None], cb[None], gg[None]
    vec = jnp.pad(jnp.stack([db, -jnp.exp(al)]), ((0, 6), (0, LANES - heads)))
    skip_cols = jnp.repeat(sk, inner // heads)[None]
    pick = (jnp.arange(inner)[:, None] // (inner // heads) == jnp.arange(LANES)[None]).astype(BF16)

    wc = wc.finish(gain, cb, gg, cw, vec, skip_cols, pick)
    normed, proj = run_project_in(place, tok, gain, wc, total, order)
    wg.there[0] = after(wg.there[0], normed)
    wg.side(0)
    proj = after(proj, wg.there[0])
    per = 8
    scan_out, sums, starts = run_scan_forward(proj, cw, cb, vec, skip_cols, inner, nstate, heads // per, per)
    wg, ow = wg.finish(scan_out), ow.finish(scan_out)
    mixed, dscan, dgate, dgg = run_gating(place, normed, wg, ow, cot, scan_out, gg, order)

    chain = lambda kept, sent, axis, *way: Total(kept, sent, axis, rep_index, groups, copies, *way)
    half = inner // 2
    out_sent = outer(mixed[:, half:], cot)
    o = chain(outer(mixed[:, :half], cot), out_sent, 0, True)
    half = model // 2
    left, right = normed[:, :half], normed[:, half:]
    gate_sent = outer(dgate, right)
    marks = o.step(gate_sent)
    g = chain(outer(after(dgate, *marks), left), gate_sent, 1)
    marks = marks + g.step(g.value)

    blocks = heads // per
    cuts = [blocks * v // 3 for v in range(4)]
    chains, grads, carried = [o, g], [], None
    for index in range(3):
        low, high = cuts[index], cuts[index + 1]
        found = run_scan_backward(
            proj, sums, scan_out, after(dscan, *marks), starts, cw, vec, skip_cols, pick, inner, nstate, low,
            high - low, per, carried, index == 2)
        grads.append(found[:5])
        carried = tuple(found[5:])
        dproj, marks = found[0], []
        if index == 1:
            marks = o.step(dproj)
        if index == 2:
            marks = ab.coming + g.step(dproj)
            marks = marks + o.step(dproj, *marks)
        dproj = after(dproj, *marks)
        sent = outer(dproj, right)
        kept = outer(dproj, left)
        new = chain(kept, sent, 1)
        chains.append(new)
        if index == 0:
            marks = marks + new.coming + o.step(kept)
        if index == 1:
            ab = Total.join(chains[2:])
            marks = marks + ab.step(kept)
            marks = marks + g.step(kept, *marks)
        if index == 2:
            marks = marks + new.step(kept)

    part = run_gate_back(place, after(dgate, *marks), model, wg)
    abc = Total.join([ab, chains[4]])
    marks = g.step(part)
    marks = marks + abc.step(part, *marks)
    marks = marks + o.step(part, *marks)
    input_grad, dgain = run_input_back(place, after(part, *marks), [v[0] for v in grads], tok, cot, gain, wc, order)

    dcw = jnp.concatenate([v[1] for v in grads], axis=1)
    dcb = jnp.concatenate([v[2][0] for v in grads])
    dskip = jnp.concatenate([v[3][0] for v in grads]).reshape(heads, -1).sum(1)
    dvec = sum(v[4] for v in grads)
    pieces = (dcb, dvec[0, :heads], dvec[1, :heads], dskip, dgg[0])
    flat = jnp.concatenate([v.reshape(groups, -1) for v in pieces]
                           + [dcw.reshape(taps, groups, -1).transpose(1, 0, 2).reshape(groups, -1)], axis=1)
    flat = jnp.concatenate([dgain[0].reshape(groups, -1), flat], axis=1)
    marks = abc.step(dgain, *g.coming, *o.coming)
    marks = marks + g.step(*marks)
    marks = marks + o.step(*marks)
    output = run_project_out(place, after(mixed, *marks), tok, ow)
    marks = abc.step(output, *g.coming, *o.coming)
    flat = after(flat, output, *marks)
    for axis, size in (("shard", groups), ("rep", copies)):
        for bit in bits_of(size):
            flat = flat + swap(flat, axis, bit, size)
    for old in (g, o, abc):
        while not old.done():
            old.step()

    in_total = jnp.concatenate(g.value + abc.value)[:outputs_all].T
    out_total = jnp.concatenate(o.value)

    own = lax.dynamic_slice_in_dim(flat, shard_index, 1, 0)[0]
    shares, low = [], 0
    for v in small:
        shares.append(own[low : low + v.size].reshape(v.shape))
        low += v.size
    d_gain, d_cb, d_db, d_al, d_sk, d_gg, d_cw = shares
    return (output[None], input_grad[None], d_gain, in_total, d_cw, d_cb, d_db, d_al, d_sk, d_gg, out_total)


def solution(mesh):
    whole = P(("shard", "rep"), None, None)
    row, matrix, cols = P("shard"), P("shard", None), P(None, "shard")
    return jax.shard_map(
        functools.partial(on_device, mesh.shape["shard"], mesh.shape["rep"]),
        mesh=mesh,
        in_specs=(whole, row, matrix, cols, row, row, row, row, row, matrix, whole),
        out_specs=(whole, whole, row, matrix, cols, row, row, row, row, row, matrix),
        check_vma=False,
    )
```

```python
import functools

import jax
import jax.numpy as jnp
from jax import lax
from jax.experimental import pallas as pl
from jax.experimental.pallas import tpu as pltpu
from jax.sharding import PartitionSpec as P

Q = 128
LANES = 128
HEAD = 64
EPS = 1e-05
F32 = jnp.float32
BF16 = jnp.bfloat16
HI = lax.Precision.HIGHEST
NEG = -1e30


def mm(a, b):
    return jnp.dot(a, b, preferred_element_type=F32)


def mm_t(a, b):
    return lax.dot_general(a, b, (((1,), (1,)), ((), ())), preferred_element_type=F32)


def softplus(v):
    return jnp.maximum(v, 0.0) + jnp.log1p(jnp.exp(-jnp.abs(v)))


def sigmoid(v):
    return 1.0 / (1.0 + jnp.exp(-v))


def tri_lower():
    rows = lax.broadcasted_iota(jnp.int32, (Q, Q), 0)
    cols = lax.broadcasted_iota(jnp.int32, (Q, Q), 1)
    return rows >= cols


def spread(table, lane):
    return jnp.broadcast_to(table[:, lane : lane + 1], (Q, LANES))


def fill_tables(dt, logs, dt_tab, log_tab, log_rows, low, groups, per):
    log_rows[...] = jnp.transpose(logs)
    for g in range(groups):
        shift = (LANES - (low + g) * per) % LANES
        dt_tab[g] = pltpu.roll(dt, shift, 1) if shift else dt
        log_tab[g] = pltpu.roll(logs, shift, 1) if shift else logs


def scan_forward(proj_ref, cw_ref, cb_ref, vec_ref, skip_ref, out_ref, sum_ref, start_ref,
                 shifted, act, state, dt_tab, log_tab, log_rows, *, inner, nstate, groups, per):
    first = pl.program_id(0) == 0
    conv = inner + 2 * nstate

    @pl.when(first)
    def _():
        shifted[0:8, :] = jnp.zeros((8, conv), F32)
        state[...] = jnp.zeros_like(state)

    shifted[8 : 8 + Q, :] = proj_ref[:, 0:conv]
    wide = 256
    for low in range(0, conv, wide):
        part = pl.ds(low, wide)
        total = cb_ref[0:1, part] + cw_ref[0:1, part] * shifted[5 : 5 + Q, part]
        for k in range(1, 4):
            total = total + cw_ref[k : k + 1, part] * shifted[5 + k : 5 + k + Q, part]
        sum_ref[:, part] = total
        act[:, part] = total * sigmoid(total)
    shifted[0:8, :] = shifted[Q : Q + 8, :]

    dt = softplus(proj_ref[:, conv : conv + LANES] + vec_ref[0:1, :])
    causal = tri_lower()
    logs = jnp.dot(causal.astype(F32), dt * vec_ref[1:2, :], precision=HI, preferred_element_type=F32)
    fill_tables(dt, logs, dt_tab, log_tab, log_rows, 0, groups, per)
    keys_b = act[:, inner : inner + nstate]
    keys_c = act[:, inner + nstate : conv].astype(BF16)
    b_cols = jnp.transpose(keys_b).astype(BF16)
    cross = mm(keys_c, b_cols)
    start_ref[...] = state[...].astype(BF16)
    span = per * HEAD
    low_half = lax.broadcasted_iota(jnp.int32, (Q, LANES), 1) < HEAD

    def group(g, carry):
        base = pl.multiple_of(g * span, span)
        dts, lgs = dt_tab[g], log_tab[g]
        carried = mm(keys_c, start_ref[:, pl.ds(base, span)])
        tails_all = []
        lasts = []
        for j in range(per // 2):
            cols = pl.ds(pl.multiple_of(base + j * LANES, LANES), LANES)
            h = g * per + 2 * j
            col0, col1 = spread(lgs, 2 * j), spread(lgs, 2 * j + 1)
            row0, row1 = log_rows[pl.ds(h, 1), :], log_rows[pl.ds(h + 1, 1), :]
            values = act[:, cols]
            stepped = (values * jnp.where(low_half, spread(dts, 2 * j), spread(dts, 2 * j + 1)))
            stepped_b = stepped.astype(BF16)
            mix0 = (jnp.exp(jnp.where(causal, col0 - row0, NEG)) * cross).astype(BF16)
            mix1 = (jnp.exp(jnp.where(causal, col1 - row1, NEG)) * cross).astype(BF16)
            zero = jnp.zeros_like(stepped_b)
            pairs = jnp.concatenate(
                [jnp.where(low_half, stepped_b, zero), jnp.where(low_half, zero, stepped_b)], axis=0)
            local = mm(jnp.concatenate([mix0, mix1], axis=1), pairs)
            both = jnp.where(low_half, col0, col1)
            last = both[Q - 1 : Q, :]
            out = local + carried[:, j * LANES : (j + 1) * LANES] * jnp.exp(both)
            out_ref[:, cols] = out + skip_ref[0:1, cols] * values
            tails_all.append((stepped * jnp.exp(last - both)).astype(BF16))
            lasts.append(jnp.exp(last))
        fresh = mm(b_cols, jnp.concatenate(tails_all, axis=1))
        cols = pl.ds(base, span)
        state[:, cols] = state[:, cols] * jnp.concatenate(lasts, axis=1) + fresh
        return carry

    lax.fori_loop(0, groups, group, 0)


def run_scan_forward(proj, cw, cb, vec, skip_cols, inner, nstate, groups, per):
    length = proj.shape[0]
    blocks = length // Q
    conv = inner + 2 * nstate
    whole = lambda shape: pl.BlockSpec(shape, lambda i: (0, 0))
    rows = lambda width: pl.BlockSpec((Q, width), lambda i: (i, 0))
    return pl.pallas_call(
        functools.partial(scan_forward, inner=inner, nstate=nstate, groups=groups, per=per),
        grid=(blocks,),
        in_specs=[rows(proj.shape[1]), whole(cw.shape), whole(cb.shape), whole(vec.shape), whole(skip_cols.shape)],
        out_specs=[rows(inner), rows(conv), pl.BlockSpec((nstate, inner), lambda i: (i, 0))],
        out_shape=[
            jax.ShapeDtypeStruct((length, inner), F32),
            jax.ShapeDtypeStruct((length, conv), F32),
            jax.ShapeDtypeStruct((blocks * nstate, inner), BF16),
        ],
        scratch_shapes=[
            pltpu.VMEM((Q + 8, conv), F32),
            pltpu.VMEM((Q, conv), F32),
            pltpu.VMEM((nstate, inner), F32),
            pltpu.VMEM((groups, Q, LANES), F32),
            pltpu.VMEM((groups, Q, LANES), F32),
            pltpu.VMEM((LANES, Q), F32),
        ],
        compiler_params=pltpu.CompilerParams(vmem_limit_bytes=60 << 20),
        cost_estimate=pl.CostEstimate(flops=12_000_000_000, bytes_accessed=60_000_000, transcendentals=20_000_000),
        name="scan_forward",
    )(proj, cw, cb, vec, skip_cols)


def piece_copies(place_ref, pieces, refs, target, sems):
    copies = []
    for index, (start, half, size, lane) in enumerate(pieces):
        rows, cols = refs[index].shape
        if half is not None:
            start = pl.multiple_of(start + jnp.bitwise_xor(place_ref[1], half) * size, 16)
        window = target.at[pl.ds(start, rows), pl.ds(lane, cols)]
        copies.append(pltpu.make_async_copy(refs[index], window, sems.at[index]))
    return copies


def load_pieces(*args):
    for copy in piece_copies(*args):
        copy.start()


def wait_pieces(*args):
    for copy in piece_copies(*args):
        copy.wait()


def columns_of(place_ref, position, order, width):
    return pl.ds(pl.multiple_of(jnp.bitwise_xor(place_ref[0], order[position]) * width, LANES), width)


def project_in(place_ref, tok_ref, gain_ref, *rest, pieces, order):
    refs, (normed_ref, proj_ref, weight, sems) = rest[: len(pieces)], rest[len(pieces) :]
    first = pl.program_id(0) == 0

    @pl.when(first)
    def _():
        load_pieces(place_ref, pieces, refs, weight, sems)

    width = tok_ref.shape[1] // len(order)
    tok = tok_ref[...].astype(F32)
    scale = lax.rsqrt(jnp.mean(tok * tok, axis=1, keepdims=True) + EPS)
    for position in range(len(order)):
        cols = columns_of(place_ref, position, order, width)
        value = tok_ref[:, cols].astype(F32) * scale * gain_ref[0:1, cols]
        normed_ref[:, position * width : (position + 1) * width] = value.astype(BF16)

    @pl.when(first)
    def _():
        wait_pieces(place_ref, pieces, refs, weight, sems)

    total = proj_ref.shape[1]
    step = 384
    for low in range(0, total, step):
        proj_ref[:, low : low + step] = mm_t(normed_ref[...], weight[low : low + step, :])


def grid_of(grid, in_specs, out_specs, scratch):
    return pltpu.PrefetchScalarGridSpec(
        num_scalar_prefetch=1, grid=grid, in_specs=in_specs, out_specs=out_specs, scratch_shapes=scratch)


def anywhere(count):
    return [pl.BlockSpec(memory_space=pl.ANY)] * count


def row_block(block, width):
    return pl.BlockSpec((block, width), lambda i, s: (i, 0))


def fixed(shape):
    return pl.BlockSpec(shape, lambda i, s: (0,) * len(shape))


def run_project_in(place, tok, gain, weight, total, order, block=256):
    pieces, arrays = weight
    length, width = tok.shape
    return pl.pallas_call(
        functools.partial(project_in, pieces=pieces, order=order),
        grid_spec=grid_of(
            (length // block,),
            [row_block(block, width), fixed(gain.shape)] + anywhere(len(pieces)),
            [row_block(block, width), row_block(block, total)],
            [pltpu.VMEM((total, width), BF16), pltpu.SemaphoreType.DMA((len(pieces),))],
        ),
        out_shape=[jax.ShapeDtypeStruct((length, width), BF16), jax.ShapeDtypeStruct((length, total), F32)],
        compiler_params=pltpu.CompilerParams(vmem_limit_bytes=50 << 20),
        cost_estimate=pl.CostEstimate(flops=20_000_000_000, bytes_accessed=30_000_000, transcendentals=1000),
        name="project_in",
    )(place, tok, gain, *arrays)


def gating(place_ref, normed_ref, cot_ref, scan_ref, gain_ref, *rest, wg_pieces, ow_pieces, order):
    n_g, n_o = len(wg_pieces), len(ow_pieces)
    wg_refs, ow_refs = rest[:n_g], rest[n_g : n_g + n_o]
    (mixed_ref, dscan_ref, dgate_ref, dgain_ref, wg, ow, gate_s, gated_s, scaled_s,
     g_sems, o_sems) = rest[n_g + n_o :]
    inner = wg.shape[0]
    parts = len(order)
    width = inner // parts
    first = pl.program_id(0) == 0

    @pl.when(first)
    def _():
        load_pieces(place_ref, wg_pieces, wg_refs, wg, g_sems)
        load_pieces(place_ref, ow_pieces, ow_refs, ow, o_sems)
        dgain_ref[...] = jnp.zeros_like(dgain_ref)
        wait_pieces(place_ref, wg_pieces, wg_refs, wg, g_sems)

    def fold(v):
        total = v[:, 0:LANES]
        for low in range(LANES, v.shape[1], LANES):
            total = total + v[:, low : low + LANES]
        return total

    power = None
    for p in range(parts):
        cols = slice(p * width, (p + 1) * width)
        gate = mm_t(normed_ref[...], wg[cols, :])
        gated = scan_ref[:, cols] * (gate * sigmoid(gate))
        gate_s[:, cols] = gate
        gated_s[:, cols] = gated
        term = fold(gated * gated)
        power = term if power is None else power + term
    scale = lax.rsqrt(jnp.sum(power, axis=1, keepdims=True) / inner + EPS)

    @pl.when(first)
    def _():
        wait_pieces(place_ref, ow_pieces, ow_refs, ow, o_sems)

    match = None
    for p in range(parts):
        true = columns_of(place_ref, p, order, width)
        rows = slice(p * width, (p + 1) * width)
        grad = mm_t(cot_ref[...], ow[rows, :])
        gated = gated_s[:, true]
        gain = gain_ref[0:1, true]
        unit = gated * scale
        mixed_ref[:, rows] = (unit * gain).astype(BF16)
        dgain_ref[0:1, true] += jnp.sum(grad * unit, axis=0, keepdims=True)
        scaled = grad * gain
        scaled_s[:, true] = scaled
        term = fold(scaled * gated)
        match = term if match is None else match + term
    pull = jnp.sum(match, axis=1, keepdims=True) * (scale * scale) / inner
    for p in range(parts):
        cols = slice(p * width, (p + 1) * width)
        gate = gate_s[:, cols]
        sig = sigmoid(gate)
        silu = gate * sig
        dgated = scale * (scaled_s[:, cols] - gated_s[:, cols] * pull)
        dscan_ref[:, cols] = dgated * silu
        dgate_ref[:, cols] = (dgated * scan_ref[:, cols] * (sig + silu * (1.0 - sig))).astype(BF16)


def run_gating(place, normed, gate_weight, out_weight, cot, scan_out, gain, order, block=256):
    wg_pieces, wg_arrays = gate_weight
    ow_pieces, ow_arrays = out_weight
    length, width = normed.shape
    inner = scan_out.shape[1]
    return pl.pallas_call(
        functools.partial(gating, wg_pieces=wg_pieces, ow_pieces=ow_pieces, order=order),
        grid_spec=grid_of(
            (length // block,),
            [row_block(block, width), row_block(block, width), row_block(block, inner), fixed((1, inner))]
            + anywhere(len(wg_pieces) + len(ow_pieces)),
            [row_block(block, inner), row_block(block, inner), row_block(block, inner), fixed((1, inner))],
            [pltpu.VMEM((inner, width), BF16), pltpu.VMEM((inner, width), BF16)]
            + [pltpu.VMEM((block, inner), F32)] * 3
            + [pltpu.SemaphoreType.DMA((len(wg_pieces),)), pltpu.SemaphoreType.DMA((len(ow_pieces),))],
        ),
        out_shape=[
            jax.ShapeDtypeStruct((length, inner), BF16),
            jax.ShapeDtypeStruct((length, inner), F32),
            jax.ShapeDtypeStruct((length, inner), BF16),
            jax.ShapeDtypeStruct((1, inner), F32),
        ],
        compiler_params=pltpu.CompilerParams(vmem_limit_bytes=62 << 20),
        cost_estimate=pl.CostEstimate(flops=40_000_000_000, bytes_accessed=70_000_000, transcendentals=10_000_000),
        name="gating",
    )(place, normed, cot, scan_out, gain, *wg_arrays, *ow_arrays)


def gate_back(place_ref, dgate_ref, *rest, pieces):
    refs, (grad_ref, weight, sems) = rest[: len(pieces)], rest[len(pieces) :]

    @pl.when(pl.program_id(0) == 0)
    def _():
        load_pieces(place_ref, pieces, refs, weight, sems)
        wait_pieces(place_ref, pieces, refs, weight, sems)

    step = 384
    for low in range(0, grad_ref.shape[1], step):
        grad_ref[:, low : low + step] = mm(dgate_ref[...], weight[:, low : low + step])


def run_gate_back(place, dgate, model, weight, block=256):
    pieces, arrays = weight
    length, inner = dgate.shape
    return pl.pallas_call(
        functools.partial(gate_back, pieces=pieces),
        grid_spec=grid_of(
            (length // block,),
            [row_block(block, inner)] + anywhere(len(pieces)),
            row_block(block, model),
            [pltpu.VMEM((inner, model), BF16), pltpu.SemaphoreType.DMA((len(pieces),))],
        ),
        out_shape=jax.ShapeDtypeStruct((length, model), F32),
        compiler_params=pltpu.CompilerParams(vmem_limit_bytes=40 << 20),
        cost_estimate=pl.CostEstimate(flops=16_000_000_000, bytes_accessed=22_000_000, transcendentals=0),
        name="gate_back",
    )(place, dgate, *arrays)


def input_back(place_ref, part_ref, tok_ref, cot_ref, gain_ref, *rest, count, pieces, order):
    dproj_refs, rest = rest[:count], rest[count:]
    refs, (grad_ref, dgain_ref, weight, dn, sems) = rest[: len(pieces)], rest[len(pieces) :]
    first = pl.program_id(0) == 0

    @pl.when(first)
    def _():
        load_pieces(place_ref, pieces, refs, weight, sems)
        dgain_ref[...] = jnp.zeros_like(dgain_ref)
        wait_pieces(place_ref, pieces, refs, weight, sems)

    model = tok_ref.shape[1]
    width = model // len(order)
    tok = tok_ref[...].astype(F32)
    scale = lax.rsqrt(jnp.mean(tok * tok, axis=1, keepdims=True) + EPS)
    match = None
    for position in range(len(order)):
        spot = slice(position * width, (position + 1) * width)
        true = columns_of(place_ref, position, order, width)
        grad, low = part_ref[:, spot], 0
        for ref in dproj_refs:
            grad = grad + mm(ref[...], weight[low : low + ref.shape[1], spot])
            low += ref.shape[1]
        value = tok_ref[:, true].astype(F32)
        dgain_ref[0:1, true] += jnp.sum(grad * (value * scale), axis=0, keepdims=True)
        grad = grad * gain_ref[0:1, true]
        dn[:, spot] = grad
        term = jnp.sum(grad * value, axis=1, keepdims=True)
        match = term if match is None else match + term
    pull = match * (scale * scale * scale) / model
    for position in range(len(order)):
        spot = slice(position * width, (position + 1) * width)
        true = columns_of(place_ref, position, order, width)
        value = tok_ref[:, true].astype(F32)
        grad_ref[:, true] = cot_ref[:, true].astype(F32) + (scale * dn[:, spot] - value * pull)


def run_input_back(place, part, dprojs, tok, cot, gain, weight, order, block=256):
    pieces, arrays = weight
    length, model = tok.shape
    widths = [d.shape[1] for d in dprojs]
    return pl.pallas_call(
        functools.partial(input_back, count=len(dprojs), pieces=pieces, order=order),
        grid_spec=grid_of(
            (length // block,),
            [row_block(block, model), row_block(block, model), row_block(block, model), fixed((1, model))]
            + [row_block(block, w) for w in widths] + anywhere(len(pieces)),
            [row_block(block, model), fixed((1, model))],
            [pltpu.VMEM((sum(widths), model), BF16), pltpu.VMEM((block, model), F32),
             pltpu.SemaphoreType.DMA((len(pieces),))],
        ),
        out_shape=[jax.ShapeDtypeStruct((length, model), F32), jax.ShapeDtypeStruct((1, model), F32)],
        compiler_params=pltpu.CompilerParams(vmem_limit_bytes=50 << 20),
        cost_estimate=pl.CostEstimate(flops=22_000_000_000, bytes_accessed=46_000_000, transcendentals=1000),
        name="input_back",
    )(place, part, tok, cot, gain, *dprojs, *arrays)


def project_out(place_ref, mixed_ref, tok_ref, *rest, pieces):
    refs, (out_ref, weight, sems) = rest[: len(pieces)], rest[len(pieces) :]

    @pl.when(pl.program_id(0) == 0)
    def _():
        load_pieces(place_ref, pieces, refs, weight, sems)
        wait_pieces(place_ref, pieces, refs, weight, sems)

    step = 384
    for low in range(0, out_ref.shape[1], step):
        cols = slice(low, low + step)
        out_ref[:, cols] = (tok_ref[:, cols].astype(F32) + mm(mixed_ref[...], weight[:, cols])).astype(BF16)


def run_project_out(place, mixed, tok, weight, block=256):
    pieces, arrays = weight
    length, model = tok.shape
    inner = mixed.shape[1]
    return pl.pallas_call(
        functools.partial(project_out, pieces=pieces),
        grid_spec=grid_of(
            (length // block,),
            [row_block(block, inner), row_block(block, model)] + anywhere(len(pieces)),
            row_block(block, model),
            [pltpu.VMEM((inner, model), BF16), pltpu.SemaphoreType.DMA((len(pieces),))],
        ),
        out_shape=jax.ShapeDtypeStruct((length, model), BF16),
        compiler_params=pltpu.CompilerParams(vmem_limit_bytes=40 << 20),
        cost_estimate=pl.CostEstimate(flops=14_000_000_000, bytes_accessed=20_000_000, transcendentals=0),
        name="project_out",
    )(place, mixed, tok, *arrays)


def scan_backward(proj_ref, tail_ref, sum_ref, keys_ref, out_ref, dout_ref, start_ref, cw_ref, cwk_ref, vec_ref,
                  skip_ref, pick_ref, *rest, nstate, low, groups, per, begin, last):
    if not begin:
        old_cross_ref, old_keys_ref, old_raw_ref = rest[:3]
        rest = rest[3:]
    dproj_ref, dcw_ref, dcb_ref, dskip_ref, dvec_ref = rest[:5]
    rest = rest[5:]
    if not last:
        cross_ref, keys_ref_out, raw_ref = rest[:3]
        rest = rest[3:]
    dsum, dstate, edge, logs_v, tails_v, steps_v, dt_tab, log_tab, log_rows, dcross, dkeys = rest
    first = pl.program_id(0) == 0
    span_all = groups * per * HEAD
    conv = dsum.shape[1]

    @pl.when(first)
    def _():
        dsum[Q : Q + 8, :] = jnp.zeros((8, conv), F32)
        dstate[...] = jnp.zeros_like(dstate)
        edge[...] = jnp.zeros_like(edge)
        dcw_ref[...] = jnp.zeros_like(dcw_ref)
        dcb_ref[...] = jnp.zeros_like(dcb_ref)
        dskip_ref[...] = jnp.zeros_like(dskip_ref)
        dvec_ref[...] = jnp.zeros_like(dvec_ref)

    raw = tail_ref[:, 2 * nstate : 2 * nstate + LANES] + vec_ref[0:1, :]
    dt = softplus(raw)
    lower = tri_lower()
    rate = vec_ref[1:2, :]
    logs = jnp.dot(lower.astype(F32), dt * rate, precision=HI, preferred_element_type=F32)
    fill_tables(dt, logs, dt_tab, log_tab, log_rows, low, groups, per)
    sum_b = keys_ref[:, 0:nstate]
    sum_c = keys_ref[:, nstate : 2 * nstate]
    sig_b, sig_c = sigmoid(sum_b), sigmoid(sum_c)
    keys_b32, keys_c32 = sum_b * sig_b, sum_c * sig_c
    keys_b, keys_c = keys_b32.astype(BF16), keys_c32.astype(BF16)
    c_cols = jnp.transpose(keys_c32).astype(BF16)
    cross = mm(keys_b, c_cols)
    span = per * HEAD
    low_half = lax.broadcasted_iota(jnp.int32, (Q, LANES), 1) < HEAD
    upper = lax.broadcasted_iota(jnp.int32, (Q, Q), 0) <= lax.broadcasted_iota(jnp.int32, (Q, Q), 1)
    if not begin:
        dcross[...] = old_cross_ref[...]
        dkeys[...] = old_keys_ref[...]
    else:
        dcross[...] = jnp.zeros_like(dcross)
        dkeys[...] = jnp.zeros_like(dkeys)

    def group(g, carry):
        base = pl.multiple_of(g * span, span)
        whole = pl.ds(base, span)
        dts, lgs = dt_tab[g], log_tab[g]
        dstate_b = dstate[:, whole].astype(BF16)
        from_state = mm(keys_b, dstate_b)
        tails_all, outs_all, lasts = [], [], []
        dcr = None
        for j in range(per // 2):
            cols = pl.ds(pl.multiple_of(base + j * LANES, LANES), LANES)
            h = (low + g) * per + 2 * j
            col0, col1 = spread(lgs, 2 * j), spread(lgs, 2 * j + 1)
            row0, row1 = log_rows[pl.ds(h, 1), :], log_rows[pl.ds(h + 1, 1), :]
            total = sum_ref[:, cols]
            sig = sigmoid(total)
            values = total * sig
            step = jnp.where(low_half, spread(dts, 2 * j), spread(dts, 2 * j + 1))
            stepped = values * step
            stepped_b = stepped.astype(BF16)
            dout = dout_ref[:, cols]
            dout_b = dout.astype(BF16)
            decay0 = jnp.exp(jnp.where(upper, row0 - col0, NEG))
            decay1 = jnp.exp(jnp.where(upper, row1 - col1, NEG))
            mix = jnp.concatenate([(decay0 * cross).astype(BF16), (decay1 * cross).astype(BF16)], axis=1)
            zero = jnp.zeros_like(dout_b)
            douts = jnp.concatenate(
                [jnp.where(low_half, dout_b, zero), jnp.where(low_half, zero, dout_b)], axis=0)
            local = mm(mix, douts)
            dmix = mm_t(stepped_b, douts)
            term = dmix[:, 0:Q] * decay0 + dmix[:, Q : 2 * Q] * decay1
            dcr = term if dcr is None else dcr + term
            both = jnp.where(low_half, col0, col1)
            last = both[Q - 1 : Q, :]
            tail = jnp.exp(last - both)
            passed = from_state[:, j * LANES : (j + 1) * LANES] * tail
            dstepped = local + passed
            skip = skip_ref[0:1, cols]
            scan = out_ref[:, cols] - skip * values
            logs_v[:, cols] = dout_b.astype(F32) * scan - stepped_b.astype(F32) * local
            tails_v[:, cols] = stepped * passed
            steps_v[:, cols] = dstepped * values
            dvalues = dstepped * step + dout * skip
            dskip_ref[0:1, cols] += jnp.sum(dout * values, axis=0, keepdims=True)
            dsum[0:Q, cols] = dvalues * (sig + values * (1.0 - sig))
            tails_all.append((stepped * tail).astype(BF16))
            outs_all.append((dout * jnp.exp(both)).astype(BF16))
            lasts.append(jnp.exp(last))
        dcross[...] += dcr
        outs = jnp.concatenate(outs_all, axis=1)
        starts = start_ref[:, whole]
        dkeys[:, nstate : 2 * nstate] += mm_t(outs, starts)
        dkeys[:, 0:nstate] += mm_t(jnp.concatenate(tails_all, axis=1), dstate_b)
        kept = dstate[:, whole] * jnp.concatenate(lasts, axis=1)
        edge[0:1, whole] = jnp.sum(kept * starts.astype(F32), axis=0, keepdims=True)
        dstate[:, whole] = kept + mm(c_cols, outs)
        return carry

    lax.fori_loop(0, groups, group, 0)

    if last:
        dcr = dcross[...]
        exact = lambda u, v: jnp.dot(u, v, precision=HI, preferred_element_type=F32)
        d_b = dkeys[:, 0:nstate] + exact(dcr, keys_c32)
        d_c = dkeys[:, nstate : 2 * nstate] + exact(jnp.transpose(dcr), keys_b32)
        dsum[0:Q, span_all : span_all + nstate] = d_b * (sig_b + keys_b32 * (1.0 - sig_b))
        dsum[0:Q, span_all + nstate : conv] = d_c * (sig_c + keys_c32 * (1.0 - sig_c))
    else:
        cross_ref[...] = dcross[...]
        keys_ref_out[...] = dkeys[...]

    def reduce_heads(v):
        high = v.astype(BF16)
        low = (v - high.astype(F32)).astype(BF16)
        return mm(high, pick_ref[...]) + mm(low, pick_ref[...])

    dlogs = reduce_heads(logs_v[...])
    dtails = reduce_heads(tails_v[...])
    dlogit = (
        jnp.dot(upper.astype(F32), dlogs, precision=HI, preferred_element_type=F32)
        + jnp.dot(1.0 - upper.astype(F32), dtails, precision=HI, preferred_element_type=F32)
        + reduce_heads(edge[...])[0:1, :]
    )
    dstep = reduce_heads(steps_v[...]) + dlogit * rate
    draw = dstep * sigmoid(raw)
    dvec_ref[0:1, :] += jnp.sum(draw, axis=0, keepdims=True)
    dvec_ref[1:2, :] += jnp.sum(dlogit * dt * rate, axis=0, keepdims=True)
    if last:
        dproj_ref[:, conv : conv + LANES] = (draw + old_raw_ref[...]).astype(BF16)
    elif begin:
        raw_ref[...] = draw
    else:
        raw_ref[...] = draw + old_raw_ref[...]

    wide = 256
    for start in range(0, conv, wide):
        part = pl.ds(start, wide)
        if start < span_all:
            source, taps_ref, local = proj_ref, cw_ref, part
        else:
            source, taps_ref, local = tail_ref, cwk_ref, pl.ds(start - span_all, wide)
        taken = source[:, local]
        total = None
        for k in range(4):
            moved = dsum[3 - k : 3 - k + Q, part]
            dcw_ref[k : k + 1, part] += jnp.sum(taken * moved, axis=0, keepdims=True)
            term = taps_ref[k : k + 1, local] * moved
            total = term if total is None else total + term
            if k == 3:
                dcb_ref[0:1, part] += jnp.sum(moved, axis=0, keepdims=True)
        dproj_ref[:, part] = total.astype(BF16)
    dsum[Q : Q + 8, :] = dsum[0:8, :]


def run_scan_backward(proj, sums, scan_out, dscan, starts, cw, vec, skip_cols, pick, inner, nstate, low, groups, per,
                      previous, last):
    length = proj.shape[0]
    blocks = length // Q
    span = groups * per * HEAD
    begin = previous is None
    conv = span + (2 * nstate if last else 0)
    where = low * per * HEAD // span
    whole = lambda shape: pl.BlockSpec(shape, lambda i: (0, 0))
    rows = lambda width, col=0: pl.BlockSpec((Q, width), lambda i: (blocks - 1 - i, col))
    part = lambda height: pl.BlockSpec((height, span), lambda i: (0, where))
    tail = 2 * nstate + LANES
    out_specs = [rows(conv + (LANES if last else 0)), whole((4, conv)), whole((1, conv)), whole((1, span)),
                 whole((8, LANES))]
    out_shape = [
        jax.ShapeDtypeStruct((length, conv + (LANES if last else 0)), BF16),
        jax.ShapeDtypeStruct((4, conv), F32),
        jax.ShapeDtypeStruct((1, conv), F32),
        jax.ShapeDtypeStruct((1, span), F32),
        jax.ShapeDtypeStruct((8, LANES), F32),
    ]
    carried = [rows(Q), rows(2 * nstate), rows(LANES)]
    if not last:
        out_specs += carried
        out_shape += [jax.ShapeDtypeStruct((length, w), F32) for w in (Q, 2 * nstate, LANES)]
    return pl.pallas_call(
        functools.partial(scan_backward, nstate=nstate, low=low, groups=groups, per=per, begin=begin, last=last),
        grid=(blocks,),
        in_specs=[
            rows(span, where), rows(tail, inner // tail), rows(span, where), rows(2 * nstate, inner // (2 * nstate)),
            rows(span, where), rows(span, where),
            pl.BlockSpec((nstate, span), lambda i: (blocks - 1 - i, where)),
            part(4), pl.BlockSpec((4, 2 * nstate), lambda i: (0, inner // (2 * nstate))),
            whole(vec.shape), part(1), pl.BlockSpec((span, LANES), lambda i: (where, 0)),
        ] + ([] if begin else carried),
        out_specs=out_specs,
        out_shape=out_shape,
        scratch_shapes=[
            pltpu.VMEM((Q + 8, conv), F32),
            pltpu.VMEM((nstate, span), F32),
            pltpu.VMEM((8, span), F32),
            pltpu.VMEM((Q, span), F32),
            pltpu.VMEM((Q, span), F32),
            pltpu.VMEM((Q, span), F32),
            pltpu.VMEM((groups, Q, LANES), F32),
            pltpu.VMEM((groups, Q, LANES), F32),
            pltpu.VMEM((LANES, Q), F32),
            pltpu.VMEM((Q, Q), F32),
            pltpu.VMEM((Q, 2 * nstate), F32),
        ],
        compiler_params=pltpu.CompilerParams(vmem_limit_bytes=50 << 20),
        cost_estimate=pl.CostEstimate(flops=40_000_000_000, bytes_accessed=40_000_000, transcendentals=15_000_000),
        name="scan_backward",
    )(proj, proj, sums, sums, scan_out, dscan, starts, cw, cw, vec, skip_cols, pick, *(previous or ()))


def bits_of(size):
    return [1 << b for b in range(size.bit_length() - 1)]


def swap(value, axis, bit, size):
    return lax.ppermute(value, axis, [(i, i ^ bit) for i in range(size)])


def after(value, *deps):
    return lax.optimization_barrier((value,) + deps)[0] if deps else value


def order_of(size):
    flipped = []
    for index in range(size):
        value = 0
        for low, high in zip(bits_of(size), reversed(bits_of(size))):
            value |= high if index & low else 0
        flipped.append(value)
    return flipped


class Gather:
    def __init__(self, shard, order, rep_index, groups, copies, lanes, chunks):
        self.order, self.groups, self.copies = order, groups, copies
        self.size = shard.shape
        self.lanes = lanes
        self.half = shard.shape[0] // 2
        self.rows = self.half // chunks
        self.shard = shard
        parity = rep_index & 1
        self.mine = [lax.dynamic_slice_in_dim(shard, parity * self.half + c * self.rows, self.rows, 0)
                     for c in range(chunks)]
        self.there, self.across = [None] * chunks, [None] * chunks
        self.own, self.early = None, []

    def far(self, chunk, *deps):
        value = after(self.mine[chunk], *deps)
        self.there[chunk] = swap(value, "shard", 2, self.groups)

    def whole(self, *deps):
        self.there = [swap(after(self.shard, *deps), "shard", 2, self.groups)]
        self.across = []

    def side(self, chunk):
        self.across[chunk] = swap(self.there[chunk], "rep", 1, self.copies)

    def core(self, value, *deps):
        return swap(after(value, *deps), "shard", 1, self.groups)

    def finish(self, *deps):
        own = self.own if self.own is not None else self.core(self.shard)
        have = {0: [(0, None, 0, self.shard)], 1: [(0, None, 0, own)]}
        if self.across:
            have[2] = [(c * self.rows, h, self.half, v) for h, vs in ((0, self.there), (1, self.across))
                       for c, v in enumerate(vs)]
        else:
            have[2] = [(0, None, 0, self.there[0])]
        have[3] = []
        for index, (row, half, size, value) in enumerate(have[2]):
            if index < len(self.early):
                partner = self.early[index]
            else:
                partner = self.core(value, *(deps if index == len(have[2]) - 1 else ()))
            have[3].append((row, half, size, partner))
        pieces, arrays = [], []
        for position, source in enumerate(self.order):
            for row, half, size, value in have[source]:
                if self.lanes:
                    pieces.append((row, half, size, position * self.size[1]))
                else:
                    pieces.append((row + position * self.size[0], half, size, 0))
                arrays.append(value)
        return tuple(pieces), tuple(arrays)


class Total:
    def __init__(self, kept, sent, axis, rep_index, groups, copies, narrow=False):
        self.axis, self.rep_index = axis, rep_index
        self.sizes = {"shard": groups, "rep": copies}
        self.stages = [("shard", index, 1) for index in range(len(bits_of(groups)))]
        count = len(bits_of(copies))
        over = [("rep", 0, 1)] + [("rep", index, min(2, count - index)) for index in range(1, count, 2)]
        self.stages += over
        self.back = list(reversed(over))
        if narrow:
            self.back = [(name, shift + bit, 1) for name, shift, width in self.back for bit in range(width)]
        self.value, self.out = kept, [sent]
        self.fly()

    @classmethod
    def join(cls, chains):
        first = chains[0]
        new = object.__new__(cls)
        new.axis, new.rep_index, new.sizes = first.axis, first.rep_index, first.sizes
        new.stages, new.back = first.stages, first.back
        new.value = jnp.concatenate([v.value for v in chains])
        new.coming = [jnp.concatenate(v) for v in zip(*(c.coming for c in chains))]
        return new

    def fly(self):
        name, shift, _ = self.stages[0]
        self.coming = [swap(v, name, (k + 1) << shift, self.sizes[name]) for k, v in enumerate(self.out)]

    def done(self):
        return not self.stages and not self.back

    def step(self, *deps):
        coming = [after(v, *deps) for v in self.coming]
        if not self.stages:
            return self.widen(coming)
        self.stages.pop(0)
        terms = [self.value] + coming
        if not self.stages:
            self.value = sum(v.astype(F32) for v in terms).astype(BF16)
            self.fly_back()
            return [self.value]
        name, shift, width = self.stages[0]
        parts = 1 << width
        axis = self.axis if name == "shard" else 0
        size = self.value.shape[axis] // parts
        mine = 0 if name == "shard" else (self.rep_index >> shift) & (parts - 1)
        cut = lambda start: sum(lax.dynamic_slice_in_dim(v, start, size, axis).astype(F32) for v in terms)
        self.out = [cut((mine ^ k) * size).astype(BF16) for k in range(1, parts)]
        self.value = cut(mine * size)
        self.fly()
        return self.out

    def fly_back(self):
        name, shift, width = self.back[0]
        self.coming = [swap(self.value, name, k << shift, self.sizes[name]) for k in range(1, 1 << width)]

    def widen(self, coming):
        name, shift, width = self.back.pop(0)
        parts = [self.value] + coming
        for bit in range(width):
            turn = ((self.rep_index >> (shift + bit)) & 1) != 0
            parts = [jnp.where(turn, parts[k ^ (1 << bit)], parts[k]) for k in range(len(parts))]
        if not self.back:
            self.value = [v.astype(F32) for v in parts]
            return self.value
        self.value = jnp.concatenate(parts)
        self.fly_back()
        return [self.value]


def outer(left, right):
    return lax.dot_general(left, right, (((0,), (0,)), ((), ())), preferred_element_type=F32).astype(BF16)


def on_device(groups, copies, tokens, norm_gain, in_weight, conv_weight, conv_bias, dt_bias, a_log, skip, gate_gain,
              out_weight, cotangent):
    if tokens.shape[0] != 1 or groups != 4:
        raise ValueError("unexpected sizes")
    order = order_of(groups)
    shard_index = lax.axis_index("shard")
    rep_index = lax.axis_index("rep")
    tok, cot = tokens[0], cotangent[0]
    inner = gate_gain.shape[0] * groups
    conv = conv_bias.shape[0] * groups
    heads = dt_bias.shape[0] * groups
    nstate = (conv - inner) // 2
    model = tok.shape[1]
    taps = conv_weight.shape[0]
    outputs_all = in_weight.shape[1]
    place = jnp.stack([shard_index, rep_index & 1]).astype(jnp.int32)

    turned = in_weight.T
    total = conv + LANES
    conv_part = jnp.pad(turned[inner:], ((0, total + inner - outputs_all), (0, 0)))
    make = lambda shard, lanes, chunks: Gather(shard, order, rep_index, groups, copies, lanes, chunks)
    wc = make(conv_part, True, 2)
    wg = make(turned[:inner], True, 1)
    ow = make(out_weight, False, 1)

    small = (norm_gain, conv_bias, dt_bias, a_log, skip, gate_gain, conv_weight)
    packed = jnp.concatenate([v.reshape(-1) for v in small])
    wc.far(0)
    wc.far(1)
    wc.side(0)
    wc.side(1)
    wc.own = wc.core(wc.shard)
    wc.early = [wc.core(wc.there[0])]
    wg.far(0, wc.there[1], wc.own, wc.early[0])
    ow.whole(wc.there[1], wc.own, wc.early[0])
    rows = [packed, swap(packed, "shard", 1, groups)]
    far = swap(packed, "shard", 2, groups)
    rows += [far, swap(far, "shard", 1, groups)]
    for bit in bits_of(groups):
        turn = (shard_index & bit) != 0
        rows = [jnp.where(turn, rows[j ^ bit], rows[j]) for j in range(groups)]
    everyone = jnp.stack(rows).astype(F32)
    parts, low = [], 0
    for v in small:
        parts.append(everyone[:, low : low + v.size])
        low += v.size
    gain, cb, db, al, sk, gg = (v.reshape(-1) for v in parts[:6])
    cw = parts[6].reshape(groups, taps, -1).transpose(1, 0, 2).reshape(taps, conv)
    gain, cb, gg = gain[None], cb[None], gg[None]
    vec = jnp.pad(jnp.stack([db, -jnp.exp(al)]), ((0, 6), (0, LANES - heads)))
    skip_cols = jnp.repeat(sk, inner // heads)[None]
    pick = (jnp.arange(inner)[:, None] // (inner // heads) == jnp.arange(LANES)[None]).astype(BF16)

    wc = wc.finish(gain, cb, gg, cw, vec, skip_cols, pick)
    normed, proj = run_project_in(place, tok, gain, wc, total, order)
    wg.there[0] = after(wg.there[0], normed)
    wg.side(0)
    proj = after(proj, wg.there[0])
    per = 8
    scan_out, sums, starts = run_scan_forward(proj, cw, cb, vec, skip_cols, inner, nstate, heads // per, per)
    wg, ow = wg.finish(scan_out), ow.finish(scan_out)
    mixed, dscan, dgate, dgg = run_gating(place, normed, wg, ow, cot, scan_out, gg, order)

    chain = lambda kept, sent, axis, *way: Total(kept, sent, axis, rep_index, groups, copies, *way)
    half = inner // 2
    out_sent = outer(mixed[:, half:], cot)
    o = chain(outer(mixed[:, :half], cot), out_sent, 0, True)
    half = model // 2
    left, right = normed[:, :half], normed[:, half:]
    gate_sent = outer(dgate, right)
    marks = o.step(o.value)
    g = chain(outer(after(dgate, *marks), left), gate_sent, 1)
    marks = marks + g.step(g.value)

    blocks = heads // per
    cuts = [blocks * v // 3 for v in range(4)]
    chains, grads, carried = [o, g], [], None
    for index in range(3):
        low, high = cuts[index], cuts[index + 1]
        found = run_scan_backward(
            proj, sums, scan_out, after(dscan, *marks), starts, cw, vec, skip_cols, pick, inner, nstate, low,
            high - low, per, carried, index == 2)
        grads.append(found[:5])
        carried = tuple(found[5:])
        dproj, marks = found[0], []
        if index == 1:
            marks = o.step(dproj)
        if index == 2:
            marks = ab.coming + g.step(dproj)
            marks = marks + o.step(dproj, *marks)
        dproj = after(dproj, *marks)
        sent = outer(dproj, right)
        kept = outer(after(dproj, sent, *g.coming) if index == 1 else dproj, left)
        new = chain(kept, sent, 1)
        chains.append(new)
        if index == 0:
            marks = marks + new.coming + o.step(kept)
        if index == 1:
            ab = Total.join(chains[2:])
            marks = marks + ab.step(kept)
            marks = marks + g.step(kept, *marks)
        if index == 2:
            marks = marks + new.step(kept)

    part = run_gate_back(place, after(dgate, *marks), model, wg)
    abc = Total.join([ab, chains[4]])
    marks = g.step(part)
    marks = marks + abc.step(part, *marks)
    marks = marks + o.step(part, *marks)
    input_grad, dgain = run_input_back(place, after(part, *marks), [v[0] for v in grads], tok, cot, gain, wc, order)

    dcw = jnp.concatenate([v[1] for v in grads], axis=1)
    dcb = jnp.concatenate([v[2][0] for v in grads])
    dskip = jnp.concatenate([v[3][0] for v in grads]).reshape(heads, -1).sum(1)
    dvec = sum(v[4] for v in grads)
    pieces = (dcb, dvec[0, :heads], dvec[1, :heads], dskip, dgg[0])
    flat = jnp.concatenate([v.reshape(groups, -1) for v in pieces]
                           + [dcw.reshape(taps, groups, -1).transpose(1, 0, 2).reshape(groups, -1)], axis=1)
    flat = jnp.concatenate([dgain[0].reshape(groups, -1), flat], axis=1)
    marks = abc.step(dgain, *g.coming)
    marks = marks + g.step(*marks)
    output = run_project_out(place, after(mixed, *marks), tok, ow)
    marks = abc.step(output, *g.coming)
    o.step(output)
    flat = after(flat, output, *marks)
    for axis, size in (("shard", groups), ("rep", copies)):
        for bit in bits_of(size):
            flat = flat + swap(flat, axis, bit, size)
    for old in (g, o, abc):
        while not old.done():
            old.step()

    in_total = jnp.concatenate(g.value + abc.value)[:outputs_all].T
    out_total = jnp.concatenate(o.value)

    own = lax.dynamic_slice_in_dim(flat, shard_index, 1, 0)[0]
    shares, low = [], 0
    for v in small:
        shares.append(own[low : low + v.size].reshape(v.shape))
        low += v.size
    d_gain, d_cb, d_db, d_al, d_sk, d_gg, d_cw = shares
    return (output[None], input_grad[None], d_gain, in_total, d_cw, d_cb, d_db, d_al, d_sk, d_gg, out_total)


def solution(mesh):
    whole = P(("shard", "rep"), None, None)
    row, matrix, cols = P("shard"), P("shard", None), P(None, "shard")
    return jax.shard_map(
        functools.partial(on_device, mesh.shape["shard"], mesh.shape["rep"]),
        mesh=mesh,
        in_specs=(whole, row, matrix, cols, row, row, row, row, row, matrix, whole),
        out_specs=(whole, whole, row, matrix, cols, row, row, row, row, row, matrix),
        check_vma=False,
    )
```

```python
import functools

import jax
import jax.numpy as jnp
from jax import lax
from jax.experimental import pallas as pl
from jax.experimental.pallas import tpu as pltpu
from jax.sharding import PartitionSpec as P

Q = 128
LANES = 128
HEAD = 64
EPS = 1e-05
F32 = jnp.float32
BF16 = jnp.bfloat16
HI = lax.Precision.HIGHEST
NEG = -1e30


def mm(a, b):
    return jnp.dot(a, b, preferred_element_type=F32)


def mm_t(a, b):
    return lax.dot_general(a, b, (((1,), (1,)), ((), ())), preferred_element_type=F32)


def softplus(v):
    return jnp.maximum(v, 0.0) + jnp.log1p(jnp.exp(-jnp.abs(v)))


def sigmoid(v):
    return 1.0 / (1.0 + jnp.exp(-v))


def tri_lower():
    rows = lax.broadcasted_iota(jnp.int32, (Q, Q), 0)
    cols = lax.broadcasted_iota(jnp.int32, (Q, Q), 1)
    return rows >= cols


def spread(table, lane):
    return jnp.broadcast_to(table[:, lane : lane + 1], (Q, LANES))


def fill_tables(dt, logs, dt_tab, log_tab, log_rows, low, groups, per):
    log_rows[...] = jnp.transpose(logs)
    for g in range(groups):
        shift = (LANES - (low + g) * per) % LANES
        dt_tab[g] = pltpu.roll(dt, shift, 1) if shift else dt
        log_tab[g] = pltpu.roll(logs, shift, 1) if shift else logs


def scan_forward(proj_ref, cw_ref, cb_ref, vec_ref, skip_ref, out_ref, sum_ref, start_ref,
                 shifted, act, state, dt_tab, log_tab, log_rows, *, inner, nstate, groups, per):
    first = pl.program_id(0) == 0
    conv = inner + 2 * nstate

    @pl.when(first)
    def _():
        shifted[0:8, :] = jnp.zeros((8, conv), F32)
        state[...] = jnp.zeros_like(state)

    shifted[8 : 8 + Q, :] = proj_ref[:, 0:conv]
    wide = 256
    for low in range(0, conv, wide):
        part = pl.ds(low, wide)
        total = cb_ref[0:1, part] + cw_ref[0:1, part] * shifted[5 : 5 + Q, part]
        for k in range(1, 4):
            total = total + cw_ref[k : k + 1, part] * shifted[5 + k : 5 + k + Q, part]
        sum_ref[:, part] = total
        act[:, part] = total * sigmoid(total)
    shifted[0:8, :] = shifted[Q : Q + 8, :]

    dt = softplus(proj_ref[:, conv : conv + LANES] + vec_ref[0:1, :])
    causal = tri_lower()
    logs = jnp.dot(causal.astype(F32), dt * vec_ref[1:2, :], precision=HI, preferred_element_type=F32)
    fill_tables(dt, logs, dt_tab, log_tab, log_rows, 0, groups, per)
    keys_b = act[:, inner : inner + nstate]
    keys_c = act[:, inner + nstate : conv].astype(BF16)
    b_cols = jnp.transpose(keys_b).astype(BF16)
    cross = mm(keys_c, b_cols)
    start_ref[...] = state[...].astype(BF16)
    span = per * HEAD
    low_half = lax.broadcasted_iota(jnp.int32, (Q, LANES), 1) < HEAD

    def group(g, carry):
        base = pl.multiple_of(g * span, span)
        dts, lgs = dt_tab[g], log_tab[g]
        carried = mm(keys_c, start_ref[:, pl.ds(base, span)])
        tails_all = []
        lasts = []
        for j in range(per // 2):
            cols = pl.ds(pl.multiple_of(base + j * LANES, LANES), LANES)
            h = g * per + 2 * j
            col0, col1 = spread(lgs, 2 * j), spread(lgs, 2 * j + 1)
            row0, row1 = log_rows[pl.ds(h, 1), :], log_rows[pl.ds(h + 1, 1), :]
            values = act[:, cols]
            stepped = (values * jnp.where(low_half, spread(dts, 2 * j), spread(dts, 2 * j + 1)))
            stepped_b = stepped.astype(BF16)
            mix0 = (jnp.exp(jnp.where(causal, col0 - row0, NEG)) * cross).astype(BF16)
            mix1 = (jnp.exp(jnp.where(causal, col1 - row1, NEG)) * cross).astype(BF16)
            zero = jnp.zeros_like(stepped_b)
            pairs = jnp.concatenate(
                [jnp.where(low_half, stepped_b, zero), jnp.where(low_half, zero, stepped_b)], axis=0)
            local = mm(jnp.concatenate([mix0, mix1], axis=1), pairs)
            both = jnp.where(low_half, col0, col1)
            last = both[Q - 1 : Q, :]
            out = local + carried[:, j * LANES : (j + 1) * LANES] * jnp.exp(both)
            out_ref[:, cols] = out + skip_ref[0:1, cols] * values
            tails_all.append((stepped * jnp.exp(last - both)).astype(BF16))
            lasts.append(jnp.exp(last))
        fresh = mm(b_cols, jnp.concatenate(tails_all, axis=1))
        cols = pl.ds(base, span)
        state[:, cols] = state[:, cols] * jnp.concatenate(lasts, axis=1) + fresh
        return carry

    lax.fori_loop(0, groups, group, 0)


def run_scan_forward(proj, cw, cb, vec, skip_cols, inner, nstate, groups, per):
    length = proj.shape[0]
    blocks = length // Q
    conv = inner + 2 * nstate
    whole = lambda shape: pl.BlockSpec(shape, lambda i: (0, 0))
    rows = lambda width: pl.BlockSpec((Q, width), lambda i: (i, 0))
    return pl.pallas_call(
        functools.partial(scan_forward, inner=inner, nstate=nstate, groups=groups, per=per),
        grid=(blocks,),
        in_specs=[rows(proj.shape[1]), whole(cw.shape), whole(cb.shape), whole(vec.shape), whole(skip_cols.shape)],
        out_specs=[rows(inner), rows(conv), pl.BlockSpec((nstate, inner), lambda i: (i, 0))],
        out_shape=[
            jax.ShapeDtypeStruct((length, inner), F32),
            jax.ShapeDtypeStruct((length, conv), F32),
            jax.ShapeDtypeStruct((blocks * nstate, inner), BF16),
        ],
        scratch_shapes=[
            pltpu.VMEM((Q + 8, conv), F32),
            pltpu.VMEM((Q, conv), F32),
            pltpu.VMEM((nstate, inner), F32),
            pltpu.VMEM((groups, Q, LANES), F32),
            pltpu.VMEM((groups, Q, LANES), F32),
            pltpu.VMEM((LANES, Q), F32),
        ],
        compiler_params=pltpu.CompilerParams(vmem_limit_bytes=60 << 20),
        cost_estimate=pl.CostEstimate(flops=12_000_000_000, bytes_accessed=60_000_000, transcendentals=20_000_000),
        name="scan_forward",
    )(proj, cw, cb, vec, skip_cols)


def piece_copies(place_ref, pieces, refs, target, sems):
    copies = []
    for index, (start, half, size, lane) in enumerate(pieces):
        rows, cols = refs[index].shape
        if half is not None:
            start = pl.multiple_of(start + jnp.bitwise_xor(place_ref[1], half) * size, 16)
        window = target.at[pl.ds(start, rows), pl.ds(lane, cols)]
        copies.append(pltpu.make_async_copy(refs[index], window, sems.at[index]))
    return copies


def load_pieces(*args):
    for copy in piece_copies(*args):
        copy.start()


def wait_pieces(*args):
    for copy in piece_copies(*args):
        copy.wait()


def columns_of(place_ref, position, order, width):
    return pl.ds(pl.multiple_of(jnp.bitwise_xor(place_ref[0], order[position]) * width, LANES), width)


def project_in(place_ref, tok_ref, gain_ref, *rest, pieces, order):
    refs, (normed_ref, proj_ref, weight, sems) = rest[: len(pieces)], rest[len(pieces) :]
    first = pl.program_id(0) == 0

    @pl.when(first)
    def _():
        load_pieces(place_ref, pieces, refs, weight, sems)

    width = tok_ref.shape[1] // len(order)
    tok = tok_ref[...].astype(F32)
    scale = lax.rsqrt(jnp.mean(tok * tok, axis=1, keepdims=True) + EPS)
    for position in range(len(order)):
        cols = columns_of(place_ref, position, order, width)
        value = tok_ref[:, cols].astype(F32) * scale * gain_ref[0:1, cols]
        normed_ref[:, position * width : (position + 1) * width] = value.astype(BF16)

    @pl.when(first)
    def _():
        wait_pieces(place_ref, pieces, refs, weight, sems)

    total = proj_ref.shape[1]
    step = 384
    for low in range(0, total, step):
        proj_ref[:, low : low + step] = mm_t(normed_ref[...], weight[low : low + step, :])


def grid_of(grid, in_specs, out_specs, scratch):
    return pltpu.PrefetchScalarGridSpec(
        num_scalar_prefetch=1, grid=grid, in_specs=in_specs, out_specs=out_specs, scratch_shapes=scratch)


def anywhere(count):
    return [pl.BlockSpec(memory_space=pl.ANY)] * count


def row_block(block, width):
    return pl.BlockSpec((block, width), lambda i, s: (i, 0))


def fixed(shape):
    return pl.BlockSpec(shape, lambda i, s: (0,) * len(shape))


def run_project_in(place, tok, gain, weight, total, order, block=256):
    pieces, arrays = weight
    length, width = tok.shape
    return pl.pallas_call(
        functools.partial(project_in, pieces=pieces, order=order),
        grid_spec=grid_of(
            (length // block,),
            [row_block(block, width), fixed(gain.shape)] + anywhere(len(pieces)),
            [row_block(block, width), row_block(block, total)],
            [pltpu.VMEM((total, width), BF16), pltpu.SemaphoreType.DMA((len(pieces),))],
        ),
        out_shape=[jax.ShapeDtypeStruct((length, width), BF16), jax.ShapeDtypeStruct((length, total), F32)],
        compiler_params=pltpu.CompilerParams(vmem_limit_bytes=50 << 20),
        cost_estimate=pl.CostEstimate(flops=20_000_000_000, bytes_accessed=30_000_000, transcendentals=1000),
        name="project_in",
    )(place, tok, gain, *arrays)


def gating(place_ref, normed_ref, cot_ref, scan_ref, gain_ref, *rest, wg_pieces, ow_pieces, order):
    n_g, n_o = len(wg_pieces), len(ow_pieces)
    wg_refs, ow_refs = rest[:n_g], rest[n_g : n_g + n_o]
    (mixed_ref, dscan_ref, dgate_ref, dgain_ref, wg, ow, gate_s, gated_s, scaled_s,
     g_sems, o_sems) = rest[n_g + n_o :]
    inner = wg.shape[0]
    parts = len(order)
    width = inner // parts
    first = pl.program_id(0) == 0

    @pl.when(first)
    def _():
        load_pieces(place_ref, wg_pieces, wg_refs, wg, g_sems)
        load_pieces(place_ref, ow_pieces, ow_refs, ow, o_sems)
        dgain_ref[...] = jnp.zeros_like(dgain_ref)
        wait_pieces(place_ref, wg_pieces, wg_refs, wg, g_sems)

    def fold(v):
        total = v[:, 0:LANES]
        for low in range(LANES, v.shape[1], LANES):
            total = total + v[:, low : low + LANES]
        return total

    power = None
    for p in range(parts):
        cols = slice(p * width, (p + 1) * width)
        gate = mm_t(normed_ref[...], wg[cols, :])
        gated = scan_ref[:, cols] * (gate * sigmoid(gate))
        gate_s[:, cols] = gate
        gated_s[:, cols] = gated
        term = fold(gated * gated)
        power = term if power is None else power + term
    scale = lax.rsqrt(jnp.sum(power, axis=1, keepdims=True) / inner + EPS)

    @pl.when(first)
    def _():
        wait_pieces(place_ref, ow_pieces, ow_refs, ow, o_sems)

    match = None
    for p in range(parts):
        true = columns_of(place_ref, p, order, width)
        rows = slice(p * width, (p + 1) * width)
        grad = mm_t(cot_ref[...], ow[rows, :])
        gated = gated_s[:, true]
        gain = gain_ref[0:1, true]
        unit = gated * scale
        mixed_ref[:, rows] = (unit * gain).astype(BF16)
        dgain_ref[0:1, true] += jnp.sum(grad * unit, axis=0, keepdims=True)
        scaled = grad * gain
        scaled_s[:, true] = scaled
        term = fold(scaled * gated)
        match = term if match is None else match + term
    pull = jnp.sum(match, axis=1, keepdims=True) * (scale * scale) / inner
    for p in range(parts):
        cols = slice(p * width, (p + 1) * width)
        gate = gate_s[:, cols]
        sig = sigmoid(gate)
        silu = gate * sig
        dgated = scale * (scaled_s[:, cols] - gated_s[:, cols] * pull)
        dscan_ref[:, cols] = dgated * silu
        dgate_ref[:, cols] = (dgated * scan_ref[:, cols] * (sig + silu * (1.0 - sig))).astype(BF16)


def run_gating(place, normed, gate_weight, out_weight, cot, scan_out, gain, order, block=256):
    wg_pieces, wg_arrays = gate_weight
    ow_pieces, ow_arrays = out_weight
    length, width = normed.shape
    inner = scan_out.shape[1]
    return pl.pallas_call(
        functools.partial(gating, wg_pieces=wg_pieces, ow_pieces=ow_pieces, order=order),
        grid_spec=grid_of(
            (length // block,),
            [row_block(block, width), row_block(block, width), row_block(block, inner), fixed((1, inner))]
            + anywhere(len(wg_pieces) + len(ow_pieces)),
            [row_block(block, inner), row_block(block, inner), row_block(block, inner), fixed((1, inner))],
            [pltpu.VMEM((inner, width), BF16), pltpu.VMEM((inner, width), BF16)]
            + [pltpu.VMEM((block, inner), F32)] * 3
            + [pltpu.SemaphoreType.DMA((len(wg_pieces),)), pltpu.SemaphoreType.DMA((len(ow_pieces),))],
        ),
        out_shape=[
            jax.ShapeDtypeStruct((length, inner), BF16),
            jax.ShapeDtypeStruct((length, inner), F32),
            jax.ShapeDtypeStruct((length, inner), BF16),
            jax.ShapeDtypeStruct((1, inner), F32),
        ],
        compiler_params=pltpu.CompilerParams(vmem_limit_bytes=62 << 20),
        cost_estimate=pl.CostEstimate(flops=40_000_000_000, bytes_accessed=70_000_000, transcendentals=10_000_000),
        name="gating",
    )(place, normed, cot, scan_out, gain, *wg_arrays, *ow_arrays)


def gate_back(place_ref, dgate_ref, *rest, pieces):
    refs, (grad_ref, weight, sems) = rest[: len(pieces)], rest[len(pieces) :]

    @pl.when(pl.program_id(0) == 0)
    def _():
        load_pieces(place_ref, pieces, refs, weight, sems)
        wait_pieces(place_ref, pieces, refs, weight, sems)

    step = 384
    for low in range(0, grad_ref.shape[1], step):
        grad_ref[:, low : low + step] = mm(dgate_ref[...], weight[:, low : low + step])


def run_gate_back(place, dgate, model, weight, block=256):
    pieces, arrays = weight
    length, inner = dgate.shape
    return pl.pallas_call(
        functools.partial(gate_back, pieces=pieces),
        grid_spec=grid_of(
            (length // block,),
            [row_block(block, inner)] + anywhere(len(pieces)),
            row_block(block, model),
            [pltpu.VMEM((inner, model), BF16), pltpu.SemaphoreType.DMA((len(pieces),))],
        ),
        out_shape=jax.ShapeDtypeStruct((length, model), F32),
        compiler_params=pltpu.CompilerParams(vmem_limit_bytes=40 << 20),
        cost_estimate=pl.CostEstimate(flops=16_000_000_000, bytes_accessed=22_000_000, transcendentals=0),
        name="gate_back",
    )(place, dgate, *arrays)


def input_back(place_ref, part_ref, tok_ref, cot_ref, gain_ref, *rest, count, pieces, order):
    dproj_refs, rest = rest[:count], rest[count:]
    refs, (grad_ref, dgain_ref, weight, dn, sems) = rest[: len(pieces)], rest[len(pieces) :]
    first = pl.program_id(0) == 0

    @pl.when(first)
    def _():
        load_pieces(place_ref, pieces, refs, weight, sems)
        dgain_ref[...] = jnp.zeros_like(dgain_ref)
        wait_pieces(place_ref, pieces, refs, weight, sems)

    model = tok_ref.shape[1]
    width = model // len(order)
    tok = tok_ref[...].astype(F32)
    scale = lax.rsqrt(jnp.mean(tok * tok, axis=1, keepdims=True) + EPS)
    match = None
    for position in range(len(order)):
        spot = slice(position * width, (position + 1) * width)
        true = columns_of(place_ref, position, order, width)
        grad, low = part_ref[:, spot], 0
        for ref in dproj_refs:
            grad = grad + mm(ref[...], weight[low : low + ref.shape[1], spot])
            low += ref.shape[1]
        value = tok_ref[:, true].astype(F32)
        dgain_ref[0:1, true] += jnp.sum(grad * (value * scale), axis=0, keepdims=True)
        grad = grad * gain_ref[0:1, true]
        dn[:, spot] = grad
        term = jnp.sum(grad * value, axis=1, keepdims=True)
        match = term if match is None else match + term
    pull = match * (scale * scale * scale) / model
    for position in range(len(order)):
        spot = slice(position * width, (position + 1) * width)
        true = columns_of(place_ref, position, order, width)
        value = tok_ref[:, true].astype(F32)
        grad_ref[:, true] = cot_ref[:, true].astype(F32) + (scale * dn[:, spot] - value * pull)


def run_input_back(place, part, dprojs, tok, cot, gain, weight, order, block=256):
    pieces, arrays = weight
    length, model = tok.shape
    widths = [d.shape[1] for d in dprojs]
    return pl.pallas_call(
        functools.partial(input_back, count=len(dprojs), pieces=pieces, order=order),
        grid_spec=grid_of(
            (length // block,),
            [row_block(block, model), row_block(block, model), row_block(block, model), fixed((1, model))]
            + [row_block(block, w) for w in widths] + anywhere(len(pieces)),
            [row_block(block, model), fixed((1, model))],
            [pltpu.VMEM((sum(widths), model), BF16), pltpu.VMEM((block, model), F32),
             pltpu.SemaphoreType.DMA((len(pieces),))],
        ),
        out_shape=[jax.ShapeDtypeStruct((length, model), F32), jax.ShapeDtypeStruct((1, model), F32)],
        compiler_params=pltpu.CompilerParams(vmem_limit_bytes=50 << 20),
        cost_estimate=pl.CostEstimate(flops=22_000_000_000, bytes_accessed=46_000_000, transcendentals=1000),
        name="input_back",
    )(place, part, tok, cot, gain, *dprojs, *arrays)


def project_out(place_ref, mixed_ref, tok_ref, *rest, pieces):
    refs, (out_ref, weight, sems) = rest[: len(pieces)], rest[len(pieces) :]

    @pl.when(pl.program_id(0) == 0)
    def _():
        load_pieces(place_ref, pieces, refs, weight, sems)
        wait_pieces(place_ref, pieces, refs, weight, sems)

    step = 384
    for low in range(0, out_ref.shape[1], step):
        cols = slice(low, low + step)
        out_ref[:, cols] = (tok_ref[:, cols].astype(F32) + mm(mixed_ref[...], weight[:, cols])).astype(BF16)


def run_project_out(place, mixed, tok, weight, block=256):
    pieces, arrays = weight
    length, model = tok.shape
    inner = mixed.shape[1]
    return pl.pallas_call(
        functools.partial(project_out, pieces=pieces),
        grid_spec=grid_of(
            (length // block,),
            [row_block(block, inner), row_block(block, model)] + anywhere(len(pieces)),
            row_block(block, model),
            [pltpu.VMEM((inner, model), BF16), pltpu.SemaphoreType.DMA((len(pieces),))],
        ),
        out_shape=jax.ShapeDtypeStruct((length, model), BF16),
        compiler_params=pltpu.CompilerParams(vmem_limit_bytes=40 << 20),
        cost_estimate=pl.CostEstimate(flops=14_000_000_000, bytes_accessed=20_000_000, transcendentals=0),
        name="project_out",
    )(place, mixed, tok, *arrays)


def scan_backward(proj_ref, tail_ref, sum_ref, keys_ref, out_ref, dout_ref, start_ref, cw_ref, cwk_ref, vec_ref,
                  skip_ref, pick_ref, *rest, nstate, low, groups, per, begin, last):
    if not begin:
        old_cross_ref, old_keys_ref, old_raw_ref = rest[:3]
        rest = rest[3:]
    dproj_ref, dcw_ref, dcb_ref, dskip_ref, dvec_ref = rest[:5]
    rest = rest[5:]
    if not last:
        cross_ref, keys_ref_out, raw_ref = rest[:3]
        rest = rest[3:]
    dsum, dstate, edge, logs_v, tails_v, steps_v, dt_tab, log_tab, log_rows, dcross, dkeys = rest
    first = pl.program_id(0) == 0
    span_all = groups * per * HEAD
    conv = dsum.shape[1]

    @pl.when(first)
    def _():
        dsum[Q : Q + 8, :] = jnp.zeros((8, conv), F32)
        dstate[...] = jnp.zeros_like(dstate)
        edge[...] = jnp.zeros_like(edge)
        dcw_ref[...] = jnp.zeros_like(dcw_ref)
        dcb_ref[...] = jnp.zeros_like(dcb_ref)
        dskip_ref[...] = jnp.zeros_like(dskip_ref)
        dvec_ref[...] = jnp.zeros_like(dvec_ref)

    raw = tail_ref[:, 2 * nstate : 2 * nstate + LANES] + vec_ref[0:1, :]
    dt = softplus(raw)
    lower = tri_lower()
    rate = vec_ref[1:2, :]
    logs = jnp.dot(lower.astype(F32), dt * rate, precision=HI, preferred_element_type=F32)
    fill_tables(dt, logs, dt_tab, log_tab, log_rows, low, groups, per)
    sum_b = keys_ref[:, 0:nstate]
    sum_c = keys_ref[:, nstate : 2 * nstate]
    sig_b, sig_c = sigmoid(sum_b), sigmoid(sum_c)
    keys_b32, keys_c32 = sum_b * sig_b, sum_c * sig_c
    keys_b, keys_c = keys_b32.astype(BF16), keys_c32.astype(BF16)
    c_cols = jnp.transpose(keys_c32).astype(BF16)
    cross = mm(keys_b, c_cols)
    span = per * HEAD
    low_half = lax.broadcasted_iota(jnp.int32, (Q, LANES), 1) < HEAD
    upper = lax.broadcasted_iota(jnp.int32, (Q, Q), 0) <= lax.broadcasted_iota(jnp.int32, (Q, Q), 1)
    if not begin:
        dcross[...] = old_cross_ref[...]
        dkeys[...] = old_keys_ref[...]
    else:
        dcross[...] = jnp.zeros_like(dcross)
        dkeys[...] = jnp.zeros_like(dkeys)

    def group(g, carry):
        base = pl.multiple_of(g * span, span)
        whole = pl.ds(base, span)
        dts, lgs = dt_tab[g], log_tab[g]
        dstate_b = dstate[:, whole].astype(BF16)
        from_state = mm(keys_b, dstate_b)
        tails_all, outs_all, lasts = [], [], []
        dcr = None
        for j in range(per // 2):
            cols = pl.ds(pl.multiple_of(base + j * LANES, LANES), LANES)
            h = (low + g) * per + 2 * j
            col0, col1 = spread(lgs, 2 * j), spread(lgs, 2 * j + 1)
            row0, row1 = log_rows[pl.ds(h, 1), :], log_rows[pl.ds(h + 1, 1), :]
            total = sum_ref[:, cols]
            sig = sigmoid(total)
            values = total * sig
            step = jnp.where(low_half, spread(dts, 2 * j), spread(dts, 2 * j + 1))
            stepped = values * step
            stepped_b = stepped.astype(BF16)
            dout = dout_ref[:, cols]
            dout_b = dout.astype(BF16)
            decay0 = jnp.exp(jnp.where(upper, row0 - col0, NEG))
            decay1 = jnp.exp(jnp.where(upper, row1 - col1, NEG))
            mix = jnp.concatenate([(decay0 * cross).astype(BF16), (decay1 * cross).astype(BF16)], axis=1)
            zero = jnp.zeros_like(dout_b)
            douts = jnp.concatenate(
                [jnp.where(low_half, dout_b, zero), jnp.where(low_half, zero, dout_b)], axis=0)
            local = mm(mix, douts)
            dmix = mm_t(stepped_b, douts)
            term = dmix[:, 0:Q] * decay0 + dmix[:, Q : 2 * Q] * decay1
            dcr = term if dcr is None else dcr + term
            both = jnp.where(low_half, col0, col1)
            last = both[Q - 1 : Q, :]
            tail = jnp.exp(last - both)
            passed = from_state[:, j * LANES : (j + 1) * LANES] * tail
            dstepped = local + passed
            skip = skip_ref[0:1, cols]
            scan = out_ref[:, cols] - skip * values
            logs_v[:, cols] = dout_b.astype(F32) * scan - stepped_b.astype(F32) * local
            tails_v[:, cols] = stepped * passed
            steps_v[:, cols] = dstepped * values
            dvalues = dstepped * step + dout * skip
            dskip_ref[0:1, cols] += jnp.sum(dout * values, axis=0, keepdims=True)
            dsum[0:Q, cols] = dvalues * (sig + values * (1.0 - sig))
            tails_all.append((stepped * tail).astype(BF16))
            outs_all.append((dout * jnp.exp(both)).astype(BF16))
            lasts.append(jnp.exp(last))
        dcross[...] += dcr
        outs = jnp.concatenate(outs_all, axis=1)
        starts = start_ref[:, whole]
        dkeys[:, nstate : 2 * nstate] += mm_t(outs, starts)
        dkeys[:, 0:nstate] += mm_t(jnp.concatenate(tails_all, axis=1), dstate_b)
        kept = dstate[:, whole] * jnp.concatenate(lasts, axis=1)
        edge[0:1, whole] = jnp.sum(kept * starts.astype(F32), axis=0, keepdims=True)
        dstate[:, whole] = kept + mm(c_cols, outs)
        return carry

    lax.fori_loop(0, groups, group, 0)

    if last:
        dcr = dcross[...]
        exact = lambda u, v: jnp.dot(u, v, precision=HI, preferred_element_type=F32)
        d_b = dkeys[:, 0:nstate] + exact(dcr, keys_c32)
        d_c = dkeys[:, nstate : 2 * nstate] + exact(jnp.transpose(dcr), keys_b32)
        dsum[0:Q, span_all : span_all + nstate] = d_b * (sig_b + keys_b32 * (1.0 - sig_b))
        dsum[0:Q, span_all + nstate : conv] = d_c * (sig_c + keys_c32 * (1.0 - sig_c))
    else:
        cross_ref[...] = dcross[...]
        keys_ref_out[...] = dkeys[...]

    def reduce_heads(v):
        high = v.astype(BF16)
        low = (v - high.astype(F32)).astype(BF16)
        return mm(high, pick_ref[...]) + mm(low, pick_ref[...])

    dlogs = reduce_heads(logs_v[...])
    dtails = reduce_heads(tails_v[...])
    dlogit = (
        jnp.dot(upper.astype(F32), dlogs, precision=HI, preferred_element_type=F32)
        + jnp.dot(1.0 - upper.astype(F32), dtails, precision=HI, preferred_element_type=F32)
        + reduce_heads(edge[...])[0:1, :]
    )
    dstep = reduce_heads(steps_v[...]) + dlogit * rate
    draw = dstep * sigmoid(raw)
    dvec_ref[0:1, :] += jnp.sum(draw, axis=0, keepdims=True)
    dvec_ref[1:2, :] += jnp.sum(dlogit * dt * rate, axis=0, keepdims=True)
    if last:
        dproj_ref[:, conv : conv + LANES] = (draw + old_raw_ref[...]).astype(BF16)
    elif begin:
        raw_ref[...] = draw
    else:
        raw_ref[...] = draw + old_raw_ref[...]

    wide = 256
    for start in range(0, conv, wide):
        part = pl.ds(start, wide)
        if start < span_all:
            source, taps_ref, local = proj_ref, cw_ref, part
        else:
            source, taps_ref, local = tail_ref, cwk_ref, pl.ds(start - span_all, wide)
        taken = source[:, local]
        total = None
        for k in range(4):
            moved = dsum[3 - k : 3 - k + Q, part]
            dcw_ref[k : k + 1, part] += jnp.sum(taken * moved, axis=0, keepdims=True)
            term = taps_ref[k : k + 1, local] * moved
            total = term if total is None else total + term
            if k == 3:
                dcb_ref[0:1, part] += jnp.sum(moved, axis=0, keepdims=True)
        dproj_ref[:, part] = total.astype(BF16)
    dsum[Q : Q + 8, :] = dsum[0:8, :]


def run_scan_backward(proj, sums, scan_out, dscan, starts, cw, vec, skip_cols, pick, inner, nstate, low, groups, per,
                      previous, last):
    length = proj.shape[0]
    blocks = length // Q
    span = groups * per * HEAD
    begin = previous is None
    conv = span + (2 * nstate if last else 0)
    where = low * per * HEAD // span
    whole = lambda shape: pl.BlockSpec(shape, lambda i: (0, 0))
    rows = lambda width, col=0: pl.BlockSpec((Q, width), lambda i: (blocks - 1 - i, col))
    part = lambda height: pl.BlockSpec((height, span), lambda i: (0, where))
    tail = 2 * nstate + LANES
    out_specs = [rows(conv + (LANES if last else 0)), whole((4, conv)), whole((1, conv)), whole((1, span)),
                 whole((8, LANES))]
    out_shape = [
        jax.ShapeDtypeStruct((length, conv + (LANES if last else 0)), BF16),
        jax.ShapeDtypeStruct((4, conv), F32),
        jax.ShapeDtypeStruct((1, conv), F32),
        jax.ShapeDtypeStruct((1, span), F32),
        jax.ShapeDtypeStruct((8, LANES), F32),
    ]
    carried = [rows(Q), rows(2 * nstate), rows(LANES)]
    if not last:
        out_specs += carried
        out_shape += [jax.ShapeDtypeStruct((length, w), F32) for w in (Q, 2 * nstate, LANES)]
    return pl.pallas_call(
        functools.partial(scan_backward, nstate=nstate, low=low, groups=groups, per=per, begin=begin, last=last),
        grid=(blocks,),
        in_specs=[
            rows(span, where), rows(tail, inner // tail), rows(span, where), rows(2 * nstate, inner // (2 * nstate)),
            rows(span, where), rows(span, where),
            pl.BlockSpec((nstate, span), lambda i: (blocks - 1 - i, where)),
            part(4), pl.BlockSpec((4, 2 * nstate), lambda i: (0, inner // (2 * nstate))),
            whole(vec.shape), part(1), pl.BlockSpec((span, LANES), lambda i: (where, 0)),
        ] + ([] if begin else carried),
        out_specs=out_specs,
        out_shape=out_shape,
        scratch_shapes=[
            pltpu.VMEM((Q + 8, conv), F32),
            pltpu.VMEM((nstate, span), F32),
            pltpu.VMEM((8, span), F32),
            pltpu.VMEM((Q, span), F32),
            pltpu.VMEM((Q, span), F32),
            pltpu.VMEM((Q, span), F32),
            pltpu.VMEM((groups, Q, LANES), F32),
            pltpu.VMEM((groups, Q, LANES), F32),
            pltpu.VMEM((LANES, Q), F32),
            pltpu.VMEM((Q, Q), F32),
            pltpu.VMEM((Q, 2 * nstate), F32),
        ],
        compiler_params=pltpu.CompilerParams(vmem_limit_bytes=50 << 20),
        cost_estimate=pl.CostEstimate(flops=40_000_000_000, bytes_accessed=40_000_000, transcendentals=15_000_000),
        name="scan_backward",
    )(proj, proj, sums, sums, scan_out, dscan, starts, cw, cw, vec, skip_cols, pick, *(previous or ()))


def bits_of(size):
    return [1 << b for b in range(size.bit_length() - 1)]


def swap(value, axis, bit, size):
    return lax.ppermute(value, axis, [(i, i ^ bit) for i in range(size)])


def after(value, *deps):
    return lax.optimization_barrier((value,) + deps)[0] if deps else value


def order_of(size):
    flipped = []
    for index in range(size):
        value = 0
        for low, high in zip(bits_of(size), reversed(bits_of(size))):
            value |= high if index & low else 0
        flipped.append(value)
    return flipped


class Gather:
    def __init__(self, shard, order, rep_index, groups, copies, lanes, chunks):
        self.order, self.groups, self.copies = order, groups, copies
        self.size = shard.shape
        self.lanes = lanes
        self.half = shard.shape[0] // 2
        self.rows = self.half // chunks
        self.shard = shard
        parity = rep_index & 1
        self.mine = [lax.dynamic_slice_in_dim(shard, parity * self.half + c * self.rows, self.rows, 0)
                     for c in range(chunks)]
        self.there, self.across = [None] * chunks, [None] * chunks
        self.own, self.early = None, []

    def far(self, chunk, *deps):
        value = after(self.mine[chunk], *deps)
        self.there[chunk] = swap(value, "shard", 2, self.groups)

    def whole(self, *deps):
        self.there = [swap(after(self.shard, *deps), "shard", 2, self.groups)]
        self.across = []

    def side(self, chunk):
        self.across[chunk] = swap(self.there[chunk], "rep", 1, self.copies)

    def core(self, value, *deps):
        return swap(after(value, *deps), "shard", 1, self.groups)

    def finish(self, *deps):
        own = self.own if self.own is not None else self.core(self.shard)
        have = {0: [(0, None, 0, self.shard)], 1: [(0, None, 0, own)]}
        if self.across:
            have[2] = [(c * self.rows, h, self.half, v) for h, vs in ((0, self.there), (1, self.across))
                       for c, v in enumerate(vs)]
        else:
            have[2] = [(0, None, 0, self.there[0])]
        have[3] = []
        for index, (row, half, size, value) in enumerate(have[2]):
            if index < len(self.early):
                partner = self.early[index]
            else:
                partner = self.core(value, *(deps if index == len(have[2]) - 1 else ()))
            have[3].append((row, half, size, partner))
        pieces, arrays = [], []
        for position, source in enumerate(self.order):
            for row, half, size, value in have[source]:
                if self.lanes:
                    pieces.append((row, half, size, position * self.size[1]))
                else:
                    pieces.append((row + position * self.size[0], half, size, 0))
                arrays.append(value)
        return tuple(pieces), tuple(arrays)


class Total:
    def __init__(self, kept, sent, axis, rep_index, groups, copies, narrow=False):
        self.axis, self.rep_index = axis, rep_index
        self.sizes = {"shard": groups, "rep": copies}
        self.stages = [("shard", index, 1) for index in range(len(bits_of(groups)))]
        count = len(bits_of(copies))
        over = [("rep", 0, 1)] + [("rep", index, min(2, count - index)) for index in range(1, count, 2)]
        self.stages += over
        self.back = list(reversed(over))
        if narrow:
            self.back = [(name, shift + bit, 1) for name, shift, width in self.back for bit in range(width)]
        self.value, self.out = kept, [sent]
        self.fly()

    @classmethod
    def join(cls, chains):
        first = chains[0]
        new = object.__new__(cls)
        new.axis, new.rep_index, new.sizes = first.axis, first.rep_index, first.sizes
        new.stages, new.back = first.stages, first.back
        new.value = jnp.concatenate([v.value for v in chains])
        new.coming = [jnp.concatenate(v) for v in zip(*(c.coming for c in chains))]
        return new

    def fly(self):
        name, shift, _ = self.stages[0]
        self.coming = [swap(v, name, (k + 1) << shift, self.sizes[name]) for k, v in enumerate(self.out)]

    def done(self):
        return not self.stages and not self.back

    def step(self, *deps):
        coming = [after(v, *deps) for v in self.coming]
        if not self.stages:
            return self.widen(coming)
        self.stages.pop(0)
        terms = [self.value] + coming
        if not self.stages:
            self.value = sum(v.astype(F32) for v in terms).astype(BF16)
            self.fly_back()
            return [self.value]
        name, shift, width = self.stages[0]
        parts = 1 << width
        axis = self.axis if name == "shard" else 0
        size = self.value.shape[axis] // parts
        mine = 0 if name == "shard" else (self.rep_index >> shift) & (parts - 1)
        cut = lambda start: sum(lax.dynamic_slice_in_dim(v, start, size, axis).astype(F32) for v in terms)
        self.out = [cut((mine ^ k) * size).astype(BF16) for k in range(1, parts)]
        self.value = cut(mine * size)
        self.fly()
        return self.out

    def fly_back(self):
        name, shift, width = self.back[0]
        self.coming = [swap(self.value, name, k << shift, self.sizes[name]) for k in range(1, 1 << width)]

    def widen(self, coming):
        name, shift, width = self.back.pop(0)
        parts = [self.value] + coming
        for bit in range(width):
            turn = ((self.rep_index >> (shift + bit)) & 1) != 0
            parts = [jnp.where(turn, parts[k ^ (1 << bit)], parts[k]) for k in range(len(parts))]
        if not self.back:
            self.value = [v.astype(F32) for v in parts]
            return self.value
        self.value = jnp.concatenate(parts)
        self.fly_back()
        return [self.value]


def outer(left, right):
    return lax.dot_general(left, right, (((0,), (0,)), ((), ())), preferred_element_type=F32).astype(BF16)


def on_device(groups, copies, tokens, norm_gain, in_weight, conv_weight, conv_bias, dt_bias, a_log, skip, gate_gain,
              out_weight, cotangent):
    if tokens.shape[0] != 1 or groups != 4:
        raise ValueError("unexpected sizes")
    order = order_of(groups)
    shard_index = lax.axis_index("shard")
    rep_index = lax.axis_index("rep")
    tok, cot = tokens[0], cotangent[0]
    inner = gate_gain.shape[0] * groups
    conv = conv_bias.shape[0] * groups
    heads = dt_bias.shape[0] * groups
    nstate = (conv - inner) // 2
    model = tok.shape[1]
    taps = conv_weight.shape[0]
    outputs_all = in_weight.shape[1]
    place = jnp.stack([shard_index, rep_index & 1]).astype(jnp.int32)

    turned = in_weight.T
    total = conv + LANES
    conv_part = jnp.pad(turned[inner:], ((0, total + inner - outputs_all), (0, 0)))
    make = lambda shard, lanes, chunks: Gather(shard, order, rep_index, groups, copies, lanes, chunks)
    wc = make(conv_part, True, 2)
    wg = make(turned[:inner], True, 1)
    ow = make(out_weight, False, 1)

    small = (norm_gain, conv_bias, dt_bias, a_log, skip, gate_gain, conv_weight)
    packed = jnp.concatenate([v.reshape(-1) for v in small])
    wc.far(0)
    wc.far(1)
    wc.side(0)
    wc.side(1)
    wc.own = wc.core(wc.shard)
    wc.early = [wc.core(wc.there[0])]
    wg.far(0, wc.there[1], wc.own, wc.early[0])
    ow.whole(wc.there[1], wc.own, wc.early[0])
    rows = [packed, swap(packed, "shard", 1, groups)]
    far = swap(packed, "shard", 2, groups)
    rows += [far, swap(far, "shard", 1, groups)]
    for bit in bits_of(groups):
        turn = (shard_index & bit) != 0
        rows = [jnp.where(turn, rows[j ^ bit], rows[j]) for j in range(groups)]
    everyone = jnp.stack(rows).astype(F32)
    parts, low = [], 0
    for v in small:
        parts.append(everyone[:, low : low + v.size])
        low += v.size
    gain, cb, db, al, sk, gg = (v.reshape(-1) for v in parts[:6])
    cw = parts[6].reshape(groups, taps, -1).transpose(1, 0, 2).reshape(taps, conv)
    gain, cb, gg = gain[None], cb[None], gg[None]
    vec = jnp.pad(jnp.stack([db, -jnp.exp(al)]), ((0, 6), (0, LANES - heads)))
    skip_cols = jnp.repeat(sk, inner // heads)[None]
    pick = (jnp.arange(inner)[:, None] // (inner // heads) == jnp.arange(LANES)[None]).astype(BF16)

    wc = wc.finish(gain, cb, gg, cw, vec, skip_cols, pick)
    normed, proj = run_project_in(place, tok, gain, wc, total, order)
    wg.there[0] = after(wg.there[0], normed)
    wg.side(0)
    proj = after(proj, wg.there[0])
    per = 8
    scan_out, sums, starts = run_scan_forward(proj, cw, cb, vec, skip_cols, inner, nstate, heads // per, per)
    wg, ow = wg.finish(scan_out), ow.finish(scan_out)
    mixed, dscan, dgate, dgg = run_gating(place, normed, wg, ow, cot, scan_out, gg, order)

    chain = lambda kept, sent, axis, *way: Total(kept, sent, axis, rep_index, groups, copies, *way)
    half = inner // 2
    out_sent = outer(mixed[:, half:], cot)
    o = chain(outer(mixed[:, :half], cot), out_sent, 0, True)
    half = model // 2
    left, right = normed[:, :half], normed[:, half:]
    gate_sent = outer(dgate, right)
    marks = o.step(o.value)
    g = chain(outer(after(dgate, *marks), left), gate_sent, 1)
    marks = marks + g.step(g.value)

    blocks = heads // per
    cuts = [0, blocks // 2, blocks]
    chains, grads, carried = [o, g], [], None
    for index in range(2):
        low, high = cuts[index], cuts[index + 1]
        found = run_scan_backward(
            proj, sums, scan_out, after(dscan, *marks), starts, cw, vec, skip_cols, pick, inner, nstate, low,
            high - low, per, carried, index == 1)
        grads.append(found[:5])
        carried = tuple(found[5:])
        dproj, marks = found[0], []
        if index == 1:
            marks = o.step(dproj)
            marks = marks + g.step(dproj, *marks) + chains[2].coming
        dproj = after(dproj, *marks)
        sent = outer(dproj, right)
        kept = outer(dproj, left)
        new = chain(kept, sent, 1)
        chains.append(new)
        if index == 0:
            marks = o.step(kept)
        marks = marks + new.step(kept, *marks)
    a, c = chains[2:]

    part = run_gate_back(place, after(dgate, *marks), model, wg)
    marks = g.step(part)
    marks = marks + o.step(part, *marks)
    output = run_project_out(place, after(mixed, *marks), tok, ow)
    abc = Total.join([a, c])
    marks = g.step(output)
    marks = marks + abc.step(output, *marks)
    marks = marks + o.step(output, *marks)
    input_grad, dgain = run_input_back(place, after(part, *marks), [v[0] for v in grads], tok, cot, gain, wc, order)

    dcw = jnp.concatenate([v[1] for v in grads], axis=1)
    dcb = jnp.concatenate([v[2][0] for v in grads])
    dskip = jnp.concatenate([v[3][0] for v in grads]).reshape(heads, -1).sum(1)
    dvec = sum(v[4] for v in grads)
    pieces = (dcb, dvec[0, :heads], dvec[1, :heads], dskip, dgg[0])
    flat = jnp.concatenate([v.reshape(groups, -1) for v in pieces]
                           + [dcw.reshape(taps, groups, -1).transpose(1, 0, 2).reshape(groups, -1)], axis=1)
    flat = jnp.concatenate([dgain[0].reshape(groups, -1), flat], axis=1)
    marks = abc.step(dgain, *g.coming)
    marks = marks + g.step(*marks)
    flat = after(flat, *marks)
    for axis, size in (("shard", groups), ("rep", copies)):
        for bit in bits_of(size):
            flat = flat + swap(flat, axis, bit, size)
    for old in (abc, g, o):
        while not old.done():
            old.step()

    in_total = jnp.concatenate(g.value + abc.value)[:outputs_all].T
    out_total = jnp.concatenate(o.value)

    own = lax.dynamic_slice_in_dim(flat, shard_index, 1, 0)[0]
    shares, low = [], 0
    for v in small:
        shares.append(own[low : low + v.size].reshape(v.shape))
        low += v.size
    d_gain, d_cb, d_db, d_al, d_sk, d_gg, d_cw = shares
    return (output[None], input_grad[None], d_gain, in_total, d_cw, d_cb, d_db, d_al, d_sk, d_gg, out_total)


def solution(mesh):
    whole = P(("shard", "rep"), None, None)
    row, matrix, cols = P("shard"), P("shard", None), P(None, "shard")
    return jax.shard_map(
        functools.partial(on_device, mesh.shape["shard"], mesh.shape["rep"]),
        mesh=mesh,
        in_specs=(whole, row, matrix, cols, row, row, row, row, row, matrix, whole),
        out_specs=(whole, whole, row, matrix, cols, row, row, row, row, row, matrix),
        check_vma=False,
    )
```

```python
import functools

import jax
import jax.numpy as jnp
from jax import lax
from jax.experimental import pallas as pl
from jax.experimental.pallas import tpu as pltpu
from jax.sharding import PartitionSpec as P

Q = 128
LANES = 128
HEAD = 64
EPS = 1e-05
F32 = jnp.float32
BF16 = jnp.bfloat16
HI = lax.Precision.HIGHEST
NEG = -1e30


def mm(a, b):
    return jnp.dot(a, b, preferred_element_type=F32)


def mm_t(a, b):
    return lax.dot_general(a, b, (((1,), (1,)), ((), ())), preferred_element_type=F32)


def softplus(v):
    return jnp.maximum(v, 0.0) + jnp.log1p(jnp.exp(-jnp.abs(v)))


def sigmoid(v):
    return 1.0 / (1.0 + jnp.exp(-v))


def tri_lower():
    rows = lax.broadcasted_iota(jnp.int32, (Q, Q), 0)
    cols = lax.broadcasted_iota(jnp.int32, (Q, Q), 1)
    return rows >= cols


def spread(table, lane):
    return jnp.broadcast_to(table[:, lane : lane + 1], (Q, LANES))


def fill_tables(dt, logs, dt_tab, log_tab, log_rows, low, groups, per):
    log_rows[...] = jnp.transpose(logs)
    for g in range(groups):
        shift = (LANES - (low + g) * per) % LANES
        dt_tab[g] = pltpu.roll(dt, shift, 1) if shift else dt
        log_tab[g] = pltpu.roll(logs, shift, 1) if shift else logs


def scan_forward(proj_ref, cw_ref, cb_ref, vec_ref, skip_ref, out_ref, sum_ref, start_ref,
                 shifted, act, state, dt_tab, log_tab, log_rows, *, inner, nstate, groups, per):
    first = pl.program_id(0) == 0
    conv = inner + 2 * nstate

    @pl.when(first)
    def _():
        shifted[0:8, :] = jnp.zeros((8, conv), F32)
        state[...] = jnp.zeros_like(state)

    shifted[8 : 8 + Q, :] = proj_ref[:, 0:conv]
    wide = 256
    for low in range(0, conv, wide):
        part = pl.ds(low, wide)
        total = cb_ref[0:1, part] + cw_ref[0:1, part] * shifted[5 : 5 + Q, part]
        for k in range(1, 4):
            total = total + cw_ref[k : k + 1, part] * shifted[5 + k : 5 + k + Q, part]
        sum_ref[:, part] = total
        act[:, part] = total * sigmoid(total)
    shifted[0:8, :] = shifted[Q : Q + 8, :]

    dt = softplus(proj_ref[:, conv : conv + LANES] + vec_ref[0:1, :])
    causal = tri_lower()
    logs = jnp.dot(causal.astype(F32), dt * vec_ref[1:2, :], precision=HI, preferred_element_type=F32)
    fill_tables(dt, logs, dt_tab, log_tab, log_rows, 0, groups, per)
    keys_b = act[:, inner : inner + nstate]
    keys_c = act[:, inner + nstate : conv].astype(BF16)
    b_cols = jnp.transpose(keys_b).astype(BF16)
    cross = mm(keys_c, b_cols)
    start_ref[...] = state[...].astype(BF16)
    span = per * HEAD
    low_half = lax.broadcasted_iota(jnp.int32, (Q, LANES), 1) < HEAD

    def group(g, carry):
        base = pl.multiple_of(g * span, span)
        dts, lgs = dt_tab[g], log_tab[g]
        carried = mm(keys_c, start_ref[:, pl.ds(base, span)])
        tails_all = []
        lasts = []
        for j in range(per // 2):
            cols = pl.ds(pl.multiple_of(base + j * LANES, LANES), LANES)
            h = g * per + 2 * j
            col0, col1 = spread(lgs, 2 * j), spread(lgs, 2 * j + 1)
            row0, row1 = log_rows[pl.ds(h, 1), :], log_rows[pl.ds(h + 1, 1), :]
            values = act[:, cols]
            stepped = (values * jnp.where(low_half, spread(dts, 2 * j), spread(dts, 2 * j + 1)))
            stepped_b = stepped.astype(BF16)
            mix0 = (jnp.exp(jnp.where(causal, col0 - row0, NEG)) * cross).astype(BF16)
            mix1 = (jnp.exp(jnp.where(causal, col1 - row1, NEG)) * cross).astype(BF16)
            zero = jnp.zeros_like(stepped_b)
            pairs = jnp.concatenate(
                [jnp.where(low_half, stepped_b, zero), jnp.where(low_half, zero, stepped_b)], axis=0)
            local = mm(jnp.concatenate([mix0, mix1], axis=1), pairs)
            both = jnp.where(low_half, col0, col1)
            last = both[Q - 1 : Q, :]
            out = local + carried[:, j * LANES : (j + 1) * LANES] * jnp.exp(both)
            out_ref[:, cols] = out + skip_ref[0:1, cols] * values
            tails_all.append((stepped * jnp.exp(last - both)).astype(BF16))
            lasts.append(jnp.exp(last))
        fresh = mm(b_cols, jnp.concatenate(tails_all, axis=1))
        cols = pl.ds(base, span)
        state[:, cols] = state[:, cols] * jnp.concatenate(lasts, axis=1) + fresh
        return carry

    lax.fori_loop(0, groups, group, 0)


def run_scan_forward(proj, cw, cb, vec, skip_cols, inner, nstate, groups, per):
    length = proj.shape[0]
    blocks = length // Q
    conv = inner + 2 * nstate
    whole = lambda shape: pl.BlockSpec(shape, lambda i: (0, 0))
    rows = lambda width: pl.BlockSpec((Q, width), lambda i: (i, 0))
    return pl.pallas_call(
        functools.partial(scan_forward, inner=inner, nstate=nstate, groups=groups, per=per),
        grid=(blocks,),
        in_specs=[rows(proj.shape[1]), whole(cw.shape), whole(cb.shape), whole(vec.shape), whole(skip_cols.shape)],
        out_specs=[rows(inner), rows(conv), pl.BlockSpec((nstate, inner), lambda i: (i, 0))],
        out_shape=[
            jax.ShapeDtypeStruct((length, inner), F32),
            jax.ShapeDtypeStruct((length, conv), F32),
            jax.ShapeDtypeStruct((blocks * nstate, inner), BF16),
        ],
        scratch_shapes=[
            pltpu.VMEM((Q + 8, conv), F32),
            pltpu.VMEM((Q, conv), F32),
            pltpu.VMEM((nstate, inner), F32),
            pltpu.VMEM((groups, Q, LANES), F32),
            pltpu.VMEM((groups, Q, LANES), F32),
            pltpu.VMEM((LANES, Q), F32),
        ],
        compiler_params=pltpu.CompilerParams(vmem_limit_bytes=60 << 20),
        cost_estimate=pl.CostEstimate(flops=12_000_000_000, bytes_accessed=60_000_000, transcendentals=20_000_000),
        name="scan_forward",
    )(proj, cw, cb, vec, skip_cols)


def piece_copies(place_ref, pieces, refs, target, sems):
    copies = []
    for index, (start, half, size, lane) in enumerate(pieces):
        rows, cols = refs[index].shape
        if half is not None:
            start = pl.multiple_of(start + jnp.bitwise_xor(place_ref[1], half) * size, 16)
        window = target.at[pl.ds(start, rows), pl.ds(lane, cols)]
        copies.append(pltpu.make_async_copy(refs[index], window, sems.at[index]))
    return copies


def load_pieces(*args):
    for copy in piece_copies(*args):
        copy.start()


def wait_pieces(*args):
    for copy in piece_copies(*args):
        copy.wait()


def columns_of(place_ref, position, order, width):
    return pl.ds(pl.multiple_of(jnp.bitwise_xor(place_ref[0], order[position]) * width, LANES), width)


def project_in(place_ref, tok_ref, gain_ref, *rest, pieces, order):
    refs, (normed_ref, proj_ref, weight, sems) = rest[: len(pieces)], rest[len(pieces) :]
    first = pl.program_id(0) == 0

    @pl.when(first)
    def _():
        load_pieces(place_ref, pieces, refs, weight, sems)

    width = tok_ref.shape[1] // len(order)
    tok = tok_ref[...].astype(F32)
    scale = lax.rsqrt(jnp.mean(tok * tok, axis=1, keepdims=True) + EPS)
    for position in range(len(order)):
        cols = columns_of(place_ref, position, order, width)
        value = tok_ref[:, cols].astype(F32) * scale * gain_ref[0:1, cols]
        normed_ref[:, position * width : (position + 1) * width] = value.astype(BF16)

    @pl.when(first)
    def _():
        wait_pieces(place_ref, pieces, refs, weight, sems)

    total = proj_ref.shape[1]
    step = 384
    for low in range(0, total, step):
        proj_ref[:, low : low + step] = mm_t(normed_ref[...], weight[low : low + step, :])


def grid_of(grid, in_specs, out_specs, scratch):
    return pltpu.PrefetchScalarGridSpec(
        num_scalar_prefetch=1, grid=grid, in_specs=in_specs, out_specs=out_specs, scratch_shapes=scratch)


def anywhere(count):
    return [pl.BlockSpec(memory_space=pl.ANY)] * count


def row_block(block, width):
    return pl.BlockSpec((block, width), lambda i, s: (i, 0))


def fixed(shape):
    return pl.BlockSpec(shape, lambda i, s: (0,) * len(shape))


def run_project_in(place, tok, gain, weight, total, order, block=256):
    pieces, arrays = weight
    length, width = tok.shape
    return pl.pallas_call(
        functools.partial(project_in, pieces=pieces, order=order),
        grid_spec=grid_of(
            (length // block,),
            [row_block(block, width), fixed(gain.shape)] + anywhere(len(pieces)),
            [row_block(block, width), row_block(block, total)],
            [pltpu.VMEM((total, width), BF16), pltpu.SemaphoreType.DMA((len(pieces),))],
        ),
        out_shape=[jax.ShapeDtypeStruct((length, width), BF16), jax.ShapeDtypeStruct((length, total), F32)],
        compiler_params=pltpu.CompilerParams(vmem_limit_bytes=50 << 20),
        cost_estimate=pl.CostEstimate(flops=20_000_000_000, bytes_accessed=30_000_000, transcendentals=1000),
        name="project_in",
    )(place, tok, gain, *arrays)


def gating(place_ref, normed_ref, cot_ref, scan_ref, gain_ref, *rest, wg_pieces, ow_pieces, order):
    n_g, n_o = len(wg_pieces), len(ow_pieces)
    wg_refs, ow_refs = rest[:n_g], rest[n_g : n_g + n_o]
    (mixed_ref, dscan_ref, dgate_ref, dgain_ref, wg, ow, gate_s, gated_s, scaled_s,
     g_sems, o_sems) = rest[n_g + n_o :]
    inner = wg.shape[0]
    parts = len(order)
    width = inner // parts
    first = pl.program_id(0) == 0

    @pl.when(first)
    def _():
        load_pieces(place_ref, wg_pieces, wg_refs, wg, g_sems)
        load_pieces(place_ref, ow_pieces, ow_refs, ow, o_sems)
        dgain_ref[...] = jnp.zeros_like(dgain_ref)
        wait_pieces(place_ref, wg_pieces, wg_refs, wg, g_sems)

    def fold(v):
        total = v[:, 0:LANES]
        for low in range(LANES, v.shape[1], LANES):
            total = total + v[:, low : low + LANES]
        return total

    power = None
    for p in range(parts):
        cols = slice(p * width, (p + 1) * width)
        gate = mm_t(normed_ref[...], wg[cols, :])
        gated = scan_ref[:, cols] * (gate * sigmoid(gate))
        gate_s[:, cols] = gate
        gated_s[:, cols] = gated
        term = fold(gated * gated)
        power = term if power is None else power + term
    scale = lax.rsqrt(jnp.sum(power, axis=1, keepdims=True) / inner + EPS)

    @pl.when(first)
    def _():
        wait_pieces(place_ref, ow_pieces, ow_refs, ow, o_sems)

    match = None
    for p in range(parts):
        true = columns_of(place_ref, p, order, width)
        rows = slice(p * width, (p + 1) * width)
        grad = mm_t(cot_ref[...], ow[rows, :])
        gated = gated_s[:, true]
        gain = gain_ref[0:1, true]
        unit = gated * scale
        mixed_ref[:, rows] = (unit * gain).astype(BF16)
        dgain_ref[0:1, true] += jnp.sum(grad * unit, axis=0, keepdims=True)
        scaled = grad * gain
        scaled_s[:, true] = scaled
        term = fold(scaled * gated)
        match = term if match is None else match + term
    pull = jnp.sum(match, axis=1, keepdims=True) * (scale * scale) / inner
    for p in range(parts):
        cols = slice(p * width, (p + 1) * width)
        gate = gate_s[:, cols]
        sig = sigmoid(gate)
        silu = gate * sig
        dgated = scale * (scaled_s[:, cols] - gated_s[:, cols] * pull)
        dscan_ref[:, cols] = dgated * silu
        dgate_ref[:, cols] = (dgated * scan_ref[:, cols] * (sig + silu * (1.0 - sig))).astype(BF16)


def run_gating(place, normed, gate_weight, out_weight, cot, scan_out, gain, order, block=256):
    wg_pieces, wg_arrays = gate_weight
    ow_pieces, ow_arrays = out_weight
    length, width = normed.shape
    inner = scan_out.shape[1]
    return pl.pallas_call(
        functools.partial(gating, wg_pieces=wg_pieces, ow_pieces=ow_pieces, order=order),
        grid_spec=grid_of(
            (length // block,),
            [row_block(block, width), row_block(block, width), row_block(block, inner), fixed((1, inner))]
            + anywhere(len(wg_pieces) + len(ow_pieces)),
            [row_block(block, inner), row_block(block, inner), row_block(block, inner), fixed((1, inner))],
            [pltpu.VMEM((inner, width), BF16), pltpu.VMEM((inner, width), BF16)]
            + [pltpu.VMEM((block, inner), F32)] * 3
            + [pltpu.SemaphoreType.DMA((len(wg_pieces),)), pltpu.SemaphoreType.DMA((len(ow_pieces),))],
        ),
        out_shape=[
            jax.ShapeDtypeStruct((length, inner), BF16),
            jax.ShapeDtypeStruct((length, inner), F32),
            jax.ShapeDtypeStruct((length, inner), BF16),
            jax.ShapeDtypeStruct((1, inner), F32),
        ],
        compiler_params=pltpu.CompilerParams(vmem_limit_bytes=62 << 20),
        cost_estimate=pl.CostEstimate(flops=40_000_000_000, bytes_accessed=70_000_000, transcendentals=10_000_000),
        name="gating",
    )(place, normed, cot, scan_out, gain, *wg_arrays, *ow_arrays)


def gate_back(place_ref, dgate_ref, *rest, pieces):
    refs, (grad_ref, weight, sems) = rest[: len(pieces)], rest[len(pieces) :]

    @pl.when(pl.program_id(0) == 0)
    def _():
        load_pieces(place_ref, pieces, refs, weight, sems)
        wait_pieces(place_ref, pieces, refs, weight, sems)

    step = 384
    for low in range(0, grad_ref.shape[1], step):
        grad_ref[:, low : low + step] = mm(dgate_ref[...], weight[:, low : low + step])


def run_gate_back(place, dgate, model, weight, block=256):
    pieces, arrays = weight
    length, inner = dgate.shape
    return pl.pallas_call(
        functools.partial(gate_back, pieces=pieces),
        grid_spec=grid_of(
            (length // block,),
            [row_block(block, inner)] + anywhere(len(pieces)),
            row_block(block, model),
            [pltpu.VMEM((inner, model), BF16), pltpu.SemaphoreType.DMA((len(pieces),))],
        ),
        out_shape=jax.ShapeDtypeStruct((length, model), F32),
        compiler_params=pltpu.CompilerParams(vmem_limit_bytes=40 << 20),
        cost_estimate=pl.CostEstimate(flops=16_000_000_000, bytes_accessed=22_000_000, transcendentals=0),
        name="gate_back",
    )(place, dgate, *arrays)


def input_back(place_ref, part_ref, tok_ref, cot_ref, gain_ref, *rest, count, pieces, order):
    dproj_refs, rest = rest[:count], rest[count:]
    refs, (grad_ref, dgain_ref, weight, dn, sems) = rest[: len(pieces)], rest[len(pieces) :]
    first = pl.program_id(0) == 0

    @pl.when(first)
    def _():
        load_pieces(place_ref, pieces, refs, weight, sems)
        dgain_ref[...] = jnp.zeros_like(dgain_ref)
        wait_pieces(place_ref, pieces, refs, weight, sems)

    model = tok_ref.shape[1]
    width = model // len(order)
    tok = tok_ref[...].astype(F32)
    scale = lax.rsqrt(jnp.mean(tok * tok, axis=1, keepdims=True) + EPS)
    match = None
    for position in range(len(order)):
        spot = slice(position * width, (position + 1) * width)
        true = columns_of(place_ref, position, order, width)
        grad, low = part_ref[:, spot], 0
        for ref in dproj_refs:
            grad = grad + mm(ref[...], weight[low : low + ref.shape[1], spot])
            low += ref.shape[1]
        value = tok_ref[:, true].astype(F32)
        dgain_ref[0:1, true] += jnp.sum(grad * (value * scale), axis=0, keepdims=True)
        grad = grad * gain_ref[0:1, true]
        dn[:, spot] = grad
        term = jnp.sum(grad * value, axis=1, keepdims=True)
        match = term if match is None else match + term
    pull = match * (scale * scale * scale) / model
    for position in range(len(order)):
        spot = slice(position * width, (position + 1) * width)
        true = columns_of(place_ref, position, order, width)
        value = tok_ref[:, true].astype(F32)
        grad_ref[:, true] = cot_ref[:, true].astype(F32) + (scale * dn[:, spot] - value * pull)


def run_input_back(place, part, dprojs, tok, cot, gain, weight, order, block=256):
    pieces, arrays = weight
    length, model = tok.shape
    widths = [d.shape[1] for d in dprojs]
    return pl.pallas_call(
        functools.partial(input_back, count=len(dprojs), pieces=pieces, order=order),
        grid_spec=grid_of(
            (length // block,),
            [row_block(block, model), row_block(block, model), row_block(block, model), fixed((1, model))]
            + [row_block(block, w) for w in widths] + anywhere(len(pieces)),
            [row_block(block, model), fixed((1, model))],
            [pltpu.VMEM((sum(widths), model), BF16), pltpu.VMEM((block, model), F32),
             pltpu.SemaphoreType.DMA((len(pieces),))],
        ),
        out_shape=[jax.ShapeDtypeStruct((length, model), F32), jax.ShapeDtypeStruct((1, model), F32)],
        compiler_params=pltpu.CompilerParams(vmem_limit_bytes=50 << 20),
        cost_estimate=pl.CostEstimate(flops=22_000_000_000, bytes_accessed=46_000_000, transcendentals=1000),
        name="input_back",
    )(place, part, tok, cot, gain, *dprojs, *arrays)


def project_out(place_ref, mixed_ref, tok_ref, *rest, pieces):
    refs, (out_ref, weight, sems) = rest[: len(pieces)], rest[len(pieces) :]

    @pl.when(pl.program_id(0) == 0)
    def _():
        load_pieces(place_ref, pieces, refs, weight, sems)
        wait_pieces(place_ref, pieces, refs, weight, sems)

    step = 384
    for low in range(0, out_ref.shape[1], step):
        cols = slice(low, low + step)
        out_ref[:, cols] = (tok_ref[:, cols].astype(F32) + mm(mixed_ref[...], weight[:, cols])).astype(BF16)


def run_project_out(place, mixed, tok, weight, block=256):
    pieces, arrays = weight
    length, model = tok.shape
    inner = mixed.shape[1]
    return pl.pallas_call(
        functools.partial(project_out, pieces=pieces),
        grid_spec=grid_of(
            (length // block,),
            [row_block(block, inner), row_block(block, model)] + anywhere(len(pieces)),
            row_block(block, model),
            [pltpu.VMEM((inner, model), BF16), pltpu.SemaphoreType.DMA((len(pieces),))],
        ),
        out_shape=jax.ShapeDtypeStruct((length, model), BF16),
        compiler_params=pltpu.CompilerParams(vmem_limit_bytes=40 << 20),
        cost_estimate=pl.CostEstimate(flops=14_000_000_000, bytes_accessed=20_000_000, transcendentals=0),
        name="project_out",
    )(place, mixed, tok, *arrays)


def scan_backward(proj_ref, tail_ref, sum_ref, keys_ref, out_ref, dout_ref, start_ref, cw_ref, cwk_ref, vec_ref,
                  skip_ref, pick_ref, *rest, nstate, low, groups, per, begin, last):
    if not begin:
        old_cross_ref, old_keys_ref, old_raw_ref = rest[:3]
        rest = rest[3:]
    dproj_ref, dcw_ref, dcb_ref, dskip_ref, dvec_ref = rest[:5]
    rest = rest[5:]
    if not last:
        cross_ref, keys_ref_out, raw_ref = rest[:3]
        rest = rest[3:]
    dsum, dstate, edge, logs_v, tails_v, steps_v, dt_tab, log_tab, log_rows, dcross, dkeys = rest
    first = pl.program_id(0) == 0
    span_all = groups * per * HEAD
    conv = dsum.shape[1]

    @pl.when(first)
    def _():
        dsum[Q : Q + 8, :] = jnp.zeros((8, conv), F32)
        dstate[...] = jnp.zeros_like(dstate)
        edge[...] = jnp.zeros_like(edge)
        dcw_ref[...] = jnp.zeros_like(dcw_ref)
        dcb_ref[...] = jnp.zeros_like(dcb_ref)
        dskip_ref[...] = jnp.zeros_like(dskip_ref)
        dvec_ref[...] = jnp.zeros_like(dvec_ref)

    raw = tail_ref[:, 2 * nstate : 2 * nstate + LANES] + vec_ref[0:1, :]
    dt = softplus(raw)
    lower = tri_lower()
    rate = vec_ref[1:2, :]
    logs = jnp.dot(lower.astype(F32), dt * rate, precision=HI, preferred_element_type=F32)
    fill_tables(dt, logs, dt_tab, log_tab, log_rows, low, groups, per)
    sum_b = keys_ref[:, 0:nstate]
    sum_c = keys_ref[:, nstate : 2 * nstate]
    sig_b, sig_c = sigmoid(sum_b), sigmoid(sum_c)
    keys_b32, keys_c32 = sum_b * sig_b, sum_c * sig_c
    keys_b, keys_c = keys_b32.astype(BF16), keys_c32.astype(BF16)
    c_cols = jnp.transpose(keys_c32).astype(BF16)
    cross = mm(keys_b, c_cols)
    span = per * HEAD
    low_half = lax.broadcasted_iota(jnp.int32, (Q, LANES), 1) < HEAD
    upper = lax.broadcasted_iota(jnp.int32, (Q, Q), 0) <= lax.broadcasted_iota(jnp.int32, (Q, Q), 1)
    if not begin:
        dcross[...] = old_cross_ref[...]
        dkeys[...] = old_keys_ref[...]
    else:
        dcross[...] = jnp.zeros_like(dcross)
        dkeys[...] = jnp.zeros_like(dkeys)

    def group(g, carry):
        base = pl.multiple_of(g * span, span)
        whole = pl.ds(base, span)
        dts, lgs = dt_tab[g], log_tab[g]
        dstate_b = dstate[:, whole].astype(BF16)
        from_state = mm(keys_b, dstate_b)
        tails_all, outs_all, lasts = [], [], []
        dcr = None
        for j in range(per // 2):
            cols = pl.ds(pl.multiple_of(base + j * LANES, LANES), LANES)
            h = (low + g) * per + 2 * j
            col0, col1 = spread(lgs, 2 * j), spread(lgs, 2 * j + 1)
            row0, row1 = log_rows[pl.ds(h, 1), :], log_rows[pl.ds(h + 1, 1), :]
            total = sum_ref[:, cols]
            sig = sigmoid(total)
            values = total * sig
            step = jnp.where(low_half, spread(dts, 2 * j), spread(dts, 2 * j + 1))
            stepped = values * step
            stepped_b = stepped.astype(BF16)
            dout = dout_ref[:, cols]
            dout_b = dout.astype(BF16)
            decay0 = jnp.exp(jnp.where(upper, row0 - col0, NEG))
            decay1 = jnp.exp(jnp.where(upper, row1 - col1, NEG))
            mix = jnp.concatenate([(decay0 * cross).astype(BF16), (decay1 * cross).astype(BF16)], axis=1)
            zero = jnp.zeros_like(dout_b)
            douts = jnp.concatenate(
                [jnp.where(low_half, dout_b, zero), jnp.where(low_half, zero, dout_b)], axis=0)
            local = mm(mix, douts)
            dmix = mm_t(stepped_b, douts)
            term = dmix[:, 0:Q] * decay0 + dmix[:, Q : 2 * Q] * decay1
            dcr = term if dcr is None else dcr + term
            both = jnp.where(low_half, col0, col1)
            last = both[Q - 1 : Q, :]
            tail = jnp.exp(last - both)
            passed = from_state[:, j * LANES : (j + 1) * LANES] * tail
            dstepped = local + passed
            skip = skip_ref[0:1, cols]
            scan = out_ref[:, cols] - skip * values
            logs_v[:, cols] = dout_b.astype(F32) * scan - stepped_b.astype(F32) * local
            tails_v[:, cols] = stepped * passed
            steps_v[:, cols] = dstepped * values
            dvalues = dstepped * step + dout * skip
            dskip_ref[0:1, cols] += jnp.sum(dout * values, axis=0, keepdims=True)
            dsum[0:Q, cols] = dvalues * (sig + values * (1.0 - sig))
            tails_all.append((stepped * tail).astype(BF16))
            outs_all.append((dout * jnp.exp(both)).astype(BF16))
            lasts.append(jnp.exp(last))
        dcross[...] += dcr
        outs = jnp.concatenate(outs_all, axis=1)
        starts = start_ref[:, whole]
        dkeys[:, nstate : 2 * nstate] += mm_t(outs, starts)
        dkeys[:, 0:nstate] += mm_t(jnp.concatenate(tails_all, axis=1), dstate_b)
        kept = dstate[:, whole] * jnp.concatenate(lasts, axis=1)
        edge[0:1, whole] = jnp.sum(kept * starts.astype(F32), axis=0, keepdims=True)
        dstate[:, whole] = kept + mm(c_cols, outs)
        return carry

    lax.fori_loop(0, groups, group, 0)

    if last:
        dcr = dcross[...]
        exact = lambda u, v: jnp.dot(u, v, precision=HI, preferred_element_type=F32)
        d_b = dkeys[:, 0:nstate] + exact(dcr, keys_c32)
        d_c = dkeys[:, nstate : 2 * nstate] + exact(jnp.transpose(dcr), keys_b32)
        dsum[0:Q, span_all : span_all + nstate] = d_b * (sig_b + keys_b32 * (1.0 - sig_b))
        dsum[0:Q, span_all + nstate : conv] = d_c * (sig_c + keys_c32 * (1.0 - sig_c))
    else:
        cross_ref[...] = dcross[...]
        keys_ref_out[...] = dkeys[...]

    def reduce_heads(v):
        high = v.astype(BF16)
        low = (v - high.astype(F32)).astype(BF16)
        return mm(high, pick_ref[...]) + mm(low, pick_ref[...])

    dlogs = reduce_heads(logs_v[...])
    dtails = reduce_heads(tails_v[...])
    dlogit = (
        jnp.dot(upper.astype(F32), dlogs, precision=HI, preferred_element_type=F32)
        + jnp.dot(1.0 - upper.astype(F32), dtails, precision=HI, preferred_element_type=F32)
        + reduce_heads(edge[...])[0:1, :]
    )
    dstep = reduce_heads(steps_v[...]) + dlogit * rate
    draw = dstep * sigmoid(raw)
    dvec_ref[0:1, :] += jnp.sum(draw, axis=0, keepdims=True)
    dvec_ref[1:2, :] += jnp.sum(dlogit * dt * rate, axis=0, keepdims=True)
    if last:
        dproj_ref[:, conv : conv + LANES] = (draw + old_raw_ref[...]).astype(BF16)
    elif begin:
        raw_ref[...] = draw
    else:
        raw_ref[...] = draw + old_raw_ref[...]

    wide = 256
    for start in range(0, conv, wide):
        part = pl.ds(start, wide)
        if start < span_all:
            source, taps_ref, local = proj_ref, cw_ref, part
        else:
            source, taps_ref, local = tail_ref, cwk_ref, pl.ds(start - span_all, wide)
        taken = source[:, local]
        total = None
        for k in range(4):
            moved = dsum[3 - k : 3 - k + Q, part]
            dcw_ref[k : k + 1, part] += jnp.sum(taken * moved, axis=0, keepdims=True)
            term = taps_ref[k : k + 1, local] * moved
            total = term if total is None else total + term
            if k == 3:
                dcb_ref[0:1, part] += jnp.sum(moved, axis=0, keepdims=True)
        dproj_ref[:, part] = total.astype(BF16)
    dsum[Q : Q + 8, :] = dsum[0:8, :]


def run_scan_backward(proj, sums, scan_out, dscan, starts, cw, vec, skip_cols, pick, inner, nstate, low, groups, per,
                      previous, last):
    length = proj.shape[0]
    blocks = length // Q
    span = groups * per * HEAD
    begin = previous is None
    conv = span + (2 * nstate if last else 0)
    where = low * per * HEAD // span
    whole = lambda shape: pl.BlockSpec(shape, lambda i: (0, 0))
    rows = lambda width, col=0: pl.BlockSpec((Q, width), lambda i: (blocks - 1 - i, col))
    part = lambda height: pl.BlockSpec((height, span), lambda i: (0, where))
    tail = 2 * nstate + LANES
    out_specs = [rows(conv + (LANES if last else 0)), whole((4, conv)), whole((1, conv)), whole((1, span)),
                 whole((8, LANES))]
    out_shape = [
        jax.ShapeDtypeStruct((length, conv + (LANES if last else 0)), BF16),
        jax.ShapeDtypeStruct((4, conv), F32),
        jax.ShapeDtypeStruct((1, conv), F32),
        jax.ShapeDtypeStruct((1, span), F32),
        jax.ShapeDtypeStruct((8, LANES), F32),
    ]
    carried = [rows(Q), rows(2 * nstate), rows(LANES)]
    if not last:
        out_specs += carried
        out_shape += [jax.ShapeDtypeStruct((length, w), F32) for w in (Q, 2 * nstate, LANES)]
    return pl.pallas_call(
        functools.partial(scan_backward, nstate=nstate, low=low, groups=groups, per=per, begin=begin, last=last),
        grid=(blocks,),
        in_specs=[
            rows(span, where), rows(tail, inner // tail), rows(span, where), rows(2 * nstate, inner // (2 * nstate)),
            rows(span, where), rows(span, where),
            pl.BlockSpec((nstate, span), lambda i: (blocks - 1 - i, where)),
            part(4), pl.BlockSpec((4, 2 * nstate), lambda i: (0, inner // (2 * nstate))),
            whole(vec.shape), part(1), pl.BlockSpec((span, LANES), lambda i: (where, 0)),
        ] + ([] if begin else carried),
        out_specs=out_specs,
        out_shape=out_shape,
        scratch_shapes=[
            pltpu.VMEM((Q + 8, conv), F32),
            pltpu.VMEM((nstate, span), F32),
            pltpu.VMEM((8, span), F32),
            pltpu.VMEM((Q, span), F32),
            pltpu.VMEM((Q, span), F32),
            pltpu.VMEM((Q, span), F32),
            pltpu.VMEM((groups, Q, LANES), F32),
            pltpu.VMEM((groups, Q, LANES), F32),
            pltpu.VMEM((LANES, Q), F32),
            pltpu.VMEM((Q, Q), F32),
            pltpu.VMEM((Q, 2 * nstate), F32),
        ],
        compiler_params=pltpu.CompilerParams(vmem_limit_bytes=50 << 20),
        cost_estimate=pl.CostEstimate(flops=40_000_000_000, bytes_accessed=40_000_000, transcendentals=15_000_000),
        name="scan_backward",
    )(proj, proj, sums, sums, scan_out, dscan, starts, cw, cw, vec, skip_cols, pick, *(previous or ()))


def bits_of(size):
    return [1 << b for b in range(size.bit_length() - 1)]


def swap(value, axis, bit, size):
    return lax.ppermute(value, axis, [(i, i ^ bit) for i in range(size)])


def after(value, *deps):
    return lax.optimization_barrier((value,) + deps)[0] if deps else value


def order_of(size):
    flipped = []
    for index in range(size):
        value = 0
        for low, high in zip(bits_of(size), reversed(bits_of(size))):
            value |= high if index & low else 0
        flipped.append(value)
    return flipped


class Gather:
    def __init__(self, shard, order, rep_index, groups, copies, lanes, chunks):
        self.order, self.groups, self.copies = order, groups, copies
        self.size = shard.shape
        self.lanes = lanes
        self.half = shard.shape[0] // 2
        self.rows = self.half // chunks
        self.shard = shard
        parity = rep_index & 1
        self.mine = [lax.dynamic_slice_in_dim(shard, parity * self.half + c * self.rows, self.rows, 0)
                     for c in range(chunks)]
        self.there, self.across = [None] * chunks, [None] * chunks
        self.own, self.early = None, []

    def far(self, chunk, *deps):
        value = after(self.mine[chunk], *deps)
        self.there[chunk] = swap(value, "shard", 2, self.groups)

    def whole(self, *deps):
        self.there = [swap(after(self.shard, *deps), "shard", 2, self.groups)]
        self.across = []

    def side(self, chunk):
        self.across[chunk] = swap(self.there[chunk], "rep", 1, self.copies)

    def core(self, value, *deps):
        return swap(after(value, *deps), "shard", 1, self.groups)

    def finish(self, *deps):
        own = self.own if self.own is not None else self.core(self.shard)
        have = {0: [(0, None, 0, self.shard)], 1: [(0, None, 0, own)]}
        if self.across:
            have[2] = [(c * self.rows, h, self.half, v) for h, vs in ((0, self.there), (1, self.across))
                       for c, v in enumerate(vs)]
        else:
            have[2] = [(0, None, 0, self.there[0])]
        have[3] = []
        for index, (row, half, size, value) in enumerate(have[2]):
            if index < len(self.early):
                partner = self.early[index]
            else:
                partner = self.core(value, *(deps if index == len(have[2]) - 1 else ()))
            have[3].append((row, half, size, partner))
        pieces, arrays = [], []
        for position, source in enumerate(self.order):
            for row, half, size, value in have[source]:
                if self.lanes:
                    pieces.append((row, half, size, position * self.size[1]))
                else:
                    pieces.append((row + position * self.size[0], half, size, 0))
                arrays.append(value)
        return tuple(pieces), tuple(arrays)


class Total:
    def __init__(self, kept, sent, axis, rep_index, groups, copies, narrow=False):
        self.axis, self.rep_index = axis, rep_index
        self.sizes = {"shard": groups, "rep": copies}
        self.stages = [("shard", index, 1) for index in range(len(bits_of(groups)))]
        count = len(bits_of(copies))
        over = [("rep", 0, 1)] + [("rep", index, min(2, count - index)) for index in range(1, count, 2)]
        self.stages += over
        self.back = list(reversed(over))
        if narrow:
            self.back = [(name, shift + bit, 1) for name, shift, width in self.back for bit in range(width)]
        self.value, self.out = kept, [sent]
        self.fly()

    @classmethod
    def join(cls, chains):
        first = chains[0]
        new = object.__new__(cls)
        new.axis, new.rep_index, new.sizes = first.axis, first.rep_index, first.sizes
        new.stages, new.back = first.stages, first.back
        new.value = jnp.concatenate([v.value for v in chains])
        new.coming = [jnp.concatenate(v) for v in zip(*(c.coming for c in chains))]
        return new

    def fly(self):
        name, shift, _ = self.stages[0]
        self.coming = [swap(v, name, (k + 1) << shift, self.sizes[name]) for k, v in enumerate(self.out)]

    def done(self):
        return not self.stages and not self.back

    def step(self, *deps):
        coming = [after(v, *deps) for v in self.coming]
        if not self.stages:
            return self.widen(coming)
        self.stages.pop(0)
        terms = [self.value] + coming
        if not self.stages:
            self.value = sum(v.astype(F32) for v in terms).astype(BF16)
            self.fly_back()
            return [self.value]
        name, shift, width = self.stages[0]
        parts = 1 << width
        axis = self.axis if name == "shard" else 0
        size = self.value.shape[axis] // parts
        mine = 0 if name == "shard" else (self.rep_index >> shift) & (parts - 1)
        cut = lambda start: sum(lax.dynamic_slice_in_dim(v, start, size, axis).astype(F32) for v in terms)
        self.out = [cut((mine ^ k) * size).astype(BF16) for k in range(1, parts)]
        self.value = cut(mine * size)
        self.fly()
        return self.out

    def fly_back(self):
        name, shift, width = self.back[0]
        self.coming = [swap(self.value, name, k << shift, self.sizes[name]) for k in range(1, 1 << width)]

    def widen(self, coming):
        name, shift, width = self.back.pop(0)
        parts = [self.value] + coming
        for bit in range(width):
            turn = ((self.rep_index >> (shift + bit)) & 1) != 0
            parts = [jnp.where(turn, parts[k ^ (1 << bit)], parts[k]) for k in range(len(parts))]
        if not self.back:
            self.value = [v.astype(F32) for v in parts]
            return self.value
        self.value = jnp.concatenate(parts)
        self.fly_back()
        return [self.value]


def outer(left, right):
    return lax.dot_general(left, right, (((0,), (0,)), ((), ())), preferred_element_type=F32).astype(BF16)


def on_device(groups, copies, tokens, norm_gain, in_weight, conv_weight, conv_bias, dt_bias, a_log, skip, gate_gain,
              out_weight, cotangent):
    if tokens.shape[0] != 1 or groups != 4:
        raise ValueError("unexpected sizes")
    order = order_of(groups)
    shard_index = lax.axis_index("shard")
    rep_index = lax.axis_index("rep")
    tok, cot = tokens[0], cotangent[0]
    inner = gate_gain.shape[0] * groups
    conv = conv_bias.shape[0] * groups
    heads = dt_bias.shape[0] * groups
    nstate = (conv - inner) // 2
    model = tok.shape[1]
    taps = conv_weight.shape[0]
    outputs_all = in_weight.shape[1]
    place = jnp.stack([shard_index, rep_index & 1]).astype(jnp.int32)

    turned = in_weight.T
    total = conv + LANES
    conv_part = jnp.pad(turned[inner:], ((0, total + inner - outputs_all), (0, 0)))
    make = lambda shard, lanes, chunks: Gather(shard, order, rep_index, groups, copies, lanes, chunks)
    wc = make(conv_part, True, 2)
    wg = make(turned[:inner], True, 1)
    ow = make(out_weight, False, 1)

    small = (norm_gain, conv_bias, dt_bias, a_log, skip, gate_gain, conv_weight)
    packed = jnp.concatenate([v.reshape(-1) for v in small])
    wc.far(0)
    wc.far(1)
    wc.side(0)
    wc.side(1)
    wc.own = wc.core(wc.shard)
    wc.early = [wc.core(wc.there[0])]
    wg.far(0, wc.there[1], wc.own, wc.early[0])
    ow.whole(wc.there[1], wc.own, wc.early[0])
    rows = [packed, swap(packed, "shard", 1, groups)]
    far = swap(packed, "shard", 2, groups)
    rows += [far, swap(far, "shard", 1, groups)]
    for bit in bits_of(groups):
        turn = (shard_index & bit) != 0
        rows = [jnp.where(turn, rows[j ^ bit], rows[j]) for j in range(groups)]
    everyone = jnp.stack(rows).astype(F32)
    parts, low = [], 0
    for v in small:
        parts.append(everyone[:, low : low + v.size])
        low += v.size
    gain, cb, db, al, sk, gg = (v.reshape(-1) for v in parts[:6])
    cw = parts[6].reshape(groups, taps, -1).transpose(1, 0, 2).reshape(taps, conv)
    gain, cb, gg = gain[None], cb[None], gg[None]
    vec = jnp.pad(jnp.stack([db, -jnp.exp(al)]), ((0, 6), (0, LANES - heads)))
    skip_cols = jnp.repeat(sk, inner // heads)[None]
    pick = (jnp.arange(inner)[:, None] // (inner // heads) == jnp.arange(LANES)[None]).astype(BF16)

    wc = wc.finish(gain, cb, gg, cw, vec, skip_cols, pick)
    normed, proj = run_project_in(place, tok, gain, wc, total, order)
    wg.there[0] = after(wg.there[0], normed)
    wg.side(0)
    proj = after(proj, wg.there[0])
    per = 8
    scan_out, sums, starts = run_scan_forward(proj, cw, cb, vec, skip_cols, inner, nstate, heads // per, per)
    wg, ow = wg.finish(scan_out), ow.finish(scan_out)
    mixed, dscan, dgate, dgg = run_gating(place, normed, wg, ow, cot, scan_out, gg, order)

    chain = lambda kept, sent, axis, *way: Total(kept, sent, axis, rep_index, groups, copies, *way)
    half = inner // 2
    out_sent = outer(mixed[:, half:], cot)
    o = chain(outer(mixed[:, :half], cot), out_sent, 0, True)
    half = model // 2
    left, right = normed[:, :half], normed[:, half:]
    gate_sent = outer(dgate, right)
    marks = o.step(o.value)
    g = chain(outer(after(dgate, *marks), left), gate_sent, 1)
    marks = marks + g.step(g.value)

    blocks = heads // per
    cuts = [blocks * v // 3 for v in range(4)]
    chains, grads, carried = [o, g], [], None
    for index in range(3):
        low, high = cuts[index], cuts[index + 1]
        found = run_scan_backward(
            proj, sums, scan_out, after(dscan, *marks), starts, cw, vec, skip_cols, pick, inner, nstate, low,
            high - low, per, carried, index == 2)
        grads.append(found[:5])
        carried = tuple(found[5:])
        dproj, marks = found[0], []
        if index == 1:
            marks = o.step(dproj)
        if index == 2:
            marks = ab.coming + g.step(dproj)
            marks = marks + o.step(dproj, *marks)
        dproj = after(dproj, *marks)
        sent = outer(dproj, right)
        kept = outer(after(dproj, sent, *g.coming) if index == 1 else dproj, left)
        new = chain(kept, sent, 1)
        chains.append(new)
        if index == 0:
            marks = marks + new.coming + o.step(kept)
        if index == 1:
            ab = Total.join(chains[2:])
            marks = marks + ab.step(kept)
            marks = marks + g.step(kept, *marks)
        if index == 2:
            marks = marks + new.step(kept)

    part = run_gate_back(place, after(dgate, *marks), model, wg)
    abc = Total.join([ab, chains[4]])
    marks = g.step(part)
    marks = marks + abc.step(part, *marks)
    marks = marks + o.step(part, *marks)
    input_grad, dgain = run_input_back(place, after(part, *marks), [v[0] for v in grads], tok, cot, gain, wc, order)

    dcw = jnp.concatenate([v[1] for v in grads], axis=1)
    dcb = jnp.concatenate([v[2][0] for v in grads])
    dskip = jnp.concatenate([v[3][0] for v in grads]).reshape(heads, -1).sum(1)
    dvec = sum(v[4] for v in grads)
    pieces = (dcb, dvec[0, :heads], dvec[1, :heads], dskip, dgg[0])
    flat = jnp.concatenate([v.reshape(groups, -1) for v in pieces]
                           + [dcw.reshape(taps, groups, -1).transpose(1, 0, 2).reshape(groups, -1)], axis=1)
    flat = jnp.concatenate([dgain[0].reshape(groups, -1), flat], axis=1)
    marks = abc.step(dgain, *g.coming)
    marks = marks + g.step(*marks)
    output = run_project_out(place, after(mixed, *marks), tok, ow)
    marks = abc.step(output, *g.coming)
    o.step(output)
    flat = after(flat, output, *marks)
    for axis, size in (("shard", groups), ("rep", copies)):
        for bit in bits_of(size):
            if axis == "rep" and bit == 2:
                flat = after(flat, *abc.step())
            flat = flat + swap(flat, axis, bit, size)
    for old in (abc, g, o):
        while not old.done():
            old.step()

    in_total = jnp.concatenate(g.value + abc.value)[:outputs_all].T
    out_total = jnp.concatenate(o.value)

    own = lax.dynamic_slice_in_dim(flat, shard_index, 1, 0)[0]
    shares, low = [], 0
    for v in small:
        shares.append(own[low : low + v.size].reshape(v.shape))
        low += v.size
    d_gain, d_cb, d_db, d_al, d_sk, d_gg, d_cw = shares
    return (output[None], input_grad[None], d_gain, in_total, d_cw, d_cb, d_db, d_al, d_sk, d_gg, out_total)


def solution(mesh):
    whole = P(("shard", "rep"), None, None)
    row, matrix, cols = P("shard"), P("shard", None), P(None, "shard")
    return jax.shard_map(
        functools.partial(on_device, mesh.shape["shard"], mesh.shape["rep"]),
        mesh=mesh,
        in_specs=(whole, row, matrix, cols, row, row, row, row, row, matrix, whole),
        out_specs=(whole, whole, row, matrix, cols, row, row, row, row, row, matrix),
        check_vma=False,
    )
```
